32 devices in a mesh: dp: 8 (over z, core), mp: 4 (over y, x).
Axes of the slice: x: 2, y: 2, z: 4, core: 2. Of those that a mesh axis runs over, the one named last changes fastest.
Arguments:
- tokens: bfloat16 [12288, 2048], P(('dp', 'mp')), may hold values from -6 to 6
- segment_ids: int32 [16, 768], P('dp'), may hold values from 0 to 5, never falling along the last dimension, each value on 1 to 256 neighbouring positions
- query_weight: bfloat16 [2048, 2048], P(None, 'mp'), may hold values from -0.125 to 0.125
- key_weight: bfloat16 [2048, 2048], P(None, 'mp'), may hold values from -0.125 to 0.125
- value_weight: bfloat16 [2048, 2048], P(None, 'mp'), may hold values from -0.125 to 0.125
- out_weight: bfloat16 [2048, 2048], P('mp'), may hold values from -0.75 to 0.75
- up_weight: bfloat16 [2048, 8192], P(None, 'mp'), may hold values from -0.125 to 0.125
- down_weight: bfloat16 [8192, 2048], P('mp'), may hold values from -0.0625 to 0.0625
- attn_gain: float32 [2048], replicated, may hold values from 0.5 to 1.5
- mlp_gain: float32 [2048], replicated, may hold values from 0.5 to 1.5
- out_cotangent: bfloat16 [12288, 2048], P(('dp', 'mp')), may hold values from -18 to 18
Outputs:
- layer_output: bfloat16 [12288, 2048], P(('dp', 'mp'))
- tokens_grad: float32 [12288, 2048], P(('dp', 'mp'))
- query_weight_grad: float32 [2048, 2048], P('dp', 'mp')
- key_weight_grad: float32 [2048, 2048], P('dp', 'mp')
- value_weight_grad: float32 [2048, 2048], P('dp', 'mp')
- out_weight_grad: float32 [2048, 2048], P('mp', 'dp')
- up_weight_grad: float32 [2048, 8192], P('dp', 'mp')
- down_weight_grad: float32 [8192, 2048], P('mp', 'dp')
- attn_gain_grad: float32 [2048], replicated
- mlp_gain_grad: float32 [2048], replicated
The draws below stay inside these ranges and needn't reach their ends.
Inputs may be any that keep to these rules, and one draw needn't show every extreme that they name: `segment_ids`: within each packed sequence the clip numbers never fall; each clip covers 1 to 256 tokens, and some clip covers exactly 256.
All inputs are finite; a program needn't handle non-finite values.
Results may differ from the reference program's by a relative error of at most 0.02.
Values may be sent and summed in bfloat16 or wider, within the bound.
A program may use at most 192 MiB of HBM per device.

```python
import math
import jax
import jax.numpy as jnp
import numpy as np
from jax import lax

D = 2048
HEADS = 16
HEAD_DIM = 128
FF = 8192
SEQ_LEN = 768
CLIPS = 6
CLIP_MOST = 256
SEQS = 16
TOKENS = 12288


def draw_out_cotangent(key, part):
    first_key = jax.random.fold_in(key, 11)
    rising = 1.0 + 2.0 * jnp.arange(TOKENS, dtype=jnp.float32)[:, None] / TOKENS
    normal_part = jnp.clip(jax.random.normal(first_key, (TOKENS, D), jnp.float32), -6.0, 6.0)
    return (normal_part * rising).astype(jnp.bfloat16)


def block_levels(rng, extent, cuts, least, high):
    level, own = 1.0, jax.random.fold_in(rng, 6)
    for dim, parts in cuts:
        heights = jnp.exp(jax.random.uniform(jax.random.fold_in(own, dim), (parts,), jnp.float32, least / len(cuts), high / len(cuts)))
        level = level * jnp.repeat(heights, extent[dim] // parts).reshape([-1 if axis == dim else 1 for axis in range(len(extent))])
    return level


def profile(number_of, total, reach, slope):
    loads = [(1 << 20) // math.isqrt(rank ** slope) + 1 for rank in range(2, number_of + 1)]
    surplus, counts = total - reach - (number_of - 1), [1] * (number_of - 1)
    while surplus > 0:
        movable = [i for i in range(number_of - 1) if counts[i] < reach]
        whole, budget = sum([loads[i] for i in movable]), surplus
        for i in movable:
            more = min(reach - counts[i], max(1, budget * loads[i] // whole), surplus)
            counts[i] = counts[i] + more
            surplus = surplus - more
    return np.array([reach] + counts)


def uneven(own_key, number_of, total, bound, slope):
    if number_of == 2:
        one = jax.random.randint(own_key, (), max(1, total - bound), min(bound, total - 1) + 1)
        return jnp.stack([one, total - one])
    sizes = jnp.asarray(profile(number_of, total, bound, slope), jnp.int32)
    couples = (number_of - 1) // 2
    donor, sink = sizes[1:1 + 2 * couples:2], sizes[2:2 + 2 * couples:2]
    margin = jnp.minimum(donor - 1, bound - sink)
    shifted = jax.random.randint(jax.random.fold_in(own_key, 1), (couples,), 0, 1 << 20) % (margin + 1)
    sizes = sizes.at[1:1 + 2 * couples:2].set(donor - shifted).at[2:2 + 2 * couples:2].set(sink + shifted)
    return sizes[jax.random.permutation(jax.random.fold_in(own_key, 2), number_of)]


def gaussian(stream_key, extent, scale, reach, split=(), kind=jnp.bfloat16):
    factor_of = block_levels(stream_key, extent, split, -0.22, 0.18) if split else 1.0
    array = jax.random.normal(stream_key, extent, jnp.float32) * scale * factor_of
    return jnp.minimum(jnp.maximum(array, -reach), reach).astype(kind)


def setup_inputs(seed: int = 0) -> dict:
    key_list = jax.random.split(jax.random.key(seed), 12)
    tokens = gaussian(key_list[0], (TOKENS, D), 1.0, 6.0, ((0, 32),))
    segment_ids = jax.vmap(lambda own: jnp.searchsorted(jnp.cumsum(uneven(own, CLIPS, SEQ_LEN, CLIP_MOST, 0)), jnp.arange(SEQ_LEN), side="right"))(jax.random.split(key_list[1], SEQS)).reshape((SEQS, SEQ_LEN)).astype(jnp.int32)
    query_weight = gaussian(key_list[2], (D, HEADS * HEAD_DIM), D ** -0.5, 0.125, ((1, 4),))
    key_weight = gaussian(key_list[3], (D, HEADS * HEAD_DIM), D ** -0.5, 0.125, ((1, 4),))
    value_weight = gaussian(key_list[4], (D, HEADS * HEAD_DIM), D ** -0.5, 0.125, ((1, 4),))
    out_weight = gaussian(key_list[5], (HEADS * HEAD_DIM, D), (HEADS * HEAD_DIM // 32) ** -0.5, 0.75, ((0, 4),))
    up_weight = gaussian(key_list[6], (D, FF), D ** -0.5, 0.125, ((1, 4),))
    down_weight = gaussian(key_list[7], (FF, D), FF ** -0.5, 0.0625, ((0, 4),))
    attn_gain = jnp.clip(1.0 + 0.1 * jax.random.normal(key_list[8], (D,), jnp.float32), 0.5, 1.5)
    mlp_gain = jnp.clip(1.0 + 0.1 * jax.random.normal(key_list[9], (D,), jnp.float32), 0.5, 1.5)
    out_cotangent = draw_out_cotangent(jax.random.fold_in(key_list[11], 71), 0)
    return {"tokens": tokens, "segment_ids": segment_ids, "query_weight": query_weight, "key_weight": key_weight, "value_weight": value_weight, "out_weight": out_weight, "up_weight": up_weight, "down_weight": down_weight, "attn_gain": attn_gain, "mlp_gain": mlp_gain, "out_cotangent": out_cotangent}


epsilon = 1e-05
highest = lax.Precision.HIGHEST

@jax.custom_vjp
def low(v):
    return lax.optimization_barrier(v.astype(jnp.bfloat16)).astype(jnp.float32)

@jax.custom_vjp
def low_back(v):
    return v

def low_keep(v):
    return (low(v), None)

def low_pass(kept, grad):
    return (grad,)

def back_keep(v):
    return (v, None)

def back_low(kept, grad):
    return (low(grad),)
low.defvjp(low_keep, low_pass)
low_back.defvjp(back_keep, back_low)

def norm_rows(values, gain):
    centre = lax.optimization_barrier(jnp.mean(values, axis=-1, keepdims=True))
    centred = values - centre
    spread = lax.optimization_barrier(jnp.mean(centred * centred, axis=-1, keepdims=True))
    return centred * lax.rsqrt(spread + epsilon) * gain

def product(left_rows, right_matrix):
    return jnp.dot(left_rows, right_matrix, precision=highest, preferred_element_type=jnp.float32)

def block_allowed(segment):
    position = jnp.arange(segment.shape[0])
    return (position[None, :] <= position[:, None]) & (segment[:, None] == segment[None, :])

def attend_sequence(packed):
    queries, keys_in, values_in, segment = packed
    scores = jnp.einsum('qhd,khd->hqk', queries, keys_in, precision=highest)
    scores = low_back(scores)
    scores = jnp.where(block_allowed(segment)[None], scores, -1e+30)
    attn_probs = low(jax.nn.softmax(scores, axis=-1))
    return jnp.einsum('hqk,khd->qhd', attn_probs, values_in, precision=highest)

def layer_forward(token_rows, query_weight, key_weight, value_weight, out_weight, up_weight, down_weight, attn_gain, mlp_gain, segment_rows):
    row_total = token_rows.shape[0]
    seq_group = segment_rows.shape[0]
    score_scale = 1.0 / math.sqrt(HEAD_DIM)
    normed_attn = low(norm_rows(token_rows, attn_gain))
    queries = low_back(low(product(normed_attn, query_weight) * score_scale))
    keys_all = low_back(low(product(normed_attn, key_weight)))
    values_all = low_back(low(product(normed_attn, value_weight)))
    shaped = (seq_group, SEQ_LEN, HEADS, HEAD_DIM)
    context = lax.map(jax.checkpoint(attend_sequence), (queries.reshape(shaped), keys_all.reshape(shaped), values_all.reshape(shaped), segment_rows))
    context = low_back(low(context.reshape(row_total, HEADS * HEAD_DIM)))
    middle = token_rows + low_back(product(context, out_weight))
    normed_mlp = low(norm_rows(middle, mlp_gain))
    pre_act = low_back(product(normed_mlp, up_weight))
    hidden = low(jax.nn.gelu(pre_act, approximate=True))
    return middle + low_back(product(hidden, down_weight))

def reference(tokens, segment_ids, query_weight, key_weight, value_weight, out_weight, up_weight, down_weight, attn_gain, mlp_gain, out_cotangent):
    group_size = math.gcd(SEQS, 4)
    rounds = SEQS // group_size
    group_rows = group_size * SEQ_LEN
    params = tuple((weight_in.astype(jnp.float32) for weight_in in (query_weight, key_weight, value_weight, out_weight, up_weight, down_weight, attn_gain, mlp_gain)))
    token_groups = tokens.astype(jnp.float32).reshape(rounds, group_rows, D)
    segment_groups = segment_ids.reshape(rounds, group_size, SEQ_LEN)
    cotangent_groups = out_cotangent.astype(jnp.float32).reshape(rounds, group_rows, D)

    def one_group(totals, inputs):
        token_rows, segment_rows, cotangent_rows = inputs

        def apply_layer(rows_in, *weights_in):
            return layer_forward(rows_in, *weights_in, segment_rows)
        result, pullback = jax.vjp(apply_layer, token_rows, *params)
        gradients = pullback(cotangent_rows)
        totals = tuple((total_in + grad_in for total_in, grad_in in zip(totals, gradients[1:])))
        return (totals, (result.astype(jnp.bfloat16), gradients[0]))
    starting = tuple((jnp.zeros(param_in.shape, jnp.float32) for param_in in params))
    totals, (outputs, input_grads) = lax.scan(one_group, starting, (token_groups, segment_groups, cotangent_groups))
    return (outputs.reshape(TOKENS, D), input_grads.reshape(TOKENS, D), totals[0], totals[1], totals[2], totals[3], totals[4], totals[5], totals[6], totals[7])
```

```python
import functools
import math

import jax
import jax.numpy as jnp
from jax import lax
from jax.experimental import pallas as pl
from jax.experimental.pallas import tpu as pltpu
from jax.sharding import PartitionSpec as P

HEAD_DIM = 128
CLIP_MOST = 256
epsilon = 1e-05
masked_score = -1e30
bf16, f32 = jnp.bfloat16, jnp.float32
VMEM_LIMIT = 60 * 1024 * 1024


def dot(a, b, ca, cb):
    return lax.dot_general(a, b, (((ca,), (cb,)), ((), ())), preferred_element_type=f32)


class Group:
    def __init__(self, count):
        self.count = count

    def swap(self, value, r):
        return lax.ppermute(value, "mp", [(m, m ^ r) for m in range(self.count)])

    def gather(self, low, high):
        if self.count == 4:
            low_x, high_y = self.swap(low, 1), self.swap(high, 2)
            high_x, low_y = self.swap(high, 1), self.swap(low, 2)
            low_d, high_d = self.swap(low_x, 2), self.swap(high_y, 1)
            return [(low, high), (low_x, high_x), (low_y, high_y), (low_d, high_d)]
        me = lax.axis_index("mp")
        blocks = lax.all_gather(jnp.concatenate([low, high]), "mp")
        half = low.shape[0]
        out = []
        for r in range(self.count):
            block = lax.dynamic_index_in_dim(blocks, me ^ r, 0, keepdims=False)
            out.append((block[:half], block[half:]))
        return out

    def reduce(self, parts):
        if self.count == 4:
            early_x, early_y = self.swap(parts[1][0], 1), self.swap(parts[2][1], 2)
            got_x, got_y = self.swap(parts[3][0], 1), self.swap(parts[3][1], 2)
            late_x = self.swap(add(parts[1][1], got_y), 1)
            late_y = self.swap(add(parts[2][0], got_x), 2)
            return (
                (parts[0][0], early_x, late_y),
                (parts[0][1], late_x, early_y),
            )
        me = lax.axis_index("mp")
        blocks = jnp.stack([jnp.concatenate(p) for p in parts])
        blocks = jnp.take(blocks, jnp.arange(self.count) ^ me, axis=0)
        own = lax.psum_scatter(blocks, "mp", scatter_dimension=0, tiled=False)
        half = own.shape[0] // 2
        return ((own[:half],), (own[half:],))


def add(a, b):
    return (a.astype(f32) + b.astype(f32)).astype(bf16)


def total(values):
    out = values[0].astype(f32)
    for v in values[1:]:
        out = out + v.astype(f32)
    return out


def norm_parts(values):
    centre = jnp.mean(values, axis=-1, keepdims=True)
    centred = values - centre
    spread = jnp.mean(centred * centred, axis=-1, keepdims=True)
    scale = lax.rsqrt(spread + epsilon)
    return centred * scale, scale


def norm_rows(values, gain):
    return norm_parts(values)[0] * gain


def norm_back(values, gain, grad):
    unit, scale = norm_parts(values)
    q = grad * gain
    back = scale * (
        q - jnp.mean(q, axis=-1, keepdims=True) - unit * jnp.mean(q * unit, axis=-1, keepdims=True)
    )
    return back, jnp.sum(grad * unit, axis=0)


def mm_kernel(trans, sizes, scaled, *refs):
    n = len(sizes)
    xs, w = refs[:n], refs[n]
    scale = refs[n + 1] if scaled else None
    outs = refs[n + 1 + scaled :]
    x = jnp.concatenate([r[...] for r in xs], axis=0) if n > 1 else xs[0][...]
    acc = dot(x, w[...], 1, 1 if trans else 0)
    if scaled:
        acc = acc * scale[...]
    at = 0
    for o in outs:
        o[...] = acc[at : at + o.shape[0]].astype(o.dtype)
        at += o.shape[0]


def mm(xs, w, *, trans=False, tile=512, scale=None, outs=None, name="mm"):
    depth = xs[0].shape[1]
    width = w.shape[0] if trans else w.shape[1]
    tile = min(tile, width)
    sizes = [x.shape[0] for x in xs]
    outs = outs or sizes
    scaled = scale is not None
    in_specs = [pl.BlockSpec((s, depth), lambda j: (0, 0)) for s in sizes]
    in_specs.append(
        pl.BlockSpec((tile, depth), lambda j: (j, 0))
        if trans
        else pl.BlockSpec((depth, tile), lambda j: (0, j))
    )
    args = [*xs, w]
    if scaled:
        in_specs.append(pl.BlockSpec((1, tile), lambda j: (0, j)))
        args.append(scale)
    rows = sum(sizes)
    return pl.pallas_call(
        functools.partial(mm_kernel, trans, sizes, scaled),
        grid=(width // tile,),
        in_specs=in_specs,
        out_specs=[pl.BlockSpec((s, tile), lambda j: (0, j)) for s in outs],
        out_shape=[jax.ShapeDtypeStruct((s, width), bf16) for s in outs],
        compiler_params=pltpu.CompilerParams(vmem_limit_bytes=VMEM_LIMIT),
        cost_estimate=pl.CostEstimate(
            flops=2 * rows * depth * width,
            bytes_accessed=2 * (rows * depth + depth * width + rows * width),
            transcendentals=0,
        ),
        name=name,
    )(*args)


def gelu_both(u):
    c = math.sqrt(2.0 / math.pi)
    square = u * u
    t = jnp.tanh(c * (u + 0.044715 * (u * square)))
    half = 0.5 * (1.0 + t)
    value = u * half
    slope = half + (0.5 * c) * u * (1.0 - t * t) * (1.0 + (3 * 0.044715) * square)
    return value, slope


def feed_kernel(tiles, x0, x1, c0, c1, up, down, hid, pre, y0, y1, g0, g1, acc_y, acc_g):
    j = pl.program_id(0)
    x = jnp.concatenate([x0[...], x1[...]], axis=0)
    c = jnp.concatenate([c0[...], c1[...]], axis=0)
    value, slope = gelu_both(dot(x, up[...], 1, 0))
    value = value.astype(bf16)
    hid[...] = value
    grad = (dot(c, down[...], 1, 1) * slope).astype(bf16)
    pre[...] = grad
    y = dot(value, down[...], 1, 0)
    g = dot(grad, up[...], 1, 1)

    @pl.when(j == 0)
    def _():
        acc_y[...] = y
        acc_g[...] = g

    @pl.when((j > 0) & (j < tiles - 1))
    def _():
        acc_y[...] += y
        acc_g[...] += g

    @pl.when(j == tiles - 1)
    def _():
        half = x0.shape[0]
        last_y, last_g = acc_y[...] + y, acc_g[...] + g
        y0[...] = last_y[:half].astype(bf16)
        y1[...] = last_y[half:].astype(bf16)
        g0[...] = last_g[:half].astype(bf16)
        g1[...] = last_g[half:].astype(bf16)


def feed_block(x, c, up, down, tile=512):
    half, width = x[0].shape
    units = up.shape[1]
    rows = 2 * half
    tiles = units // tile
    whole = pl.BlockSpec((half, width), lambda j: (0, 0))
    part = pl.BlockSpec((rows, tile), lambda j: (0, j))
    small = jax.ShapeDtypeStruct((half, width), bf16)
    big = jax.ShapeDtypeStruct((rows, units), bf16)
    hid, pre, y0, y1, g0, g1 = pl.pallas_call(
        functools.partial(feed_kernel, tiles),
        grid=(tiles,),
        in_specs=[
            whole,
            whole,
            whole,
            whole,
            pl.BlockSpec((width, tile), lambda j: (0, j)),
            pl.BlockSpec((tile, width), lambda j: (j, 0)),
        ],
        out_specs=[part, part, whole, whole, whole, whole],
        out_shape=[big, big, small, small, small, small],
        scratch_shapes=[pltpu.VMEM((rows, width), f32), pltpu.VMEM((rows, width), f32)],
        compiler_params=pltpu.CompilerParams(vmem_limit_bytes=VMEM_LIMIT),
        cost_estimate=pl.CostEstimate(
            flops=8 * rows * width * units,
            bytes_accessed=4 * (2 * rows * width + width * units + rows * units),
            transcendentals=rows * units,
        ),
        name="feed_block",
    )(*x, *c, up, down)
    return hid, pre, (y0, y1), (g0, g1)


def load_blocks(order, blocks, target):
    rows = blocks[0][0].shape[0] * 2
    for r, (low, high) in enumerate(blocks):
        at = pl.multiple_of((order[0] ^ r) * rows, rows)
        target[pl.ds(at, rows // 2), :] = low[...]
        target[pl.ds(at + rows // 2, rows // 2), :] = high[...]


def store_blocks(order, source, blocks, cast=None):
    rows = blocks[0][0].shape[0] * 2
    for r, (low, high) in enumerate(blocks):
        at = pl.multiple_of((order[0] ^ r) * rows, rows)
        low[...] = source[pl.ds(at, rows // 2), :].astype(low.dtype)
        high[...] = source[pl.ds(at + rows // 2, rows // 2), :].astype(high.dtype)


def pairs(refs):
    return [(refs[i], refs[i + 1]) for i in range(0, len(refs), 2)]


def allowed_of(seg_col, seg_row, q0, k0, k1, rows):
    same = seg_col[q0 : q0 + rows, :] == seg_row[:, k0:k1]
    shape = (rows, k1 - k0)
    i = lax.broadcasted_iota(jnp.int32, shape, 0) + q0
    j = lax.broadcasted_iota(jnp.int32, shape, 1) + k0
    return same & (j <= i)


def attend_kernel(nb, order, seg_col, seg_row, *refs):
    q_in, k_in, v_in = pairs(refs[: 2 * nb]), pairs(refs[2 * nb : 4 * nb]), pairs(refs[4 * nb : 6 * nb])
    out = pairs(refs[6 * nb : 8 * nb])
    q, k, v, o = refs[8 * nb :]
    load_blocks(order, q_in, q)
    load_blocks(order, k_in, k)
    load_blocks(order, v_in, v)
    step = CLIP_MOST
    for q0 in range(0, q.shape[0], step):
        k0, k1 = max(0, q0 - step), q0 + step
        s = dot(q[q0:k1, :], k[k0:k1, :], 1, 1)
        s = jnp.where(allowed_of(seg_col, seg_row, q0, k0, k1, step), s, masked_score)
        e = jnp.exp(s - jnp.max(s, axis=-1, keepdims=True))
        p = (e * (1.0 / jnp.sum(e, axis=-1, keepdims=True))).astype(bf16)
        o[q0:k1, :] = dot(p, v[k0:k1, :], 1, 0)
    store_blocks(order, o, out)


def attend_specs(blocks, heads):
    half = blocks[0][0].shape[0]
    specs, args = [], []
    for which in range(3):
        for low, high in blocks:
            for value in (low, high):
                specs.append(pl.BlockSpec((half, HEAD_DIM), lambda h, o, w=which: (0, w * heads + h)))
                args.append(value)
    return specs, args


def attend(order, seg, blocks):
    nb = len(blocks)
    half = blocks[0][0].shape[0]
    heads = blocks[0][0].shape[1] // (3 * HEAD_DIM)
    length = seg.shape[0]
    specs, args = attend_specs(blocks, heads)
    outs = pl.pallas_call(
        functools.partial(attend_kernel, nb),
        grid_spec=pltpu.PrefetchScalarGridSpec(
            num_scalar_prefetch=1,
            grid=(heads,),
            in_specs=[
                pl.BlockSpec((length, 1), lambda h, o: (0, 0)),
                pl.BlockSpec((1, length), lambda h, o: (0, 0)),
                *specs,
            ],
            out_specs=[pl.BlockSpec((half, HEAD_DIM), lambda h, o: (0, h))] * (2 * nb),
            scratch_shapes=[pltpu.VMEM((length, HEAD_DIM), bf16)] * 3
            + [pltpu.VMEM((length, HEAD_DIM), f32)],
        ),
        out_shape=[jax.ShapeDtypeStruct((half, heads * HEAD_DIM), bf16)] * (2 * nb),
        compiler_params=pltpu.CompilerParams(vmem_limit_bytes=VMEM_LIMIT),
        cost_estimate=pl.CostEstimate(
            flops=4 * heads * length * 512 * HEAD_DIM,
            bytes_accessed=8 * heads * length * HEAD_DIM,
            transcendentals=heads * length * 512,
        ),
        name="attend",
    )(order, seg.reshape(length, 1), seg.reshape(1, length), *args)
    return pairs(outs)


def attend_back_kernel(nb, scale, order, seg_col, seg_row, *refs):
    q_in, k_in, v_in, c_in = (pairs(refs[i * 2 * nb : (i + 1) * 2 * nb]) for i in range(4))
    dq_out, dk_out, dv_out = (pairs(refs[i * 2 * nb : (i + 1) * 2 * nb]) for i in range(4, 7))
    q, k, v, c, dq, dk, dv = refs[14 * nb :]
    load_blocks(order, q_in, q)
    load_blocks(order, k_in, k)
    load_blocks(order, v_in, v)
    load_blocks(order, c_in, c)
    step = CLIP_MOST
    length = q.shape[0]
    for q0 in range(0, length, step):
        k0, k1 = max(0, q0 - step), q0 + step
        qb, cb, kb, vb = q[q0:k1, :], c[q0:k1, :], k[k0:k1, :], v[k0:k1, :]
        s = dot(qb, kb, 1, 1)
        s = jnp.where(allowed_of(seg_col, seg_row, q0, k0, k1, step), s, masked_score)
        e = jnp.exp(s - jnp.max(s, axis=-1, keepdims=True))
        p = e * (1.0 / jnp.sum(e, axis=-1, keepdims=True))
        dp = dot(cb, vb, 1, 1)
        inner = jnp.sum(p * dp, axis=-1, keepdims=True)
        ds = (p * (dp - inner)).astype(bf16)
        dq[q0:k1, :] = dot(ds, kb, 1, 0) * scale
        dkb = dot(ds, qb, 0, 0)
        dvb = dot(p.astype(bf16), cb, 0, 0)
        if q0 > 0:
            dk[k0:q0, :] += dkb[:step]
            dv[k0:q0, :] += dvb[:step]
            dkb, dvb = dkb[step:], dvb[step:]
        dk[q0:k1, :] = dkb
        dv[q0:k1, :] = dvb
    store_blocks(order, dq, dq_out)
    store_blocks(order, dk, dk_out)
    store_blocks(order, dv, dv_out)


def attend_back(order, seg, blocks, grads, scale):
    nb = len(blocks)
    half = blocks[0][0].shape[0]
    heads = blocks[0][0].shape[1] // (3 * HEAD_DIM)
    length = seg.shape[0]
    specs, args = attend_specs(blocks, heads)
    for low, high in grads:
        specs += [pl.BlockSpec((half, HEAD_DIM), lambda h, o: (0, h))] * 2
        args += [low, high]
    outs = pl.pallas_call(
        functools.partial(attend_back_kernel, nb, scale),
        grid_spec=pltpu.PrefetchScalarGridSpec(
            num_scalar_prefetch=1,
            grid=(heads,),
            in_specs=[
                pl.BlockSpec((length, 1), lambda h, o: (0, 0)),
                pl.BlockSpec((1, length), lambda h, o: (0, 0)),
                *specs,
            ],
            out_specs=[pl.BlockSpec((half, HEAD_DIM), lambda h, o: (0, h))] * (6 * nb),
            scratch_shapes=[pltpu.VMEM((length, HEAD_DIM), bf16)] * 4
            + [pltpu.VMEM((length, HEAD_DIM), f32)] * 3,
        ),
        out_shape=[jax.ShapeDtypeStruct((half, heads * HEAD_DIM), bf16)] * (6 * nb),
        compiler_params=pltpu.CompilerParams(vmem_limit_bytes=VMEM_LIMIT),
        cost_estimate=pl.CostEstimate(
            flops=10 * heads * length * 512 * HEAD_DIM,
            bytes_accessed=14 * heads * length * HEAD_DIM,
            transcendentals=heads * length * 512,
        ),
        name="attend_back",
    )(order, seg.reshape(length, 1), seg.reshape(1, length), *args)
    outs = [pairs(outs[i * 2 * nb : (i + 1) * 2 * nb]) for i in range(3)]
    return [
        tuple(jnp.concatenate([outs[w][b][i] for w in range(3)], axis=1) for i in range(2))
        for b in range(nb)
    ]


def rows_of(blocks):
    return jnp.concatenate([half for block in blocks for half in block], axis=0)


def weight_grad(left, right):
    return lax.dot_general(left, right, (((0,), (0,)), ((), ())), preferred_element_type=f32).astype(bf16)


def scatter_sum(value, dim):
    return lax.psum_scatter(value, "dp", scatter_dimension=dim, tiled=True).astype(f32)


def local(
    group_count,
    tokens,
    segment_ids,
    query_weight,
    key_weight,
    value_weight,
    out_weight,
    up_weight,
    down_weight,
    attn_gain,
    mlp_gain,
    out_cotangent,
):
    group = Group(group_count)
    seq_count, length = segment_ids.shape
    per_seq = group_count // seq_count
    score_scale = 1.0 / math.sqrt(HEAD_DIM)
    me = lax.axis_index("mp")
    order = (me % per_seq).astype(jnp.int32).reshape(1)
    half = tokens.shape[0] // 2
    columns = query_weight.shape[1]

    def halves(value):
        return value[:half], value[half:]

    segs = [
        lax.dynamic_index_in_dim(segment_ids, (me // per_seq) ^ s, 0, keepdims=False)
        for s in range(seq_count)
    ]
    residual_in = [part.astype(f32) for part in halves(tokens)]
    normed = [norm_rows(part, attn_gain).astype(bf16) for part in residual_in]
    attn_in = group.gather(*normed)
    cot = group.gather(*halves(out_cotangent))

    qkv_weight = jnp.concatenate([query_weight, key_weight, value_weight], axis=1)
    qkv_scale = jnp.concatenate(
        [jnp.full((1, columns), score_scale, f32), jnp.ones((1, 2 * columns), f32)], axis=1
    )
    qkv = [mm(block, qkv_weight, scale=qkv_scale, name="qkv") for block in attn_in]
    context = []
    for s in range(seq_count):
        context += attend(order, segs[s], qkv[s * per_seq : (s + 1) * per_seq])
    attn_parts = [mm(block, out_weight, name="out_proj") for block in context]
    attn_rows = group.reduce(attn_parts)
    residual_mid = [residual_in[i] + total(attn_rows[i]) for i in range(2)]
    normed_mid = [norm_rows(part, mlp_gain).astype(bf16) for part in residual_mid]
    mlp_in = group.gather(*normed_mid)

    fed = [feed_block(mlp_in[r], cot[r], up_weight, down_weight) for r in range(group_count)]
    mlp_rows = group.reduce([f[2] for f in fed])
    mid_rows = group.reduce([f[3] for f in fed])
    hidden = jnp.concatenate([f[0] for f in fed], axis=0)
    pre_grad = jnp.concatenate([f[1] for f in fed], axis=0)
    layer_output = jnp.concatenate(
        [(residual_mid[i] + total(mlp_rows[i])).astype(bf16) for i in range(2)], axis=0
    )
    down_grad = scatter_sum(weight_grad(hidden, rows_of(cot)), 1)
    up_grad = scatter_sum(weight_grad(rows_of(mlp_in), pre_grad), 0)

    middle, mlp_gain_grad = [], 0.0
    for i in range(2):
        back, gain_grad = norm_back(residual_mid[i], mlp_gain, total(mid_rows[i]))
        middle.append(halves(out_cotangent)[i].astype(f32) + back)
        mlp_gain_grad = mlp_gain_grad + gain_grad
    middle_all = group.gather(*[part.astype(bf16) for part in middle])
    context_grad = [mm(block, out_weight, trans=True, name="context_grad") for block in middle_all]
    out_grad = scatter_sum(weight_grad(rows_of(context), rows_of(middle_all)), 1)

    qkv_grad = []
    for s in range(seq_count):
        at = slice(s * per_seq, (s + 1) * per_seq)
        qkv_grad += attend_back(order, segs[s], qkv[at], context_grad[at], score_scale)
    parts = [mm(block, qkv_weight, trans=True, name="qkv_back") for block in qkv_grad]
    attn_back_rows = group.reduce(parts)
    qkv_weight_grad = scatter_sum(weight_grad(rows_of(attn_in), rows_of(qkv_grad)), 0)

    tokens_grad, attn_gain_grad = [], 0.0
    for i in range(2):
        back, gain_grad = norm_back(residual_in[i], attn_gain, total(attn_back_rows[i]))
        tokens_grad.append(middle[i] + back)
        attn_gain_grad = attn_gain_grad + gain_grad
    attn_gain_grad, mlp_gain_grad = lax.psum((attn_gain_grad, mlp_gain_grad), ("dp", "mp"))
    return (
        layer_output,
        jnp.concatenate(tokens_grad, axis=0),
        qkv_weight_grad[:, :columns],
        qkv_weight_grad[:, columns : 2 * columns],
        qkv_weight_grad[:, 2 * columns :],
        out_grad,
        up_grad,
        down_grad,
        attn_gain_grad,
        mlp_gain_grad,
    )


def solution(mesh):
    return jax.shard_map(
        functools.partial(local, mesh.shape["mp"]),
        mesh=mesh,
        in_specs=(
            P(("dp", "mp"), None),
            P("dp", None),
            P(None, "mp"),
            P(None, "mp"),
            P(None, "mp"),
            P("mp", None),
            P(None, "mp"),
            P("mp", None),
            P(),
            P(),
            P(("dp", "mp"), None),
        ),
        out_specs=(
            P(("dp", "mp"), None),
            P(("dp", "mp"), None),
            P("dp", "mp"),
            P("dp", "mp"),
            P("dp", "mp"),
            P("mp", "dp"),
            P("dp", "mp"),
            P("mp", "dp"),
            P(),
            P(),
        ),
        check_vma=False,
    )
```

```python
import functools
import math

import jax
import jax.numpy as jnp
from jax import lax
from jax.experimental import pallas as pl
from jax.experimental.pallas import tpu as pltpu
from jax.sharding import PartitionSpec as P

HEAD_DIM = 128
CLIP_MOST = 256
epsilon = 1e-05
masked_score = -1e30
bf16, f32 = jnp.bfloat16, jnp.float32
VMEM_LIMIT = 60 * 1024 * 1024
MESH = pl.DeviceIdType.MESH
COST = 20


def dot(a, b, ca, cb):
    return lax.dot_general(a, b, (((ca,), (cb,)), ((), ())), preferred_element_type=f32)


def shape(dims, kind=bf16):
    return jax.ShapeDtypeStruct(dims, kind)


def call(kernel, args, grid, in_specs, out_specs, outs, *, name, scalars=(), scratch=(), after=(), flops=0, moved=0, **extra):
    lead = len(scalars) + len(args)

    def body(*refs):
        kernel(*refs[:lead], *refs[lead + len(after) :])

    return pl.pallas_call(
        body,
        grid_spec=pltpu.PrefetchScalarGridSpec(
            num_scalar_prefetch=len(scalars),
            grid=grid,
            in_specs=[*in_specs, *[pl.BlockSpec(memory_space=pl.ANY)] * len(after)],
            out_specs=out_specs,
            scratch_shapes=list(scratch),
        ),
        out_shape=outs,
        compiler_params=pltpu.CompilerParams(vmem_limit_bytes=VMEM_LIMIT, **extra),
        cost_estimate=pl.CostEstimate(flops=flops // COST, bytes_accessed=moved // COST, transcendentals=0),
        name=name,
    )(*scalars, *args, *after)


class Group:
    def __init__(self, count):
        self.count = count

    def swap(self, value, r):
        return lax.ppermute(value, "mp", [(m, m ^ r) for m in range(self.count)])

    def gather(self, low, high):
        if self.count == 4:
            low_x, high_y = self.swap(low, 1), self.swap(high, 2)
            high_x, low_y = self.swap(high, 1), self.swap(low, 2)
            low_d, high_d = self.swap(low_x, 2), self.swap(high_y, 1)
            return [(low, high), (low_x, high_x), (low_y, high_y), (low_d, high_d)]
        me = lax.axis_index("mp")
        blocks = lax.all_gather(jnp.concatenate([low, high]), "mp")
        half = low.shape[0]
        out = []
        for r in range(self.count):
            block = lax.dynamic_index_in_dim(blocks, me ^ r, 0, keepdims=False)
            out.append((block[:half], block[half:]))
        return out

    def reduce(self, parts):
        if self.count == 4:
            got_x, got_y = self.swap(parts[3][0], 1), self.swap(parts[3][1], 2)
            early_x, early_y = self.swap(parts[1][0], 1), self.swap(parts[2][1], 2)
            late_x = self.swap(add_rows([parts[1][1], got_y]), 1)
            late_y = self.swap(add_rows([parts[2][0], got_x]), 2)
            return [(parts[0][0], early_x, late_y), (parts[0][1], late_x, early_y)]
        me = lax.axis_index("mp")
        blocks = jnp.stack([jnp.concatenate(p) for p in parts])
        blocks = jnp.take(blocks, jnp.arange(self.count) ^ me, axis=0)
        own = lax.psum_scatter(blocks, "mp", scatter_dimension=0, tiled=False)
        half = own.shape[0] // 2
        return [(own[:half],), (own[half:],)]


def add_rows(values, kind=bf16):
    rows, width = values[0].shape
    tile = rows // 2

    def kernel(*refs):
        out = refs[-1]
        sum_ = refs[0][...].astype(f32)
        for r in refs[1:-1]:
            sum_ = sum_ + r[...].astype(f32)
        out[...] = sum_.astype(out.dtype)

    spec = pl.BlockSpec((tile, width), lambda i: (i, 0))
    return call(
        kernel,
        values,
        (2,),
        [spec] * len(values),
        spec,
        shape((rows, width), kind),
        name="add_rows",
        flops=rows * width,
        moved=2 * rows * width * (len(values) + 1),
    )


def norm_parts(values):
    centred = values - jnp.mean(values, axis=-1, keepdims=True)
    spread = jnp.mean(centred * centred, axis=-1, keepdims=True)
    scale = lax.rsqrt(spread + epsilon)
    return centred * scale, scale


def norm_back(values, gain, grad):
    unit, scale = norm_parts(values)
    q = grad * gain
    back = scale * (
        q - jnp.mean(q, axis=-1, keepdims=True) - unit * jnp.mean(q * unit, axis=-1, keepdims=True)
    )
    return back, jnp.sum(grad * unit, axis=0, keepdims=True)


def row_stage(fn, ins, outs, *, name, after=(), steps=2):
    half, width = next((v[0].shape if k == "pair" else (v.shape[0] // 2, v.shape[1])) for k, v in ins if k != "vec")
    tile = half // steps
    low_map, high_map = (lambda i: (jnp.minimum(i, steps - 1), 0)), (lambda i: (jnp.maximum(i - steps, 0), 0))

    def specs(kind):
        if kind == "pair":
            return [pl.BlockSpec((tile, width), low_map), pl.BlockSpec((tile, width), high_map)]
        if kind == "whole":
            return [pl.BlockSpec((tile, width), lambda i: (i, 0))]
        return [pl.BlockSpec((1, width), lambda i: (0, 0))]

    def side_of(kinds, refs, side):
        out, at = [], 0
        for kind in kinds:
            out.append(refs[at + (side if kind == "pair" else 0)])
            at += 2 if kind == "pair" else 1
        return out

    in_kinds, out_kinds = [k for k, _ in ins], [k for k, _ in outs]
    n_in = sum(2 if k == "pair" else 1 for k in in_kinds)

    def kernel(*refs):
        i = pl.program_id(0)

        def run(side):
            values = fn(*[r[...] for r in side_of(in_kinds, refs[:n_in], side)])
            for kind, ref, value in zip(out_kinds, side_of(out_kinds, refs[n_in:], side), values):
                if kind == "vec":

                    @pl.when(i == 0)
                    def _():
                        ref[...] = value

                    @pl.when(i > 0)
                    def _():
                        ref[...] += value
                else:
                    ref[...] = value.astype(ref.dtype)

        pl.when(i < steps)(lambda: run(0))
        pl.when(i >= steps)(lambda: run(1))

    args, in_specs, out_specs, out_shapes = [], [], [], []
    for kind, value in ins:
        args += list(value) if kind == "pair" else [value]
        in_specs += specs(kind)
    for kind, dtype in outs:
        out_specs += specs(kind)
        out_shapes += {
            "pair": [shape((half, width), dtype)] * 2,
            "whole": [shape((2 * half, width), dtype)],
            "vec": [shape((1, width), dtype)],
        }[kind]
    got = call(
        kernel,
        args,
        (2 * steps,),
        in_specs,
        out_specs,
        out_shapes,
        name=name,
        after=after,
        flops=20 * half * width,
        moved=8 * half * width * (len(ins) + len(outs)),
    )
    out, at = [], 0
    for kind in out_kinds:
        out.append((got[at], got[at + 1]) if kind == "pair" else got[at])
        at += 2 if kind == "pair" else 1
    return out


def terms(rows):
    return [("pair", (low, high)) for low, high in zip(*rows)]


def total(values):
    out = values[0].astype(f32)
    for v in values[1:]:
        out = out + v.astype(f32)
    return out


def mm(blocks, w, *, trans=False, tile=512, scale=None, name="mm", after=()):
    xs = [half for block in blocks for half in block]
    depth = xs[0].shape[1]
    width = w.shape[0] if trans else w.shape[1]
    tile = min(tile, width)
    sizes = [x.shape[0] for x in xs]
    n = len(xs)

    def kernel(*refs):
        outs = refs[-n:]
        x = jnp.concatenate([r[...] for r in refs[:n]], axis=0)
        acc = dot(x, refs[n][...], 1, 1 if trans else 0)
        if scale is not None:
            acc = acc * refs[n + 1][...]
        at = 0
        for o in outs:
            o[...] = acc[at : at + o.shape[0]].astype(o.dtype)
            at += o.shape[0]

    in_specs = [pl.BlockSpec((s, depth), lambda j: (0, 0)) for s in sizes]
    in_specs.append(
        pl.BlockSpec((tile, depth), lambda j: (j, 0)) if trans else pl.BlockSpec((depth, tile), lambda j: (0, j))
    )
    args = [*xs, w]
    if scale is not None:
        in_specs.append(pl.BlockSpec((1, tile), lambda j: (0, j)))
        args.append(scale)
    rows = sum(sizes)
    got = call(
        kernel,
        args,
        (width // tile,),
        in_specs,
        [pl.BlockSpec((s, tile), lambda j: (0, j)) for s in sizes],
        [shape((s, width)) for s in sizes],
        name=name,
        after=after,
        flops=2 * rows * depth * width,
        moved=2 * (rows * depth + depth * width + rows * width),
    )
    return pairs(got)


def pairs(refs):
    return [(refs[i], refs[i + 1]) for i in range(0, len(refs), 2)]


def gelu_both(u):
    c = math.sqrt(2.0 / math.pi)
    square = u * u
    t = jnp.tanh(c * (u + 0.044715 * (u * square)))
    half = 0.5 * (1.0 + t)
    value = u * half
    slope = half + (0.5 * c) * u * (1.0 - t * t) * (1.0 + (3 * 0.044715) * square)
    return value, slope


def feed_kernel(tiles, x0, x1, c0, c1, up, down, hid, pre, y0, y1, g0, g1, acc_y, acc_g):
    j = pl.program_id(0)
    x = jnp.concatenate([x0[...], x1[...]], axis=0)
    c = jnp.concatenate([c0[...], c1[...]], axis=0)
    value, slope = gelu_both(dot(x, up[...], 1, 0))
    value = value.astype(bf16)
    hid[...] = value
    grad = (dot(c, down[...], 1, 1) * slope).astype(bf16)
    pre[...] = grad
    y = dot(value, down[...], 1, 0)
    g = dot(grad, up[...], 1, 1)

    @pl.when(j == 0)
    def _():
        acc_y[...] = y
        acc_g[...] = g

    @pl.when((j > 0) & (j < tiles - 1))
    def _():
        acc_y[...] += y
        acc_g[...] += g

    @pl.when(j == tiles - 1)
    def _():
        half = x0.shape[0]
        last_y, last_g = acc_y[...] + y, acc_g[...] + g
        y0[...] = last_y[:half].astype(bf16)
        y1[...] = last_y[half:].astype(bf16)
        g0[...] = last_g[:half].astype(bf16)
        g1[...] = last_g[half:].astype(bf16)


def feed_block(x, c, up, down, tile=512, after=()):
    half, width = x[0].shape
    units = up.shape[1]
    rows = 2 * half
    tiles = units // tile
    whole = pl.BlockSpec((half, width), lambda j: (0, 0))
    part = pl.BlockSpec((rows, tile), lambda j: (0, j))
    small, big = shape((half, width)), shape((rows, units))
    hid, pre, y0, y1, g0, g1 = call(
        functools.partial(feed_kernel, tiles),
        [*x, *c, up, down],
        (tiles,),
        [
            whole,
            whole,
            whole,
            whole,
            pl.BlockSpec((width, tile), lambda j: (0, j)),
            pl.BlockSpec((tile, width), lambda j: (j, 0)),
        ],
        [part, part, whole, whole, whole, whole],
        [big, big, small, small, small, small],
        scratch=[pltpu.VMEM((rows, width), f32), pltpu.VMEM((rows, width), f32)],
        name="feed_block",
        after=after,
        flops=8 * rows * width * units,
        moved=4 * (2 * rows * width + width * units + rows * units),
    )
    return hid, pre, (y0, y1), (g0, g1)


def load_blocks(order, blocks, target):
    rows = blocks[0][0].shape[0] * 2
    for r, (low, high) in enumerate(blocks):
        at = pl.multiple_of((order[0] ^ r) * rows, rows)
        target[pl.ds(at, rows // 2), :] = low[...]
        target[pl.ds(at + rows // 2, rows // 2), :] = high[...]


def store_blocks(order, source, blocks, column=None):
    rows = blocks[0][0].shape[0] * 2
    for r, block in enumerate(blocks):
        at = pl.multiple_of((order[0] ^ r) * rows, rows)
        for i, ref in enumerate(block):
            value = source[pl.ds(at + i * (rows // 2), rows // 2), :].astype(ref.dtype)
            if column is None:
                ref[...] = value
            else:
                ref[:, pl.ds(column, HEAD_DIM)] = value


def allowed_of(seg_col, seg_row, q0, k0, k1, rows):
    same = seg_col[q0 : q0 + rows, :] == seg_row[:, k0:k1]
    dims = (rows, k1 - k0)
    i = lax.broadcasted_iota(jnp.int32, dims, 0) + q0
    j = lax.broadcasted_iota(jnp.int32, dims, 1) + k0
    return same & (j <= i)


def attend_kernel(nb, order, seg_col, seg_row, *refs):
    q_in, k_in, v_in = (pairs(refs[i * 2 * nb : (i + 1) * 2 * nb]) for i in range(3))
    out = pairs(refs[6 * nb : 8 * nb])
    q, k, v, o = refs[8 * nb :]
    load_blocks(order, q_in, q)
    load_blocks(order, k_in, k)
    load_blocks(order, v_in, v)
    step = CLIP_MOST
    for q0 in range(0, q.shape[0], step):
        k0, k1 = max(0, q0 - step), q0 + step
        s = dot(q[q0:k1, :], k[k0:k1, :], 1, 1)
        s = jnp.where(allowed_of(seg_col, seg_row, q0, k0, k1, step), s, masked_score)
        e = jnp.exp(s - jnp.max(s, axis=-1, keepdims=True))
        p = (e * (1.0 / jnp.sum(e, axis=-1, keepdims=True))).astype(bf16)
        o[q0:k1, :] = dot(p, v[k0:k1, :], 1, 0)
    store_blocks(order, o, out)


def attend_specs(blocks, heads, seg):
    half = blocks[0][0].shape[0]
    length = seg.shape[0]
    specs = [pl.BlockSpec((length, 1), lambda h, o: (0, 0)), pl.BlockSpec((1, length), lambda h, o: (0, 0))]
    args = [seg.reshape(length, 1), seg.reshape(1, length)]
    for which in range(3):
        for block in blocks:
            for value in block:
                specs.append(pl.BlockSpec((half, HEAD_DIM), lambda h, o, w=which: (0, w * heads + h)))
                args.append(value)
    return specs, args


def attend(order, seg, blocks, after=()):
    nb = len(blocks)
    half = blocks[0][0].shape[0]
    heads = blocks[0][0].shape[1] // (3 * HEAD_DIM)
    length = seg.shape[0]
    specs, args = attend_specs(blocks, heads, seg)
    outs = call(
        functools.partial(attend_kernel, nb),
        args,
        (heads,),
        specs,
        [pl.BlockSpec((half, HEAD_DIM), lambda h, o: (0, h))] * (2 * nb),
        [shape((half, heads * HEAD_DIM))] * (2 * nb),
        scalars=[order],
        scratch=[pltpu.VMEM((length, HEAD_DIM), bf16)] * 3 + [pltpu.VMEM((length, HEAD_DIM), f32)],
        name="attend",
        after=after,
        flops=4 * heads * length * 512 * HEAD_DIM,
        moved=8 * heads * length * HEAD_DIM,
    )
    return pairs(outs)


def attend_back_kernel(nb, heads, scale, order, seg_col, seg_row, *refs):
    q_in, k_in, v_in, c_in = (pairs(refs[i * 2 * nb : (i + 1) * 2 * nb]) for i in range(4))
    out = pairs(refs[8 * nb : 10 * nb])
    q, k, v, c, dq, dk, dv = refs[10 * nb :]
    load_blocks(order, q_in, q)
    load_blocks(order, k_in, k)
    load_blocks(order, v_in, v)
    load_blocks(order, c_in, c)
    step = CLIP_MOST
    for q0 in range(0, q.shape[0], step):
        k0, k1 = max(0, q0 - step), q0 + step
        qb, cb, kb, vb = q[q0:k1, :], c[q0:k1, :], k[k0:k1, :], v[k0:k1, :]
        s = dot(qb, kb, 1, 1)
        s = jnp.where(allowed_of(seg_col, seg_row, q0, k0, k1, step), s, masked_score)
        e = jnp.exp(s - jnp.max(s, axis=-1, keepdims=True))
        p = e * (1.0 / jnp.sum(e, axis=-1, keepdims=True))
        dp = dot(cb, vb, 1, 1)
        inner = jnp.sum(p * dp, axis=-1, keepdims=True)
        ds = (p * (dp - inner)).astype(bf16)
        dq[q0:k1, :] = dot(ds, kb, 1, 0) * scale
        dkb = dot(ds, qb, 0, 0)
        dvb = dot(p.astype(bf16), cb, 0, 0)
        if q0 > 0:
            dk[k0:q0, :] += dkb[:step]
            dv[k0:q0, :] += dvb[:step]
            dkb, dvb = dkb[step:], dvb[step:]
        dk[q0:k1, :] = dkb
        dv[q0:k1, :] = dvb
    column = pl.multiple_of(pl.program_id(0) * HEAD_DIM, HEAD_DIM)
    for which, source in enumerate((dq, dk, dv)):
        store_blocks(order, source, out, column + which * heads * HEAD_DIM)


def attend_back(order, seg, blocks, grads, scale, after=()):
    nb = len(blocks)
    half, width = blocks[0][0].shape
    heads = width // (3 * HEAD_DIM)
    length = seg.shape[0]
    specs, args = attend_specs(blocks, heads, seg)
    for low, high in grads:
        specs += [pl.BlockSpec((half, HEAD_DIM), lambda h, o: (0, h))] * 2
        args += [low, high]
    outs = call(
        functools.partial(attend_back_kernel, nb, heads, scale),
        args,
        (heads,),
        specs,
        [pl.BlockSpec((half, width), lambda h, o: (0, 0))] * (2 * nb),
        [shape((half, width))] * (2 * nb),
        scalars=[order],
        scratch=[pltpu.VMEM((length, HEAD_DIM), bf16)] * 4 + [pltpu.VMEM((length, HEAD_DIM), f32)] * 3,
        name="attend_back",
        after=after,
        flops=10 * heads * length * 512 * HEAD_DIM,
        moved=14 * heads * length * HEAD_DIM,
    )
    return pairs(outs)


class Shares:
    def __init__(self, count):
        self.count = count
        self.split = count == 8
        me = lax.axis_index("dp")
        self.core, self.z = (me % 2).astype(jnp.int32), (me // 2).astype(jnp.int32)

    def product(self, lefts, rights, by_left, which=None, plus=None, after=(), name="weight_grad"):
        rows, right_rows = [l.shape[0] for l in lefts], [r.shape[0] for r in rights]
        depth, width = lefts[0].shape[1], rights[0].shape[1]
        n, count = len(rows), self.count
        both = n + len(rights)
        stack = count // 2 if which is not None else count
        left_tile = depth // count if by_left else min(512, depth)
        right_tile = width if by_left else width // count
        dims = (stack, left_tile if by_left else depth, right_tile)
        scalars = [which.reshape(1)] if which is not None else []
        share = (lambda s, w: 2 * s + w[0][0]) if which is not None else (lambda s, w: s)
        if by_left:
            grid = (stack,)
            left_map = lambda s, *w: (0, share(s, w))
            right_map = lambda s, *w: (0, 0)
            out_spec = pl.BlockSpec((1, left_tile, right_tile), lambda s, *w: (s, 0, 0))
            scratch = []
        else:
            grid = (depth // left_tile, stack)
            left_map = lambda i, s, *w: (0, i)
            right_map = lambda i, s, *w: (0, share(s, w))
            out_spec = pl.BlockSpec((1, left_tile, right_tile), lambda i, s, *w: (s, i, 0))
            scratch = [pltpu.VMEM((left_tile, sum(rows)), bf16)]

        def kernel(*refs):
            refs = refs[len(scalars) :]
            ls, rs = refs[:n], refs[n:both]
            out = refs[both + (plus is not None)]
            right = jnp.concatenate([r[...] for r in rs], axis=0)
            if by_left:
                left = jnp.concatenate([l[...] for l in ls], axis=0)
                acc = dot(left, right, 0, 0)
            else:
                turned = refs[-1]

                @pl.when(pl.program_id(1) == 0)
                def _():
                    at = 0
                    for l in ls:
                        turned[:, at : at + l.shape[0]] = l[...].T
                        at += l.shape[0]

                acc = dot(turned[...], right, 1, 0)
            if plus is not None:
                acc = acc + refs[both][0].astype(f32)
            out[0] = acc.astype(bf16)

        return call(
            kernel,
            [*lefts, *rights, *([plus] if plus is not None else [])],
            grid,
            [pl.BlockSpec((r, left_tile), left_map) for r in rows]
            + [pl.BlockSpec((r, right_tile), right_map) for r in right_rows]
            + ([out_spec] if plus is not None else []),
            out_spec,
            shape(dims),
            scalars=scalars,
            scratch=scratch,
            name=name,
            after=after,
            flops=2 * sum(rows) * depth * width * stack // count,
            moved=2 * (sum(rows) * (depth + width) + depth * width),
        )

    def send(self, value, moves):
        return lax.ppermute(value, "dp", moves)

    def first(self, lefts, rights, by_left, after=(), name="weight_grad"):
        if not self.split:
            return None
        other = self.product(lefts, rights, by_left, 1 - self.core, after=after, name=name)
        return self.send(other, [(d, d ^ 1) for d in range(8)])

    def second(self, lefts, rights, by_left, got, after=(), name="weight_grad"):
        if not self.split:
            return self.product(lefts, rights, by_left, after=after, name=name)
        return self.product(lefts, rights, by_left, self.core, plus=got, after=after, name=name)

    def along(self, step, sources):
        return [(2 * z + c, 2 * (z + step) + c) for z in sources for c in range(2)]

    def line(self, mine, columns):
        if not self.split:
            summed = lax.psum_scatter(mine, "dp", scatter_dimension=0, tiled=False)
            return share_sum(summed[None], jnp.zeros((1,), jnp.int32), [], f32, columns)
        z = self.z
        right = self.send(mine[3], self.along(1, [0]))
        left = self.send(mine[0], self.along(-1, [3]))
        pick = lambda at: jnp.clip(at, 0, 3).reshape(1)
        right = self.send(share_sum(mine, pick(z + 2), [right], bf16), self.along(1, [0, 1]))
        left = self.send(share_sum(mine, pick(z - 2), [left], bf16), self.along(-1, [3, 2]))
        right = self.send(share_sum(mine, pick(z + 1), [right], bf16), self.along(1, [0, 1, 2]))
        left = self.send(share_sum(mine, pick(z - 1), [left], bf16), self.along(-1, [3, 2, 1]))
        return share_sum(mine, z.reshape(1), [right, left], f32, columns)


def share_sum(stack, at, others, kind, columns=None):
    _, rows, width = stack.shape
    tile = rows // 2 if rows % 32 == 0 else rows
    cuts = columns or [width]

    def kernel(_, own, *refs):
        value = own[0].astype(f32)
        for r in refs[: len(others)]:
            value = value + r[...].astype(f32)
        at = 0
        for out in refs[len(others) :]:
            out[...] = value[:, at : at + out.shape[1]].astype(out.dtype)
            at += out.shape[1]

    spec = pl.BlockSpec((tile, width), lambda i, a: (i, 0))
    got = call(
        kernel,
        [stack, *others],
        (rows // tile,),
        [pl.BlockSpec((1, tile, width), lambda i, a: (a[0], i, 0))] + [spec] * len(others),
        [pl.BlockSpec((tile, c), lambda i, a: (i, 0)) for c in cuts],
        [shape((rows, c), kind) for c in cuts],
        scalars=[at],
        name="share_sum",
        flops=rows * width,
        moved=rows * width * 6,
    )
    return got if columns else got[0]


def everyone_kernel(mp, dp, x, out, near, far, sum_, send_near, recv_near, send_far, recv_far):
    m, d = lax.axis_index("mp"), lax.axis_index("dp")
    barrier = pltpu.get_barrier_semaphore()
    for r in range(1, mp):
        pl.semaphore_signal(barrier, inc=1, device_id={"mp": lax.rem(m + r, mp)}, device_id_type=MESH)
    for r in range(1, dp):
        pl.semaphore_signal(barrier, inc=1, device_id={"dp": lax.rem(d + r, dp)}, device_id_type=MESH)
    pl.semaphore_wait(barrier, mp + dp - 2)

    def exchange(source, slots, me, count, axis, send, recv):
        copies = []
        for r in range(1, count):
            copy = pltpu.make_async_remote_copy(
                src_ref=source,
                dst_ref=slots.at[me],
                send_sem=send.at[r],
                recv_sem=recv.at[r],
                device_id={axis: lax.rem(me + r, count)},
                device_id_type=MESH,
            )
            copy.start()
            copies.append(copy)
        slots[pl.ds(me, 1)] = source[...][None]
        for copy in copies:
            copy.wait()
        value = slots[0]
        for r in range(1, count):
            value = value + slots[r]
        return value

    sum_[...] = exchange(x, near, m, mp, "mp", send_near, recv_near)
    out[...] = exchange(sum_, far, d, dp, "dp", send_far, recv_far)


def everyone(x, mp, dp):
    vmem = pl.BlockSpec(memory_space=pltpu.VMEM)
    return pl.pallas_call(
        functools.partial(everyone_kernel, mp, dp),
        in_specs=[vmem],
        out_specs=vmem,
        out_shape=jax.ShapeDtypeStruct(x.shape, f32),
        scratch_shapes=[
            pltpu.VMEM((mp, *x.shape), f32),
            pltpu.VMEM((dp, *x.shape), f32),
            pltpu.VMEM(x.shape, f32),
            pltpu.SemaphoreType.DMA((mp,)),
            pltpu.SemaphoreType.DMA((mp,)),
            pltpu.SemaphoreType.DMA((dp,)),
            pltpu.SemaphoreType.DMA((dp,)),
        ],
        compiler_params=pltpu.CompilerParams(collective_id=0, has_side_effects=True),
        name="everyone",
    )(x)


def halves_of(blocks):
    return [half for block in blocks for half in block]


def local(
    mp,
    dp,
    tokens,
    segment_ids,
    query_weight,
    key_weight,
    value_weight,
    out_weight,
    up_weight,
    down_weight,
    attn_gain,
    mlp_gain,
    out_cotangent,
):
    group, shares = Group(mp), Shares(dp)
    seq_count, length = segment_ids.shape
    per_seq = mp // seq_count
    score_scale = 1.0 / math.sqrt(HEAD_DIM)
    me = lax.axis_index("mp")
    order = (me % per_seq).astype(jnp.int32).reshape(1)
    half, width = tokens.shape[0] // 2, tokens.shape[1]
    columns = query_weight.shape[1]
    attn_gain, mlp_gain = attn_gain.reshape(1, width), mlp_gain.reshape(1, width)
    segs = [
        lax.dynamic_index_in_dim(segment_ids, (me // per_seq) ^ s, 0, keepdims=False)
        for s in range(seq_count)
    ]

    def seq(s):
        return slice(s * per_seq, (s + 1) * per_seq)

    (normed,) = row_stage(
        lambda v, g: (norm_parts(v.astype(f32))[0] * g,),
        [("whole", tokens), ("vec", attn_gain)],
        [("pair", bf16)],
        name="norm_first",
    )
    attn_in = group.gather(*normed)
    cot = group.gather(out_cotangent[:half], out_cotangent[half:])
    parts = lax.optimization_barrier((query_weight, key_weight, value_weight, normed[0]))
    qkv_weight = jnp.concatenate(parts[:3], axis=1)
    qkv_scale = jnp.concatenate(
        [jnp.full((1, columns), score_scale, f32), jnp.ones((1, 2 * columns), f32)], axis=1
    )
    project = functools.partial(mm, w=qkv_weight, scale=qkv_scale, name="qkv")
    last = mp - 1
    qkv = project(attn_in[:1])
    qkv += project(attn_in[1:last], after=[qkv[0][0]])
    context = []
    if seq_count > 1:
        context += attend(order, segs[0], qkv[seq(0)])
        qkv += project(attn_in[last:], after=[context[0][0]])
    else:
        qkv += project(attn_in[last:])
    for s in range(len(context) // per_seq, seq_count):
        context += attend(order, segs[s], qkv[seq(s)])
    part_d = mm(context[last:], out_weight, tile=1024, name="out_proj")
    part_rest = mm(context[:last], out_weight, name="out_proj", after=[part_d[0][0]])
    attn_rows = group.reduce(part_rest + part_d)

    residual_mid, normed_mid = row_stage(
        lambda v, g, *t: (lambda r: (r, norm_parts(r)[0] * g))(v.astype(f32) + total(t)),
        [("whole", tokens), ("vec", mlp_gain), *terms(attn_rows)],
        [("whole", f32), ("pair", bf16)],
        name="norm_second",
    )
    mlp_in = group.gather(*normed_mid)
    fed = []
    for r in range(mp):
        fed.append(feed_block(mlp_in[r], cot[r], up_weight, down_weight, after=[f[0] for f in fed[-1:]]))
    mid_rows = group.reduce([f[3] for f in fed])
    hidden, pre_grad = [f[0] for f in fed], [f[1] for f in fed]
    cot_halves, mlp_halves = halves_of(cot), halves_of(mlp_in)
    down_args = (hidden, cot_halves, False)
    down_got = shares.first(*down_args, name="down_grad")
    down_mine = shares.second(*down_args, down_got, name="down_grad")
    down_grad = shares.line(down_mine, [width // dp])[0]

    mlp_rows = group.reduce([f[2] for f in fed])
    middle, middle_low, mlp_gain_grad = row_stage(
        lambda r, g, c, *t: (lambda b: (c.astype(f32) + b[0], c.astype(f32) + b[0], b[1]))(norm_back(r, g, total(t))),
        [("whole", residual_mid), ("vec", mlp_gain), ("whole", out_cotangent), *terms(mid_rows)],
        [("whole", f32), ("pair", bf16), ("vec", f32)],
        name="norm_second_back",
        after=[down_mine],
    )
    middle_all = group.gather(*middle_low)
    up_args = (mlp_halves, pre_grad, True)
    up_got = shares.first(*up_args, after=[middle_low[0]], name="up_grad")
    up_mine = shares.second(*up_args, up_got, name="up_grad")
    up_grad = shares.line(up_mine, [up_weight.shape[1]])[0]
    (layer_output,) = row_stage(
        lambda r, *t: (r + total(t),),
        [("whole", residual_mid), *terms(mlp_rows)],
        [("whole", bf16)],
        name="output",
        after=[up_mine],
    )

    back = functools.partial(mm, w=out_weight, trans=True, name="context_grad")
    context_grad = back(middle_all[:1], after=[up_mine])
    context_grad += back(middle_all[1:last], after=[context_grad[0][0]])
    qkv_grad = []
    for s in range(seq_count):
        if s == seq_count - 1:
            context_grad += back(middle_all[last:], after=[g[0] for g in qkv_grad[:1]])
        qkv_grad += attend_back(order, segs[s], qkv[seq(s)], context_grad[seq(s)], score_scale)
    part_d = mm(qkv_grad[last:], qkv_weight, trans=True, tile=1024, name="qkv_back")
    qkv_args = (halves_of(attn_in), halves_of(qkv_grad), True)
    qkv_got = shares.first(*qkv_args, after=[part_d[0][0]], name="qkv_grad")
    part_rest = mm(qkv_grad[:last], qkv_weight, trans=True, name="qkv_back", after=[qkv_got] if qkv_got is not None else [])
    qkv_mine = shares.second(*qkv_args, qkv_got, name="qkv_grad", after=[part_rest[0][0]])
    attn_back_rows = group.reduce(part_rest + part_d)
    out_args = (halves_of(context), halves_of(middle_all), False)
    out_got = shares.first(*out_args, after=[qkv_mine], name="out_grad")
    out_mine = shares.second(*out_args, out_got, name="out_grad")
    qkv_weight_grads = shares.line(qkv_mine, [columns] * 3)
    out_grad = shares.line(out_mine, [width // dp])[0]

    tokens_grad, attn_gain_grad = row_stage(
        lambda v, m, g, *t: (lambda b: (m + b[0], b[1]))(norm_back(v.astype(f32), g, total(t))),
        [("whole", tokens), ("whole", middle), ("vec", attn_gain), *terms(attn_back_rows)],
        [("whole", f32), ("vec", f32)],
        name="norm_first_back",
    )
    gains = jnp.concatenate([attn_gain_grad, mlp_gain_grad], axis=0).reshape(8, width // 4)
    gains = everyone(gains, mp, dp).reshape(2, width)
    return (layer_output, tokens_grad, *qkv_weight_grads, out_grad, up_grad, down_grad, gains[0], gains[1])


def solution(mesh):
    return jax.shard_map(
        functools.partial(local, mesh.shape["mp"], mesh.shape["dp"]),
        mesh=mesh,
        in_specs=(
            P(("dp", "mp"), None),
            P("dp", None),
            P(None, "mp"),
            P(None, "mp"),
            P(None, "mp"),
            P("mp", None),
            P(None, "mp"),
            P("mp", None),
            P(),
            P(),
            P(("dp", "mp"), None),
        ),
        out_specs=(
            P(("dp", "mp"), None),
            P(("dp", "mp"), None),
            P("dp", "mp"),
            P("dp", "mp"),
            P("dp", "mp"),
            P("mp", "dp"),
            P("dp", "mp"),
            P("mp", "dp"),
            P(),
            P(),
        ),
        check_vma=False,
    )
```

```python
import functools
import math
from types import SimpleNamespace as Names

import jax
import jax.numpy as jnp
from jax import lax
from jax.experimental import pallas as pl
from jax.experimental.pallas import tpu as pltpu
from jax.sharding import PartitionSpec as P

HEAD_DIM = 128
CLIP_MOST = 256
epsilon = 1e-05
masked_score = -1e30
bf16, f32 = jnp.bfloat16, jnp.float32
VMEM_LIMIT = 60 * 1024 * 1024
MESH = pl.DeviceIdType.MESH
WHOLE, VEC = range(2)
DP, MP = BOTH = ("dp", "mp")


def dot(a, b, ca, cb):
    return lax.dot_general(a, b, (((ca,), (cb,)), ((), ())), preferred_element_type=f32)


def shape(dims, kind=bf16):
    return jax.ShapeDtypeStruct(dims, kind)


def call(kernel, args, grid, in_specs, out_specs, outs, *, name, scalars=(), scratch=(), after=(), flops=0, moved=0, **extra):
    lead = len(scalars) + len(args)

    def body(*refs):
        kernel(*refs[:lead], *refs[lead + len(after) :])

    return pl.pallas_call(
        body,
        grid_spec=pltpu.PrefetchScalarGridSpec(
            num_scalar_prefetch=len(scalars),
            grid=grid,
            in_specs=[*in_specs, *[pl.BlockSpec(memory_space=pl.ANY)] * len(after)],
            out_specs=out_specs,
            scratch_shapes=list(scratch),
        ),
        out_shape=outs,
        compiler_params=pltpu.CompilerParams(vmem_limit_bytes=VMEM_LIMIT, **extra),
        cost_estimate=pl.CostEstimate(flops=flops, bytes_accessed=moved, transcendentals=0),
        name=name,
    )(*scalars, *args, *after)


def norm_parts(values):
    centred = values - jnp.mean(values, axis=-1, keepdims=True)
    spread = jnp.mean(centred * centred, axis=-1, keepdims=True)
    scale = lax.rsqrt(spread + epsilon)
    return centred * scale, scale


def norm_back(values, gain, grad):
    unit, scale = norm_parts(values)
    q = grad * gain
    back = scale * (
        q - jnp.mean(q, axis=-1, keepdims=True) - unit * jnp.mean(q * unit, axis=-1, keepdims=True)
    )
    return back, jnp.sum(grad * unit, axis=0, keepdims=True)


def row_stage(fn, ins, outs, *, name, steps=4):
    rows, width = ins[0][1].shape
    tile = rows // steps

    def spec(kind):
        return pl.BlockSpec((tile, width), lambda i: (i, 0)) if kind == WHOLE else pl.BlockSpec((1, width), lambda i: (0, 0))

    def kernel(*refs):
        i = pl.program_id(0)
        for (kind, _), ref, value in zip(outs, refs[len(ins) :], fn(*[r[...] for r in refs[: len(ins)]])):
            if kind == VEC:
                value = jnp.where(i == 0, value, ref[...] + value)
            ref[...] = value.astype(ref.dtype)

    return call(
        kernel,
        [v for _, v in ins],
        (steps,),
        [spec(k) for k, _ in ins],
        [spec(k) for k, _ in outs],
        [shape((rows, width) if k == WHOLE else (1, width), t) for k, t in outs],
        name=name,
        flops=20 * rows * width,
        moved=4 * rows * width * (len(ins) + len(outs)),
    )


def total(values):
    out = values[0].astype(f32)
    for v in values[1:]:
        out = out + v.astype(f32)
    return out


def gelu_both(u):
    c = math.sqrt(2.0 / math.pi)
    square = u * u
    t = jnp.tanh(c * (u + 0.044715 * (u * square)))
    half = 0.5 * (1.0 + t)
    value = u * half
    slope = half + (0.5 * c) * u * (1.0 - t * t) * (1.0 + (3 * 0.044715) * square)
    return value, slope


def allowed_of(seg_col, seg_row, q0, k0, k1, rows):
    same = seg_col[q0 : q0 + rows, :] == seg_row[:, k0:k1]
    dims = (rows, k1 - k0)
    i = lax.broadcasted_iota(jnp.int32, dims, 0) + q0
    j = lax.broadcasted_iota(jnp.int32, dims, 1) + k0
    return same & (j <= i)


def everyone_kernel(mp, dp, x, out, near, far, sum_, send_near, recv_near, send_far, recv_far):
    m, d = lax.axis_index(MP), lax.axis_index(DP)
    barrier = pltpu.get_barrier_semaphore()
    for r in range(1, mp):
        pl.semaphore_signal(barrier, inc=1, device_id={MP: lax.rem(m + r, mp)}, device_id_type=MESH)
    for r in range(1, dp):
        pl.semaphore_signal(barrier, inc=1, device_id={DP: lax.rem(d + r, dp)}, device_id_type=MESH)
    pl.semaphore_wait(barrier, mp + dp - 2)

    def exchange(source, slots, me, count, axis, send, recv):
        copies = []
        for r in range(1, count):
            copy = pltpu.make_async_remote_copy(
                src_ref=source,
                dst_ref=slots.at[me],
                send_sem=send.at[r],
                recv_sem=recv.at[r],
                device_id={axis: lax.rem(me + r, count)},
                device_id_type=MESH,
            )
            copy.start()
            copies.append(copy)
        slots[pl.ds(me, 1)] = source[...][None]
        for copy in copies:
            copy.wait()
        value = slots[0]
        for r in range(1, count):
            value = value + slots[r]
        return value

    sum_[...] = exchange(x, near, m, mp, MP, send_near, recv_near)
    out[...] = exchange(sum_, far, d, dp, DP, send_far, recv_far)


def everyone(x, mp, dp):
    vmem = pl.BlockSpec(memory_space=pltpu.VMEM)
    return pl.pallas_call(
        functools.partial(everyone_kernel, mp, dp),
        in_specs=[vmem],
        out_specs=vmem,
        out_shape=jax.ShapeDtypeStruct(x.shape, f32),
        scratch_shapes=[
            pltpu.VMEM((mp, *x.shape), f32),
            pltpu.VMEM((dp, *x.shape), f32),
            pltpu.VMEM(x.shape, f32),
            pltpu.SemaphoreType.DMA((mp,)),
            pltpu.SemaphoreType.DMA((mp,)),
            pltpu.SemaphoreType.DMA((dp,)),
            pltpu.SemaphoreType.DMA((dp,)),
        ],
        compiler_params=pltpu.CompilerParams(collective_id=0, has_side_effects=True),
        name="everyone",
    )(x)


class Wire:
    def __init__(self, send, recv):
        self.send, self.recv, self.count, self.ends = send, recv, 0, []

    def slot(self):
        self.count += 1
        return self.count - 1

    def copy(self, slot, source, target, to):
        return pltpu.make_async_remote_copy(
            src_ref=source,
            dst_ref=target,
            send_sem=self.send.at[slot],
            recv_sem=self.recv.at[slot],
            device_id=to,
            device_id_type=MESH,
        )

    def go(self, source, target, to):
        copy = self.copy(self.slot(), source, target, to)
        copy.start()
        self.ends.append(copy)
        return copy

    def sent(self, *copies):
        for copy in copies:
            copy.wait_send()
            self.ends = [c for c in self.ends if c is not copy]

    def finish(self):
        self.sent(*list(self.ends))


def stage(body, grid, ins, outs):
    pltpu.emit_pipeline(
        body,
        grid=grid,
        in_specs=[pl.BlockSpec(b, f) for _, b, f in ins],
        out_specs=[pl.BlockSpec(b, f) for _, b, f in outs],
    )(*[r for r, _, _ in ins], *[r for r, _, _ in outs])


def layer_kernel(dims, tree, *refs):
    half, width, columns, units, length = dims
    full = 2 * half
    rows = 4 * full
    r = named(jax.tree.unflatten(tree, refs))
    m, d = lax.axis_index(MP), lax.axis_index(DP)
    core, z = lax.rem(d, 2), d // 2
    parity = lax.rem(m, 2)
    to_x = {MP: m + 1 - 2 * parity}
    to_y = {MP: m + 2 - 4 * (m // 2)}
    to_core = {DP: d + 1 - 2 * core}
    wire = Wire(r.send, r.recv)
    heads = columns // HEAD_DIM
    score_scale = 1.0 / math.sqrt(HEAD_DIM)

    barrier = pltpu.get_barrier_semaphore()
    for peer in (to_x, to_y, to_core):
        pl.semaphore_signal(barrier, inc=1, device_id=peer, device_id_type=MESH)
    for step in (1, -1):

        @pl.when((z + step >= 0) & (z + step < 4))
        def _():
            pl.semaphore_signal(barrier, inc=1, device_id={DP: d + 2 * step}, device_id_type=MESH)

    pl.semaphore_wait(barrier, jnp.where((z == 0) | (z == 3), 4, 5))

    def at(ref, block):
        return ref.at[pl.ds(block * half, half)]

    qkv_w = r.qkv_w
    loads = [
        pltpu.make_async_copy(w, qkv_w.at[:, pl.ds(i * columns, columns)], r.load.at[i])
        for i, w in enumerate((r.query_weight, r.key_weight, r.value_weight))
    ]
    for load in loads:
        load.start()

    tile = half // 2

    def row_ins(*values):
        out = []
        for v in values:
            ref, f = v if isinstance(v, tuple) else (v, lambda i: (i, 0))
            out.append((ref, (1 if ref.shape[0] == 1 else tile, width), (lambda i: (0, 0)) if ref.shape[0] == 1 else f))
        return out

    def row_wise(fn, ins, outs):
        n = len(ins)

        def body(*refs):
            for ref, value in zip(refs[n:], fn(*[x[...] for x in refs[:n]])):
                ref[...] = value.astype(ref.dtype)

        stage(body, (4,), row_ins(*ins), row_ins(*outs))

    def spread(ref):
        return {
            2: wire.go(at(ref, 0), at(ref, 2), to_x),
            5: wire.go(at(ref, 1), at(ref, 5), to_y),
            3: wire.go(at(ref, 1), at(ref, 3), to_x),
            4: wire.go(at(ref, 0), at(ref, 4), to_y),
        }

    def relay(ref):
        return {6: wire.go(at(ref, 2), at(ref, 6), to_y), 7: wire.go(at(ref, 5), at(ref, 7), to_x)}

    def send_far(into, terms):
        return [wire.go(at(terms, 6), at(into.far, 0), to_x), wire.go(at(terms, 7), at(into.far, 1), to_y)]

    def send_early(into, terms):
        return [wire.go(at(terms, 2), at(into.early, 0), to_x), wire.go(at(terms, 5), at(into.early, 1), to_y)]

    def send_late(into, terms, far, sums):
        for copy in far:
            copy.wait_recv()
        row_wise(
            lambda a, b: (a.astype(f32) + b.astype(f32),),
            [(terms, lambda i: (jnp.where(i < 2, 8 + i, 4 + i), 0)), into.far],
            [sums],
        )
        return [wire.go(at(sums, 0), at(into.late, 0), to_y), wire.go(at(sums, 1), at(into.late, 1), to_x)]

    def arrive(*copies):
        for copy in copies:
            copy.wait_recv()

    def product(source, target, blocks, weight, size, count, trans=False, scale=None):
        n = len(blocks)
        depth = source.shape[1]
        ref, ref_block, ref_map = weight if isinstance(weight, tuple) else (None, None, None)

        def body(*refs):
            j = pl.program_id(0)
            x = jnp.concatenate([b[...] for b in refs[:n]], axis=0) if n > 1 else refs[0][...]
            w = refs[n][...] if ref is not None else weight(j)
            acc = dot(x, w, 1, 1 if trans else 0)
            if scale is not None:
                acc = acc * scale(j)
            for i, out in enumerate(refs[-n:]):
                out[...] = acc[i * half : (i + 1) * half].astype(bf16)

        stage(
            body,
            (count,),
            [(source, (half, depth), lambda j, b=b: (b, 0)) for b in blocks]
            + ([(ref, ref_block, ref_map)] if ref is not None else []),
            [(target, (half, size), lambda j, b=b: (b, j)) for b in blocks],
        )

    def project(*blocks):
        product(
            r.attn_in,
            r.qkv,
            blocks,
            lambda j: qkv_w[:, pl.ds(pl.multiple_of(j * columns, columns), columns)],
            columns,
            3,
            scale=lambda j: jnp.where(j == 0, score_scale, 1.0),
        )

    def out_project(*blocks):
        product(
            r.context,
            r.out_terms,
            blocks,
            (r.out_weight, (columns, width // 2), lambda j: (0, j)),
            width // 2,
            2,
        )

    def context_back(*blocks):
        product(
            r.middle_all,
            r.context_grad,
            blocks,
            (r.out_weight, (columns // 2, width), lambda j: (j, 0)),
            columns // 2,
            2,
            trans=True,
        )

    def project_back(*blocks):
        size = width // 4
        product(
            r.qkv_grad,
            r.out_terms,
            blocks,
            lambda j: qkv_w[pl.ds(pl.multiple_of(j * size, size), size), :],
            size,
            4,
            trans=True,
        )

    def turn(block, target):
        for b in range(2):
            to = pl.multiple_of(lax.rem(parity + b, 2) * full, full)
            target[pl.ds(to, full), :] = block[b * full : (b + 1) * full, :]

    def turn_back(source, block):
        for b in range(2):
            come = pl.multiple_of(lax.rem(parity + b, 2) * full, full)
            block[b * full : (b + 1) * full, :] = source[pl.ds(come, full), :].astype(bf16)

    q, k, v, c = r.q, r.k, r.v, r.c
    f0, f1, f2 = r.f0, r.f1, r.f2

    def head_ins(s):
        ins = [
            (r.seg_col, (1, length, 1), lambda h: (s, 0, 0)),
            (r.seg_row, (1, 1, length), lambda h: (s, 0, 0)),
        ]
        for which in range(3):
            ins.append((r.qkv, (length, HEAD_DIM), lambda h, w=which: (s, w * heads + h)))
        return ins

    def scores_of(seg_col, seg_row, q0, k0, k1):
        s = dot(q[q0:k1, :], k[k0:k1, :], 1, 1)
        keep = allowed_of(seg_col.at[0], seg_row.at[0], q0, k0, k1, CLIP_MOST)
        s = jnp.where(keep, s, masked_score)
        e = jnp.exp(s - jnp.max(s, axis=-1, keepdims=True))
        return e * (1.0 / jnp.sum(e, axis=-1, keepdims=True))

    def attend(s):
        def body(seg_col, seg_row, q_in, k_in, v_in, out):
            turn(q_in, q)
            turn(k_in, k)
            turn(v_in, v)
            for q0 in range(0, length, CLIP_MOST):
                k0, k1 = max(0, q0 - CLIP_MOST), q0 + CLIP_MOST
                p = scores_of(seg_col, seg_row, q0, k0, k1).astype(bf16)
                f0[q0:k1, :] = dot(p, v[k0:k1, :], 1, 0)
            turn_back(f0, out)

        stage(body, (heads,), head_ins(s), [(r.context, (length, HEAD_DIM), lambda h: (s, h))])

    def attend_back(s):
        def body(seg_col, seg_row, q_in, k_in, v_in, c_in, dq_out, dk_out, dv_out):
            turn(q_in, q)
            turn(k_in, k)
            turn(v_in, v)
            turn(c_in, c)
            for q0 in range(0, length, CLIP_MOST):
                k0, k1 = max(0, q0 - CLIP_MOST), q0 + CLIP_MOST
                p = scores_of(seg_col, seg_row, q0, k0, k1)
                qb, cb, kb, vb = q[q0:k1, :], c[q0:k1, :], k[k0:k1, :], v[k0:k1, :]
                dp = dot(cb, vb, 1, 1)
                inner = jnp.sum(p * dp, axis=-1, keepdims=True)
                ds = (p * (dp - inner)).astype(bf16)
                f0[q0:k1, :] = dot(ds, kb, 1, 0) * score_scale
                dk, dv = dot(ds, qb, 0, 0), dot(p.astype(bf16), cb, 0, 0)
                if q0 > 0:
                    f1[k0:q0, :] += dk[:CLIP_MOST]
                    f2[k0:q0, :] += dv[:CLIP_MOST]
                    dk, dv = dk[CLIP_MOST:], dv[CLIP_MOST:]
                f1[q0:k1, :] = dk
                f2[q0:k1, :] = dv
            turn_back(f0, dq_out)
            turn_back(f1, dk_out)
            turn_back(f2, dv_out)

        stage(
            body,
            (heads,),
            [*head_ins(s), (r.context_grad, (length, HEAD_DIM), lambda h: (s, h))],
            [(r.qkv_grad, (length, HEAD_DIM), lambda h, w=w: (s, w * heads + h)) for w in range(3)],
        )

    acc_y, acc_g = r.acc_y, r.acc_g

    def feed(a, b):
        size = 512
        tiles = units // size

        def body(x0, x1, c0, c1, up, down, h0, h1, p0, p1, y0, y1, g0, g1):
            j = pl.program_id(0)
            x = jnp.concatenate([x0[...], x1[...]], axis=0)
            cot = jnp.concatenate([c0[...], c1[...]], axis=0)
            value, slope = gelu_both(dot(x, up[...], 1, 0))
            value = value.astype(bf16)
            h0[...], h1[...] = value[:half], value[half:]
            grad = (dot(cot, down[...], 1, 1) * slope).astype(bf16)
            p0[...], p1[...] = grad[:half], grad[half:]
            y = dot(value, down[...], 1, 0)
            g = dot(grad, up[...], 1, 1)

            @pl.when(j == 0)
            def _():
                acc_y[...] = y
                acc_g[...] = g

            @pl.when((j > 0) & (j < tiles - 1))
            def _():
                acc_y[...] += y
                acc_g[...] += g

            @pl.when(j == tiles - 1)
            def _():
                last_y, last_g = acc_y[...] + y, acc_g[...] + g
                y0[...], y1[...] = last_y[:half].astype(bf16), last_y[half:].astype(bf16)
                g0[...], g1[...] = last_g[:half].astype(bf16), last_g[half:].astype(bf16)

        both = (a, b)
        whole = lambda ref: [(ref, (half, width), lambda j, i=i: (i, 0)) for i in both]
        part = lambda ref: [(ref, (half, size), lambda j, i=i: (i, j)) for i in both]
        stage(
            body,
            (tiles,),
            [
                *whole(r.mlp_in),
                *whole(r.cot_all),
                (r.up_weight, (width, size), lambda j: (0, j)),
                (r.down_weight, (size, width), lambda j: (j, 0)),
            ],
            [*part(r.hidden), *part(r.pre_grad), *whole(r.mlp_terms), *whole(r.mid_terms)],
        )

    def grad_product(left, right, which, target, plus=None):
        share = left.shape[1] // 8
        size = min(1024, right.shape[1]) if right.shape[1] % 1024 == 0 else right.shape[1] // (2 if right.shape[1] > 512 else 1)

        def body(a, b, *rest):
            acc = dot(a[...], b[...], 0, 0)
            if plus is not None:
                acc = acc + rest[0][0].astype(f32)
            rest[-1][0] = acc.astype(bf16)

        block = (1, share, size)
        place = lambda n, s: (s, 0, n)
        stage(
            body,
            (right.shape[1] // size, 4),
            [
                (left, (rows, share), lambda n, s: (0, 2 * s + which)),
                (right, (rows, size), lambda n, s: (0, n)),
                *([(plus, block, place)] if plus is not None else []),
            ],
            [(target, block, place)],
        )

    def grad_first(into, left, right):
        grad_product(left, right, 1 - core, into.mine)
        return wire.go(into.mine, into.got, to_core)

    def line(mine, got, sums, step, place):
        pick = lambda at: jnp.clip(at if step > 0 else 3 - at, 0, 3)
        slots = [wire.slot() for _ in range(3)]
        to = {DP: jnp.clip(d + 2 * step, 0, 7)}

        def copy(t, source):
            return wire.copy(slots[t], source, got.at[t], to)

        @pl.when(place == 0)
        def _():
            for t in range(3):
                copy(t, mine.at[pick(3 - t)]).start()

        def forward(t):
            @pl.when((place >= 1) & (place <= t + 1))
            def _():
                copy(t, mine.at[0]).wait_recv()
                n = mine.shape[2]
                size = mine.shape[1] // 2

                def body(a, b, out):
                    out[...] = (a[0].astype(f32) + b[...].astype(f32)).astype(bf16)

                stage(
                    body,
                    (2,),
                    [
                        (mine, (1, size, n), lambda i: (pick(place + 2 - t), i, 0)),
                        (got.at[t], (size, n), lambda i: (i, 0)),
                    ],
                    [(sums.at[t], (size, n), lambda i: (i, 0))],
                )
                copy(t + 1, sums.at[t]).start()

        def end():
            @pl.when(place >= 1)
            def _():
                copy(2, mine.at[0]).wait_recv()

            for t in range(3):

                @pl.when((place <= t) & (place < 3))
                def _():
                    copy(t, mine.at[0]).wait_send()

        return forward, end

    def grad_second(into, left, right, swap):
        swap.wait_recv()
        wire.sent(swap)
        grad_product(left, right, core, into.mine, into.got)
        up = line(into.mine, into.right, into.right_sums, 1, z)
        down = line(into.mine, into.left, into.left_sums, -1, 3 - z)

        def forward(t):
            up[0](t)
            down[0](t)

        def end():
            up[1]()
            down[1]()

        return forward, end

    attn_in, cot_all, mlp_in, middle_all = r.attn_in, r.cot_all, r.mlp_in, r.middle_all
    row_wise(
        lambda x, g: (norm_parts(x.astype(f32))[0] * g,), [r.tokens, r.attn_gain], [attn_in]
    )
    near = spread(attn_in)
    row_wise(lambda x: (x,), [r.out_cotangent], [cot_all])
    for load in loads:
        load.wait()
    project(0, 1)
    arrive(near[2], near[5])
    far = relay(attn_in)
    arrive(near[3], near[4])
    cot_near = {2: wire.go(at(cot_all, 0), at(cot_all, 2), to_x), 5: wire.go(at(cot_all, 1), at(cot_all, 5), to_y)}
    project(2, 3, 4, 5)
    attend(0)
    arrive(far[6], far[7])
    project(6, 7)
    attend(1)
    out_terms = r.out_terms
    out_project(6, 7)
    attn_far = send_far(r.attn, out_terms)
    out_project(2, 3, 4, 5)
    attn_early = send_early(r.attn, out_terms)
    out_project(0, 1)
    attn_late = send_late(r.attn, out_terms, attn_far, r.sums_a)
    cot_near[3] = wire.go(at(cot_all, 1), at(cot_all, 3), to_x)
    cot_near[4] = wire.go(at(cot_all, 0), at(cot_all, 4), to_y)
    arrive(*attn_early, *attn_late)

    def second(x, g, a, b, c_):
        mid = x.astype(f32) + a.astype(f32) + b.astype(f32) + c_.astype(f32)
        return mid, norm_parts(mid)[0] * g

    row_wise(
        second,
        [r.tokens, r.mlp_gain, out_terms, r.attn.early, r.attn.late],
        [r.residual_mid, mlp_in],
    )
    near = spread(mlp_in)
    arrive(cot_near[2], cot_near[5])
    cot_far = relay(cot_all)
    feed(0, 1)
    arrive(near[2], near[5])
    far = relay(mlp_in)
    feed(2, 5)
    mid_terms = r.mid_terms
    mid_early = send_early(r.mid, mid_terms)
    arrive(near[3], near[4], cot_near[3], cot_near[4])
    feed(3, 4)
    arrive(far[6], far[7], cot_far[6], cot_far[7])
    feed(6, 7)
    mid_far = send_far(r.mid, mid_terms)
    swap = grad_first(r.down_grad, cot_all, r.hidden)
    mid_late = send_late(r.mid, mid_terms, mid_far, r.sums_b)
    down_forward, down_end = grad_second(r.down_grad, cot_all, r.hidden, swap)
    arrive(*mid_early, *mid_late)
    gain_sum = r.mlp_gain_grad
    gain_sum[...] = jnp.zeros_like(gain_sum)

    def second_back(mid, g, cot, a, b, c_):
        back, gain = norm_back(mid, g, a.astype(f32) + b.astype(f32) + c_.astype(f32))
        gain_sum[...] += gain
        value = cot.astype(f32) + back
        return value, value

    row_wise(
        second_back,
        [r.residual_mid, r.mlp_gain, r.out_cotangent, mid_terms, r.mid.early, r.mid.late],
        [r.middle, middle_all],
    )
    near = spread(middle_all)
    swap = grad_first(r.up_grad, mlp_in, r.pre_grad)
    arrive(near[2], near[5])
    far = relay(middle_all)
    down_forward(0)
    up_forward, up_end = grad_second(r.up_grad, mlp_in, r.pre_grad, swap)

    context_back(0, 1)
    arrive(near[3], near[4])
    down_forward(1)
    context_back(2, 3, 4, 5)
    attend_back(0)
    arrive(far[6], far[7])
    mlp_terms = r.mlp_terms
    mlp_far = send_far(r.mlp, mlp_terms)
    context_back(6, 7)
    up_forward(0)
    attend_back(1)
    wire.sent(*attn_far, *attn_early)
    project_back(6, 7)
    back_far = send_far(r.back, out_terms)
    swap = grad_first(r.qkv_w_grad, attn_in, r.qkv_grad)
    project_back(2, 3, 4, 5)
    back_early = send_early(r.back, out_terms)
    up_forward(1)
    qkv_forward, qkv_end = grad_second(r.qkv_w_grad, attn_in, r.qkv_grad, swap)
    wire.sent(*mid_late)
    back_late = send_late(r.back, out_terms, back_far, r.sums_b)
    mlp_early = send_early(r.mlp, mlp_terms)
    swap = grad_first(r.out_grad, middle_all, r.context)
    wire.sent(*attn_late)
    mlp_late = send_late(r.mlp, mlp_terms, mlp_far, r.sums_a)
    project_back(0, 1)
    out_forward, out_end = grad_second(r.out_grad, middle_all, r.context, swap)
    qkv_forward(0)
    qkv_forward(1)
    out_forward(0)
    out_forward(1)
    arrive(*back_early, *back_late, *mlp_early, *mlp_late)
    down_end()
    up_end()
    qkv_end()
    out_end()
    wire.finish()


def named(tree):
    return Names(**{k: named(v) for k, v in tree.items()}) if isinstance(tree, dict) else tree


def layer(ins, half, width, columns, units, length):
    full, rows = 2 * half, 8 * half
    share = width // 8
    big, own = shape((rows, width)), shape((full, width))
    arrivals = dict(far=own, early=own, late=own)

    def grad(n):
        line, sums = shape((3, share, n)), shape((2, share, n))
        stack = shape((4, share, n))
        return dict(mine=stack, got=stack, right=line, left=line, right_sums=sums, left_sums=sums)

    outs = dict(
        attn_in=big,
        cot_all=big,
        mlp_in=big,
        middle_all=big,
        out_terms=big,
        mlp_terms=big,
        mid_terms=big,
        hidden=shape((rows, units)),
        pre_grad=shape((rows, units)),
        qkv=shape((rows, 3 * columns)),
        qkv_grad=shape((rows, 3 * columns)),
        context=shape((rows, columns)),
        context_grad=shape((rows, columns)),
        attn=arrivals,
        mid=arrivals,
        mlp=arrivals,
        back=arrivals,
        sums_a=own,
        sums_b=own,
        down_grad=grad(units),
        up_grad=grad(units),
        qkv_w_grad=grad(3 * columns),
        out_grad=grad(columns),
        residual_mid=shape((full, width), f32),
        middle=shape((full, width), f32),
    )
    any_, vmem = pl.BlockSpec(memory_space=pl.ANY), pl.BlockSpec(memory_space=pltpu.VMEM)
    places = dict(jax.tree.map(lambda _: any_, outs), mlp_gain_grad=vmem)
    outs = dict(outs, mlp_gain_grad=shape((1, width), f32))
    head, head_sum = pltpu.VMEM((length, HEAD_DIM), bf16), pltpu.VMEM((length, HEAD_DIM), f32)
    acc = pltpu.VMEM((full, width), f32)
    scratch = dict(
        qkv_w=pltpu.VMEM((width, 3 * columns), bf16),
        acc_y=acc,
        acc_g=acc,
        q=head,
        k=head,
        v=head,
        c=head,
        f0=head_sum,
        f1=head_sum,
        f2=head_sum,
        send=pltpu.SemaphoreType.DMA((96,)),
        recv=pltpu.SemaphoreType.DMA((96,)),
        load=pltpu.SemaphoreType.DMA((3,)),
    )
    parts = [jax.tree.flatten(t) for t in (ins, outs, scratch)]
    kinds = [jax.tree.unflatten(t, range(len(v))) for v, t in parts]
    starts = (0, len(parts[0][0]), len(parts[0][0]) + len(parts[1][0]))
    place_of = {}
    for kind, begin in zip(kinds, starts):
        place_of.update(jax.tree.map(lambda i, b=begin: b + i, kind))
    order, tree = jax.tree.flatten(place_of)

    def kernel(*refs):
        layer_kernel((half, width, columns, units, length), tree, *[refs[i] for i in order])

    got = pl.pallas_call(
        kernel,
        in_specs=[any_] * len(parts[0][0]),
        out_specs=jax.tree.leaves(places),
        out_shape=parts[1][0],
        scratch_shapes=parts[2][0],
        compiler_params=pltpu.CompilerParams(
            collective_id=1, has_side_effects=True, vmem_limit_bytes=VMEM_LIMIT
        ),
        name="layer",
    )(*parts[0][0])
    return named(jax.tree.unflatten(parts[1][1], got))


def share_total(got, z, turned, columns=None):
    mine, right, left = got.mine, got.right, got.left
    _, rows, width = mine.shape
    cuts = columns or [width]
    tile = 128

    def kernel(place, own, a, b, *outs):
        value = own[0].astype(f32)
        value = value + jnp.where(place[0] > 0, a[0].astype(f32), 0.0)
        value = value + jnp.where(place[0] < 3, b[0].astype(f32), 0.0)
        if turned:
            outs[0][...] = value.T
            return
        at = 0
        for out in outs:
            out[...] = value[:, at : at + out.shape[1]]
            at += out.shape[1]

    return call(
        kernel,
        [mine, right, left],
        (rows // tile,),
        [pl.BlockSpec((1, tile, width), lambda i, p: (p[0], i, 0))]
        + [pl.BlockSpec((1, tile, width), lambda i, p: (2, i, 0))] * 2,
        [pl.BlockSpec((width, tile), lambda i, p: (0, i))]
        if turned
        else [pl.BlockSpec((tile, c), lambda i, p: (i, 0)) for c in cuts],
        [shape((width, rows), f32)] if turned else [shape((rows, c), f32) for c in cuts],
        scalars=[z.astype(jnp.int32).reshape(1)],
        name="share_total",
        flops=rows * width,
        moved=rows * width * 10,
    )


def norm_rows(values, gain):
    centre = jnp.mean(values, axis=-1, keepdims=True)
    centred = values - centre
    spread = jnp.mean(centred * centred, axis=-1, keepdims=True)
    return centred * lax.rsqrt(spread + epsilon) * gain


def gelu_tanh(values):
    return jax.nn.gelu(values, approximate=True)


def block_allowed(segment):
    position = jnp.arange(segment.shape[0])
    return (position[None, :] <= position[:, None]) & (segment[:, None] == segment[None, :])


def rows_times(left_rows, right_matrix):
    return jnp.dot(left_rows, right_matrix, preferred_element_type=jnp.float32)


def rows_times_back(left_rows, right_matrix):
    return lax.dot_general(
        left_rows, right_matrix, (((1,), (1,)), ((), ())), preferred_element_type=jnp.float32
    )


def attn_input_back(
    queries_grad, keys_grad, values_grad, query_weight, key_weight, value_weight, score_scale
):
    total_grad = rows_times_back(queries_grad, query_weight) * score_scale
    total_grad = total_grad + rows_times_back(keys_grad, key_weight)
    return total_grad + rows_times_back(values_grad, value_weight)


def attend_forward(packed):
    queries, keys_in, values_in, segment = packed
    scores = jnp.einsum("qhd,khd->hqk", queries, keys_in, preferred_element_type=jnp.float32)
    scores = jnp.where(block_allowed(segment)[None], scores, masked_score)
    row_max = jnp.max(scores, axis=-1, keepdims=True)
    expanded = jnp.exp(scores - row_max)
    row_total = jnp.sum(expanded, axis=-1, keepdims=True)
    probs_low = (expanded / row_total).astype(jnp.bfloat16)
    context = jnp.einsum("hqk,khd->qhd", probs_low, values_in, preferred_element_type=jnp.float32)
    return (context.astype(jnp.bfloat16), (row_max + jnp.log(row_total))[:, :, 0])


def attend_backward(packed):
    queries, keys_in, values_in, segment, context_grad, log_total = packed
    scores = jnp.einsum("qhd,khd->hqk", queries, keys_in, preferred_element_type=jnp.float32)
    scores = jnp.where(block_allowed(segment)[None], scores, masked_score)
    attn_probs = jnp.exp(scores - log_total[:, :, None])
    probs_grad = jnp.einsum(
        "qhd,khd->hqk", context_grad, values_in, preferred_element_type=jnp.float32
    )
    values_grad = jnp.einsum(
        "hqk,qhd->khd",
        attn_probs.astype(jnp.bfloat16),
        context_grad,
        preferred_element_type=jnp.float32,
    )
    inner_sum = jnp.sum(attn_probs * probs_grad, axis=-1, keepdims=True)
    scores_grad = (attn_probs * (probs_grad - inner_sum)).astype(jnp.bfloat16)
    queries_grad = jnp.einsum(
        "hqk,khd->qhd", scores_grad, keys_in, preferred_element_type=jnp.float32
    )
    keys_grad = jnp.einsum("hqk,qhd->khd", scores_grad, queries, preferred_element_type=jnp.float32)
    return (
        queries_grad.astype(jnp.bfloat16),
        keys_grad.astype(jnp.bfloat16),
        values_grad.astype(jnp.bfloat16),
    )


def local_plain(
    tokens,
    segment_ids,
    query_weight,
    key_weight,
    value_weight,
    out_weight,
    up_weight,
    down_weight,
    attn_gain,
    mlp_gain,
    out_cotangent,
):
    seq_count, seq_length = segment_ids.shape
    group_rows = seq_count * seq_length
    head_count = query_weight.shape[1] // HEAD_DIM
    score_scale = 1.0 / math.sqrt(HEAD_DIM)
    shaped = (seq_count, seq_length, head_count, HEAD_DIM)
    flat_shape = (group_rows, head_count * HEAD_DIM)
    residual_in = tokens.astype(jnp.float32)
    normed_attn, attn_norm_back = jax.vjp(norm_rows, residual_in, attn_gain)
    gathered_attn = lax.all_gather(normed_attn.astype(jnp.bfloat16), MP, axis=0, tiled=True)
    queries = (
        jnp.dot(gathered_attn, query_weight, preferred_element_type=jnp.float32) * score_scale
    ).astype(jnp.bfloat16)
    keys_all = jnp.dot(gathered_attn, key_weight, preferred_element_type=jnp.float32).astype(
        jnp.bfloat16
    )
    values_all = jnp.dot(gathered_attn, value_weight, preferred_element_type=jnp.float32).astype(
        jnp.bfloat16
    )
    queries_seq = queries.reshape(shaped)
    keys_seq = keys_all.reshape(shaped)
    values_seq = values_all.reshape(shaped)
    context, log_total = lax.map(attend_forward, (queries_seq, keys_seq, values_seq, segment_ids))
    context_flat = context.reshape(flat_shape)
    attn_rows = lax.psum_scatter(
        rows_times(context_flat, out_weight).astype(jnp.bfloat16),
        MP,
        scatter_dimension=0,
        tiled=True,
    ).astype(jnp.float32)
    residual_mid = residual_in + attn_rows
    normed_mlp, mlp_norm_back = jax.vjp(norm_rows, residual_mid, mlp_gain)
    gathered_mlp = lax.all_gather(normed_mlp.astype(jnp.bfloat16), MP, axis=0, tiled=True)
    pre_act = jnp.dot(gathered_mlp, up_weight, preferred_element_type=jnp.float32)
    activated, gelu_back = jax.vjp(gelu_tanh, pre_act)
    hidden = activated.astype(jnp.bfloat16)
    mlp_rows = lax.psum_scatter(
        rows_times(hidden, down_weight).astype(jnp.bfloat16), MP, scatter_dimension=0, tiled=True
    ).astype(jnp.float32)
    layer_output = (residual_mid + mlp_rows).astype(jnp.bfloat16)
    cotangent_all = lax.all_gather(out_cotangent, MP, axis=0, tiled=True)
    down_weight_grad = jnp.einsum(
        "rf,rd->fd", hidden, cotangent_all, preferred_element_type=jnp.float32
    )
    hidden_grad = lax.dot_general(
        cotangent_all, down_weight, (((1,), (1,)), ((), ())), preferred_element_type=jnp.float32
    )
    pre_grad = gelu_back(hidden_grad)[0].astype(jnp.bfloat16)
    up_weight_grad = jnp.einsum(
        "rd,rf->df", gathered_mlp, pre_grad, preferred_element_type=jnp.float32
    )
    normed_mlp_grad = lax.psum_scatter(
        rows_times_back(pre_grad, up_weight).astype(jnp.bfloat16),
        MP,
        scatter_dimension=0,
        tiled=True,
    ).astype(jnp.float32)
    middle_back, mlp_gain_grad = mlp_norm_back(normed_mlp_grad)
    middle_grad = out_cotangent.astype(jnp.float32) + middle_back
    middle_all_grad = lax.all_gather(middle_grad.astype(jnp.bfloat16), MP, axis=0, tiled=True)
    out_weight_grad = jnp.einsum(
        "rc,rd->cd", context_flat, middle_all_grad, preferred_element_type=jnp.float32
    )
    context_grad = lax.dot_general(
        middle_all_grad, out_weight, (((1,), (1,)), ((), ())), preferred_element_type=jnp.float32
    ).astype(jnp.bfloat16)
    queries_grad, keys_grad, values_grad = lax.map(
        attend_backward,
        (queries_seq, keys_seq, values_seq, segment_ids, context_grad.reshape(shaped), log_total),
    )
    queries_grad = queries_grad.reshape(flat_shape)
    keys_grad = keys_grad.reshape(flat_shape)
    values_grad = values_grad.reshape(flat_shape)
    query_weight_grad = (
        jnp.einsum("rd,rc->dc", gathered_attn, queries_grad, preferred_element_type=jnp.float32)
        * score_scale
    )
    key_weight_grad = jnp.einsum(
        "rd,rc->dc", gathered_attn, keys_grad, preferred_element_type=jnp.float32
    )
    value_weight_grad = jnp.einsum(
        "rd,rc->dc", gathered_attn, values_grad, preferred_element_type=jnp.float32
    )
    normed_attn_grad = lax.psum_scatter(
        attn_input_back(
            queries_grad,
            keys_grad,
            values_grad,
            query_weight,
            key_weight,
            value_weight,
            score_scale,
        ).astype(jnp.bfloat16),
        MP,
        scatter_dimension=0,
        tiled=True,
    ).astype(jnp.float32)
    token_back, attn_gain_grad = attn_norm_back(normed_attn_grad)
    tokens_grad = middle_grad + token_back
    attn_gain_grad, mlp_gain_grad = lax.psum((attn_gain_grad, mlp_gain_grad), (DP, MP))
    (
        query_weight_grad,
        key_weight_grad,
        value_weight_grad,
        out_weight_grad,
        up_weight_grad,
        down_weight_grad,
    ) = (
        lax.psum_scatter(
            query_weight_grad.astype(jnp.bfloat16), DP, scatter_dimension=0, tiled=True
        ).astype(jnp.float32),
        lax.psum_scatter(
            key_weight_grad.astype(jnp.bfloat16), DP, scatter_dimension=0, tiled=True
        ).astype(jnp.float32),
        lax.psum_scatter(
            value_weight_grad.astype(jnp.bfloat16), DP, scatter_dimension=0, tiled=True
        ).astype(jnp.float32),
        lax.psum_scatter(
            out_weight_grad.astype(jnp.bfloat16), DP, scatter_dimension=1, tiled=True
        ).astype(jnp.float32),
        lax.psum_scatter(
            up_weight_grad.astype(jnp.bfloat16), DP, scatter_dimension=0, tiled=True
        ).astype(jnp.float32),
        lax.psum_scatter(
            down_weight_grad.astype(jnp.bfloat16), DP, scatter_dimension=1, tiled=True
        ).astype(jnp.float32),
    )
    return (
        layer_output,
        tokens_grad,
        query_weight_grad,
        key_weight_grad,
        value_weight_grad,
        out_weight_grad,
        up_weight_grad,
        down_weight_grad,
        attn_gain_grad,
        mlp_gain_grad,
    )


def local(
    mp,
    dp,
    tokens,
    segment_ids,
    query_weight,
    key_weight,
    value_weight,
    out_weight,
    up_weight,
    down_weight,
    attn_gain,
    mlp_gain,
    out_cotangent,
):
    width, columns = query_weight.shape
    length = segment_ids.shape[1]
    half = tokens.shape[0] // 2
    z = lax.axis_index(DP) // 2
    attn_gain, mlp_gain = attn_gain.reshape(1, width), mlp_gain.reshape(1, width)
    flip = lax.axis_index(MP) // 2
    segs = jnp.where(flip == 0, segment_ids, segment_ids[::-1])
    got = layer(
        dict(
            tokens=tokens,
            seg_col=segs.reshape(2, length, 1),
            seg_row=segs.reshape(2, 1, length),
            query_weight=query_weight,
            key_weight=key_weight,
            value_weight=value_weight,
            out_weight=out_weight,
            up_weight=up_weight,
            down_weight=down_weight,
            attn_gain=attn_gain,
            mlp_gain=mlp_gain,
            out_cotangent=out_cotangent,
        ),
        half,
        width,
        columns,
        up_weight.shape[1],
        length,
    )

    def own_terms(terms, more):
        return [(WHOLE, terms), (WHOLE, more.early), (WHOLE, more.late)]

    tokens_grad, attn_gain_grad = row_stage(
        lambda v, m, g, *t: (lambda b: (m + b[0], b[1]))(norm_back(v.astype(f32), g, total(t))),
        [(WHOLE, tokens), (WHOLE, got.middle), (VEC, attn_gain), *own_terms(got.out_terms, got.back)],
        [(WHOLE, f32), (VEC, f32)],
        name="norm_first_back",
    )
    gains = jnp.concatenate([attn_gain_grad, got.mlp_gain_grad], axis=0).reshape(8, width // 4)
    gains = everyone(gains, mp, dp).reshape(2, width)
    (layer_output,) = row_stage(
        lambda m, *t: (m + total(t),),
        [(WHOLE, got.residual_mid), *own_terms(got.mlp_terms, got.mlp)],
        [(WHOLE, bf16)],
        name="output",
    )
    qkv_grads = share_total(got.qkv_w_grad, z, False, [columns] * 3)
    out_grad = share_total(got.out_grad, z, True)[0]
    up_grad = share_total(got.up_grad, z, False)[0]
    down_grad = share_total(got.down_grad, z, True)[0]
    return (layer_output, tokens_grad, *qkv_grads, out_grad, up_grad, down_grad, gains[0], gains[1])


def solution(mesh):
    mp, dp = mesh.shape[MP], mesh.shape[DP]
    return jax.shard_map(
        functools.partial(local, mp, dp) if (mp, dp) == (4, 8) else local_plain,
        mesh=mesh,
        in_specs=(
            P(BOTH, None),
            P(DP, None),
            P(None, MP),
            P(None, MP),
            P(None, MP),
            P(MP, None),
            P(None, MP),
            P(MP, None),
            P(),
            P(),
            P(BOTH, None),
        ),
        out_specs=(
            P(BOTH, None),
            P(BOTH, None),
            P(DP, MP),
            P(DP, MP),
            P(DP, MP),
            P(MP, DP),
            P(DP, MP),
            P(MP, DP),
            P(),
            P(),
        ),
        check_vma=False,
    )
```

```python
import functools
import math
from types import SimpleNamespace as Names

import jax
import jax.numpy as jnp
from jax import lax
from jax.experimental import pallas as pl
from jax.experimental.pallas import tpu as pltpu
from jax.sharding import PartitionSpec as P

HEAD_DIM = 128
CLIP_MOST = 256
epsilon = 1e-05
masked_score = -1e30
bf16, f32 = jnp.bfloat16, jnp.float32
VMEM_LIMIT = 60 * 1024 * 1024
MESH = pl.DeviceIdType.MESH
WHOLE, VEC = range(2)
DP, MP = BOTH = ("dp", "mp")


def dot(a, b, ca, cb):
    return lax.dot_general(a, b, (((ca,), (cb,)), ((), ())), preferred_element_type=f32)


def shape(dims, kind=bf16):
    return jax.ShapeDtypeStruct(dims, kind)


def call(kernel, args, grid, in_specs, out_specs, outs, *, name, scalars=(), scratch=(), after=(), flops=0, moved=0, **extra):
    lead = len(scalars) + len(args)

    def body(*refs):
        kernel(*refs[:lead], *refs[lead + len(after) :])

    return pl.pallas_call(
        body,
        grid_spec=pltpu.PrefetchScalarGridSpec(
            num_scalar_prefetch=len(scalars),
            grid=grid,
            in_specs=[*in_specs, *[pl.BlockSpec(memory_space=pl.ANY)] * len(after)],
            out_specs=out_specs,
            scratch_shapes=list(scratch),
        ),
        out_shape=outs,
        compiler_params=pltpu.CompilerParams(vmem_limit_bytes=VMEM_LIMIT, **extra),
        cost_estimate=pl.CostEstimate(flops=flops, bytes_accessed=moved, transcendentals=0),
        name=name,
    )(*scalars, *args, *after)


def norm_parts(values):
    centred = values - jnp.mean(values, axis=-1, keepdims=True)
    spread = jnp.mean(centred * centred, axis=-1, keepdims=True)
    scale = lax.rsqrt(spread + epsilon)
    return centred * scale, scale


def norm_back(values, gain, grad):
    unit, scale = norm_parts(values)
    q = grad * gain
    back = scale * (
        q - jnp.mean(q, axis=-1, keepdims=True) - unit * jnp.mean(q * unit, axis=-1, keepdims=True)
    )
    return back, jnp.sum(grad * unit, axis=0, keepdims=True)


def total(values):
    out = values[0].astype(f32)
    for v in values[1:]:
        out = out + v.astype(f32)
    return out


def gelu_both(u):
    c = math.sqrt(2.0 / math.pi)
    square = u * u
    t = jnp.tanh(c * (u + 0.044715 * (u * square)))
    half = 0.5 * (1.0 + t)
    value = u * half
    slope = half + (0.5 * c) * u * (1.0 - t * t) * (1.0 + (3 * 0.044715) * square)
    return value, slope


def allowed_of(seg_col, seg_row, q0, k0, k1, rows):
    same = seg_col[q0 : q0 + rows, :] == seg_row[:, k0:k1]
    dims = (rows, k1 - k0)
    i = lax.broadcasted_iota(jnp.int32, dims, 0) + q0
    j = lax.broadcasted_iota(jnp.int32, dims, 1) + k0
    return same & (j <= i)


class Wire:
    def __init__(self, send, recv):
        self.send, self.recv, self.count, self.ends = send, recv, 0, []

    def slot(self):
        self.count += 1
        return self.count - 1

    def copy(self, slot, source, target, to):
        return pltpu.make_async_remote_copy(
            src_ref=source,
            dst_ref=target,
            send_sem=self.send.at[slot],
            recv_sem=self.recv.at[slot],
            device_id=to,
            device_id_type=MESH,
        )

    def go(self, source, target, to):
        copy = self.copy(self.slot(), source, target, to)
        copy.start()
        self.ends.append(copy)
        return copy

    def sent(self, *copies):
        for copy in copies:
            copy.wait_send()
            self.ends = [c for c in self.ends if c is not copy]

    def finish(self):
        self.sent(*list(self.ends))


def stage(body, grid, ins, outs):
    pltpu.emit_pipeline(
        body,
        grid=grid,
        in_specs=[pl.BlockSpec(b, f) for _, b, f in ins],
        out_specs=[pl.BlockSpec(b, f) for _, b, f in outs],
    )(*[r for r, _, _ in ins], *[r for r, _, _ in outs])


def layer_kernel(dims, tree, *refs):
    half, width, columns, units, length = dims
    full = 2 * half
    rows = 4 * full
    r = named(jax.tree.unflatten(tree, refs))
    m, d = lax.axis_index(MP), lax.axis_index(DP)
    core, z = lax.rem(d, 2), d // 2
    parity = lax.rem(m, 2)
    to_x = {MP: m + 1 - 2 * parity}
    to_y = {MP: m + 2 - 4 * (m // 2)}
    to_core = {DP: d + 1 - 2 * core}
    wire = Wire(r.send, r.recv)
    heads = columns // HEAD_DIM
    score_scale = 1.0 / math.sqrt(HEAD_DIM)

    barrier = pltpu.get_barrier_semaphore()
    others = [{MP: lax.rem(m + i, 4)} for i in range(1, 4)] + [{DP: lax.rem(d + i, 8)} for i in range(1, 8)]
    for peer in others:
        pl.semaphore_signal(barrier, inc=1, device_id=peer, device_id_type=MESH)
    pl.semaphore_wait(barrier, len(others))

    def at(ref, block):
        return ref.at[pl.ds(block * half, half)]

    qkv_w = r.qkv_w
    loads = [
        pltpu.make_async_copy(w, qkv_w.at[:, pl.ds(i * columns, columns)], r.load.at[i])
        for i, w in enumerate((r.query_weight, r.key_weight, r.value_weight))
    ]
    for load in loads:
        load.start()

    tile = half // 2

    def row_ins(*values):
        out = []
        for v in values:
            ref, f = v if isinstance(v, tuple) else (v, lambda i: (i, 0))
            out.append((ref, (1 if ref.shape[0] == 1 else tile, width), (lambda i: (0, 0)) if ref.shape[0] == 1 else f))
        return out

    def row_wise(fn, ins, outs):
        n = len(ins)

        def body(*refs):
            for ref, value in zip(refs[n:], fn(*[x[...] for x in refs[:n]])):
                ref[...] = value.astype(ref.dtype)

        stage(body, (4,), row_ins(*ins), row_ins(*outs))

    def spread(ref):
        return {
            2: wire.go(at(ref, 0), at(ref, 2), to_x),
            5: wire.go(at(ref, 1), at(ref, 5), to_y),
            3: wire.go(at(ref, 1), at(ref, 3), to_x),
            4: wire.go(at(ref, 0), at(ref, 4), to_y),
        }

    def relay(ref):
        return {6: wire.go(at(ref, 2), at(ref, 6), to_y), 7: wire.go(at(ref, 5), at(ref, 7), to_x)}

    def send_far(into, terms):
        return [wire.go(at(terms, 6), at(into.far, 0), to_x), wire.go(at(terms, 7), at(into.far, 1), to_y)]

    def send_early(into, terms):
        return [wire.go(at(terms, 2), at(into.early, 0), to_x), wire.go(at(terms, 5), at(into.early, 1), to_y)]

    def send_late(into, terms, far, sums):
        for copy in far:
            copy.wait_recv()
        row_wise(
            lambda a, b: (a.astype(f32) + b.astype(f32),),
            [(terms, lambda i: (jnp.where(i < 2, 8 + i, 4 + i), 0)), into.far],
            [sums],
        )
        return [wire.go(at(sums, 0), at(into.late, 0), to_y), wire.go(at(sums, 1), at(into.late, 1), to_x)]

    def arrive(*copies):
        for copy in copies:
            copy.wait_recv()

    def product(source, target, blocks, weight, size, count, trans=False, scale=None):
        n = len(blocks)
        depth = source.shape[1]
        ref, ref_block, ref_map = weight if isinstance(weight, tuple) else (None, None, None)

        def body(*refs):
            j = pl.program_id(0)
            x = jnp.concatenate([b[...] for b in refs[:n]], axis=0) if n > 1 else refs[0][...]
            w = refs[n][...] if ref is not None else weight(j)
            acc = dot(x, w, 1, 1 if trans else 0)
            if scale is not None:
                acc = acc * scale(j)
            for i, out in enumerate(refs[-n:]):
                out[...] = acc[i * half : (i + 1) * half].astype(bf16)

        stage(
            body,
            (count,),
            [(source, (half, depth), lambda j, b=b: (b, 0)) for b in blocks]
            + ([(ref, ref_block, ref_map)] if ref is not None else []),
            [(target, (half, size), lambda j, b=b: (b, j)) for b in blocks],
        )

    def project(*blocks):
        product(
            r.attn_in,
            r.qkv,
            blocks,
            lambda j: qkv_w[:, pl.ds(pl.multiple_of(j * columns, columns), columns)],
            columns,
            3,
            scale=lambda j: jnp.where(j == 0, score_scale, 1.0),
        )

    def out_project(*blocks):
        product(
            r.context,
            r.out_terms,
            blocks,
            (r.out_weight, (columns, width // 2), lambda j: (0, j)),
            width // 2,
            2,
        )

    def context_back(*blocks):
        product(
            r.middle_all,
            r.context_grad,
            blocks,
            (r.out_weight, (columns // 2, width), lambda j: (j, 0)),
            columns // 2,
            2,
            trans=True,
        )

    def project_back(*blocks):
        size = width // 4
        product(
            r.qkv_grad,
            r.out_terms,
            blocks,
            lambda j: qkv_w[pl.ds(pl.multiple_of(j * size, size), size), :],
            size,
            4,
            trans=True,
        )

    def turn(block, target):
        for b in range(2):
            to = pl.multiple_of(lax.rem(parity + b, 2) * full, full)
            target[pl.ds(to, full), :] = block[b * full : (b + 1) * full, :]

    def turn_back(source, block):
        for b in range(2):
            come = pl.multiple_of(lax.rem(parity + b, 2) * full, full)
            block[b * full : (b + 1) * full, :] = source[pl.ds(come, full), :].astype(bf16)

    q, k, v, c = r.q, r.k, r.v, r.c
    f0, f1, f2 = r.f0, r.f1, r.f2

    def head_ins(s):
        ins = [
            (r.seg_col, (1, length, 1), lambda h: (lax.rem(m // 2 + s, 2), 0, 0)),
            (r.seg_row, (1, 1, length), lambda h: (lax.rem(m // 2 + s, 2), 0, 0)),
        ]
        for which in range(3):
            ins.append((r.qkv, (length, HEAD_DIM), lambda h, w=which: (s, w * heads + h)))
        return ins

    def scores_of(seg_col, seg_row, q0, k0, k1):
        s = dot(q[q0:k1, :], k[k0:k1, :], 1, 1)
        keep = allowed_of(seg_col.at[0], seg_row.at[0], q0, k0, k1, CLIP_MOST)
        s = jnp.where(keep, s, masked_score)
        e = jnp.exp(s - jnp.max(s, axis=-1, keepdims=True))
        return e * (1.0 / jnp.sum(e, axis=-1, keepdims=True))

    def attend(s):
        def body(seg_col, seg_row, q_in, k_in, v_in, out):
            turn(q_in, q)
            turn(k_in, k)
            turn(v_in, v)
            for q0 in range(0, length, CLIP_MOST):
                k0, k1 = max(0, q0 - CLIP_MOST), q0 + CLIP_MOST
                p = scores_of(seg_col, seg_row, q0, k0, k1).astype(bf16)
                f0[q0:k1, :] = dot(p, v[k0:k1, :], 1, 0)
            turn_back(f0, out)

        stage(body, (heads,), head_ins(s), [(r.context, (length, HEAD_DIM), lambda h: (s, h))])

    def attend_back(s):
        def body(seg_col, seg_row, q_in, k_in, v_in, c_in, dq_out, dk_out, dv_out):
            turn(q_in, q)
            turn(k_in, k)
            turn(v_in, v)
            turn(c_in, c)
            for q0 in range(0, length, CLIP_MOST):
                k0, k1 = max(0, q0 - CLIP_MOST), q0 + CLIP_MOST
                p = scores_of(seg_col, seg_row, q0, k0, k1)
                qb, cb, kb, vb = q[q0:k1, :], c[q0:k1, :], k[k0:k1, :], v[k0:k1, :]
                dp = dot(cb, vb, 1, 1)
                inner = jnp.sum(p * dp, axis=-1, keepdims=True)
                ds = (p * (dp - inner)).astype(bf16)
                f0[q0:k1, :] = dot(ds, kb, 1, 0) * score_scale
                dk, dv = dot(ds, qb, 0, 0), dot(p.astype(bf16), cb, 0, 0)
                if q0 > 0:
                    f1[k0:q0, :] += dk[:CLIP_MOST]
                    f2[k0:q0, :] += dv[:CLIP_MOST]
                    dk, dv = dk[CLIP_MOST:], dv[CLIP_MOST:]
                f1[q0:k1, :] = dk
                f2[q0:k1, :] = dv
            turn_back(f0, dq_out)
            turn_back(f1, dk_out)
            turn_back(f2, dv_out)

        stage(
            body,
            (heads,),
            [*head_ins(s), (r.context_grad, (length, HEAD_DIM), lambda h: (s, h))],
            [(r.qkv_grad, (length, HEAD_DIM), lambda h, w=w: (s, w * heads + h)) for w in range(3)],
        )

    acc_g, slopes = r.acc_g, r.slopes
    size = 512
    tiles = units // size
    up_tile = (r.up_weight, (width, size), lambda j: (0, j))
    down_tile = (r.down_weight, (size, width), lambda j: (j, 0))

    def whole(ref, both):
        return [(ref, (half, width), lambda j, i=i: (i, 0)) for i in both]

    def part(ref, both):
        return [(ref, (half, size), lambda j, i=i: (i, j)) for i in both]

    def rows_of(a, b):
        return jnp.concatenate([a[...], b[...]], axis=0)

    def grads_of(grad, up, p0, p1, g0, g1):
        j = pl.program_id(0)
        grad = grad.astype(bf16)
        p0[...], p1[...] = grad[:half], grad[half:]
        g = dot(grad, up[...], 1, 1)

        @pl.when(j == 0)
        def _():
            acc_g[...] = g

        @pl.when((j > 0) & (j < tiles - 1))
        def _():
            acc_g[...] += g

        @pl.when(j == tiles - 1)
        def _():
            last = acc_g[...] + g
            g0[...], g1[...] = last[:half].astype(bf16), last[half:].astype(bf16)

    def feed(*both):
        def body(x0, x1, c0, c1, up, down, h0, h1, *outs):
            value, slope = gelu_both(dot(rows_of(x0, x1), up[...], 1, 0))
            value = value.astype(bf16)
            h0[...], h1[...] = value[:half], value[half:]
            grads_of(dot(rows_of(c0, c1), down[...], 1, 1) * slope, up, *outs)

        stage(
            body,
            (tiles,),
            [*whole(r.mlp_in, both), *whole(r.cot_all, both), up_tile, down_tile],
            [*part(r.hidden, both), *part(r.pre_grad, both), *whole(r.mid_terms, both)],
        )

    def feed_forward(*both):
        def body(x0, x1, up, h0, h1):
            value, slope = gelu_both(dot(rows_of(x0, x1), up[...], 1, 0))
            value = value.astype(bf16)
            h0[...], h1[...] = value[:half], value[half:]
            slopes[pl.program_id(0)] = slope

        stage(body, (tiles,), [*whole(r.mlp_in, both), up_tile], part(r.hidden, both))

    def feed_back(*both):
        def body(c0, c1, up, down, *outs):
            grads_of(dot(rows_of(c0, c1), down[...], 1, 1) * slopes[pl.program_id(0)], up, *outs)

        stage(
            body,
            (tiles,),
            [*whole(r.cot_all, both), up_tile, down_tile],
            [*part(r.pre_grad, both), *whole(r.mid_terms, both)],
        )

    down_acc = r.down_acc
    share = width // 8

    def down_some(first, count, both, target=None, plus=None):
        begin = 0 in both
        n = len(both)

        def body(*refs):
            s = pl.program_id(0)
            left, right = ([b[...] for b in refs[i * n : (i + 1) * n]] for i in range(2))
            acc = dot(jnp.concatenate(left, axis=0), jnp.concatenate(right, axis=0), 0, 0)
            if not begin:
                acc = acc + down_acc[first + s]
            if target is None:
                down_acc[first + s] = acc
                return
            if plus is not None:
                acc = acc + refs[2 * n][0].astype(f32)
            refs[-1][0] = acc.astype(bf16)

        def column(s):
            k = first + s
            return 2 * lax.rem(k, 4) + jnp.where(k < 4, 1 - core, core)

        block = (1, share, units)
        stage(
            body,
            (count,),
            [(r.cot_all, (half, share), lambda s, i=i: (i, column(s))) for i in both]
            + [(r.hidden, (half, units), lambda s, i=i: (i, 0)) for i in both]
            + ([(plus, block, lambda s: (s, 0, 0))] if plus is not None else []),
            [(target, block, lambda s: (s, 0, 0))] if target is not None else [],
        )

    def grad_product(left, right, which, target, plus=None):
        def body(a, b, *rest):
            acc = dot(a[...], b[...], 0, 0)
            if plus is not None:
                acc = acc + rest[0][0].astype(f32)
            rest[-1][0] = acc.astype(bf16)

        n = right.shape[1]
        block = (1, share, n)
        place = lambda s: (s, 0, 0)
        stage(
            body,
            (4,),
            [
                (left, (rows, share), lambda s: (0, 2 * s + which)),
                (right, (rows, n), lambda s: (0, 0)),
                *([(plus, block, place)] if plus is not None else []),
            ],
            [(target, block, place)],
        )

    def grad_first(into, left, right):
        grad_product(left, right, 1 - core, into.mine)
        return wire.go(into.mine, into.got, to_core)

    def line(mine, got, sums, step, place):
        pick = lambda at: jnp.clip(at if step > 0 else 3 - at, 0, 3)
        slots = [wire.slot() for _ in range(3)]
        to = {DP: jnp.clip(d + 2 * step, 0, 7)}

        def copy(t, source):
            return wire.copy(slots[t], source, got.at[t], to)

        @pl.when(place == 0)
        def _():
            for t in range(3):
                copy(t, mine.at[pick(3 - t)]).start()

        def forward(t):
            @pl.when((place >= 1) & (place <= t + 1))
            def _():
                copy(t, mine.at[0]).wait_recv()
                n = mine.shape[2]
                size = mine.shape[1] // 2

                def body(a, b, out):
                    out[...] = (a[0].astype(f32) + b[...].astype(f32)).astype(bf16)

                stage(
                    body,
                    (2,),
                    [
                        (mine, (1, size, n), lambda i: (pick(place + 2 - t), i, 0)),
                        (got.at[t], (size, n), lambda i: (i, 0)),
                    ],
                    [(sums.at[t], (size, n), lambda i: (i, 0))],
                )
                copy(t + 1, sums.at[t]).start()

        def end():
            @pl.when(place >= 1)
            def _():
                copy(2, mine.at[0]).wait_recv()

            for t in range(3):

                @pl.when((place <= t) & (place < 3))
                def _():
                    copy(t, mine.at[0]).wait_send()

        return forward, end

    def grad_second(into, left, right, swap):
        swap.wait_recv()
        wire.sent(swap)
        grad_product(left, right, core, into.mine, into.got)
        return start_line(into)

    def start_line(into):
        up = line(into.mine, into.right, into.right_sums, 1, z)
        down = line(into.mine, into.left, into.left_sums, -1, 3 - z)

        def forward(t):
            up[0](t)
            down[0](t)

        def end(turned=None):
            up[1]()
            down[1]()
            if turned is not None:
                share_total(into, turned)

        return forward, end

    def share_total(into, target):
        turned = target.shape[1] == share
        n = into.mine.shape[2]
        tile = 128

        def body(own, right, left, out):
            value = own[0].astype(f32)
            value = value + jnp.where(z > 0, right[0].astype(f32), 0.0)
            value = value + jnp.where(z < 3, left[0].astype(f32), 0.0)
            out[...] = value.T if turned else value

        block = (1, tile, n)
        stage(
            body,
            (share // tile,),
            [(into.mine, block, lambda i: (z, i, 0)), (into.right, block, lambda i: (2, i, 0)), (into.left, block, lambda i: (2, i, 0))],
            [(target, (n, tile), lambda i: (0, i)) if turned else (target, (tile, n), lambda i: (i, 0))],
        )

    def over_all(slots, value, me, axis, count):
        copies = [wire.go(value, slots.at[me], {axis: lax.rem(me + i, count)}) for i in range(1, count)]
        slots[pl.ds(me, 1)] = value[...][None]
        arrive(*copies)
        return functools.reduce(lambda a, i: a + slots[i], range(1, count), slots[0])

    attn_in, cot_all, mlp_in, middle_all = r.attn_in, r.cot_all, r.mlp_in, r.middle_all
    row_wise(
        lambda x, g: (norm_parts(x.astype(f32))[0] * g,), [r.tokens, r.attn_gain], [attn_in]
    )
    near = spread(attn_in)
    row_wise(lambda x: (x,), [r.out_cotangent], [cot_all])
    for load in loads:
        load.wait()
    project(0, 1)
    arrive(near[2], near[5])
    far = relay(attn_in)
    arrive(near[3], near[4])
    cot_near = {2: wire.go(at(cot_all, 0), at(cot_all, 2), to_x), 5: wire.go(at(cot_all, 1), at(cot_all, 5), to_y)}
    project(2, 3, 4, 5)
    attend(0)
    arrive(far[6], far[7])
    project(6, 7)
    attend(1)
    out_terms = r.out_terms
    out_project(6, 7)
    attn_far = send_far(r.attn, out_terms)
    out_project(2, 3, 4, 5)
    attn_early = send_early(r.attn, out_terms)
    out_project(0, 1)
    attn_late = send_late(r.attn, out_terms, attn_far, r.sums_a)
    cot_near[3] = wire.go(at(cot_all, 1), at(cot_all, 3), to_x)
    cot_near[4] = wire.go(at(cot_all, 0), at(cot_all, 4), to_y)
    arrive(*attn_early, *attn_late)

    def second(x, g, a, b, c_):
        mid = x.astype(f32) + a.astype(f32) + b.astype(f32) + c_.astype(f32)
        return mid, norm_parts(mid)[0] * g

    row_wise(
        second,
        [r.tokens, r.mlp_gain, out_terms, r.attn.early, r.attn.late],
        [r.residual_mid, mlp_in],
    )
    near = spread(mlp_in)
    arrive(cot_near[2], cot_near[5])
    feed(0, 1)
    arrive(near[2], near[5])
    far = relay(mlp_in)
    cot_far = relay(cot_all)
    feed(2, 5)
    mid_terms = r.mid_terms
    mid_early = send_early(r.mid, mid_terms)
    down_some(0, 8, (0, 1, 2, 5))
    arrive(near[3], near[4], cot_near[3], cot_near[4])
    feed(3, 4)
    arrive(far[6], far[7])
    feed_forward(6, 7)
    arrive(cot_far[6], cot_far[7])
    down, last = r.down_grad, (3, 4, 6, 7)
    down_some(0, 4, last, down.mine)
    swap = wire.go(down.mine, down.got, to_core)
    arrive(swap)
    wire.sent(swap)
    down_some(4, 4, last, down.mine, down.got)
    down_forward, down_end = start_line(down)
    feed_back(6, 7)
    mid_far = send_far(r.mid, mid_terms)
    swap = grad_first(r.up_grad, mlp_in, r.pre_grad)
    mid_late = send_late(r.mid, mid_terms, mid_far, r.sums_b)
    up_forward, up_end = grad_second(r.up_grad, mlp_in, r.pre_grad, swap)
    down_forward(0)
    arrive(*mid_early, *mid_late)
    gain_sum = r.gain_sum
    gain_sum[...] = jnp.zeros_like(gain_sum)

    def second_back(mid, g, cot, a, b, c_):
        back, gain = norm_back(mid, g, a.astype(f32) + b.astype(f32) + c_.astype(f32))
        gain_sum[1:2, :] += gain
        value = cot.astype(f32) + back
        return value, value

    row_wise(
        second_back,
        [r.residual_mid, r.mlp_gain, r.out_cotangent, mid_terms, r.mid.early, r.mid.late],
        [r.middle, middle_all],
    )
    near = spread(middle_all)

    mlp_terms = r.mlp_terms

    def down_project(*blocks):
        product(r.hidden, mlp_terms, blocks, (r.down_weight, (units, size), lambda j: (0, j)), size, width // size)

    context_back(0, 1)
    down_project(6, 7, 2, 3)
    arrive(near[2], near[5])
    far = relay(middle_all)
    down_project(4, 5, 0, 1)
    mlp_far = send_far(r.attn, mlp_terms)
    arrive(near[3], near[4])
    context_back(2, 3, 4, 5)
    down_forward(1)
    attend_back(0)
    up_forward(0)
    arrive(far[6], far[7])
    context_back(6, 7)
    swap = grad_first(r.out_grad, middle_all, r.context)
    attend_back(1)
    wire.sent(*attn_far, *attn_early)
    project_back(6, 7)
    back_far = send_far(r.mid, out_terms)
    out_forward, out_end = grad_second(r.out_grad, middle_all, r.context, swap)
    swap = grad_first(r.qkv_w_grad, attn_in, r.qkv_grad)
    project_back(2, 3, 4, 5)
    back_early = send_early(r.mid, out_terms)
    up_forward(1)
    qkv_forward, qkv_end = grad_second(r.qkv_w_grad, attn_in, r.qkv_grad, swap)
    wire.sent(*mid_late)
    back_late = send_late(r.mid, out_terms, back_far, r.sums_b)
    mlp_early = send_early(r.attn, mlp_terms)
    wire.sent(*attn_late)
    mlp_late = send_late(r.attn, mlp_terms, mlp_far, r.sums_a)
    project_back(0, 1)
    out_forward(0)
    down_end(r.down_total)
    arrive(*back_early, *back_late)

    def first_back(x, mid, g, a, b, c_):
        back, gain = norm_back(x.astype(f32), g, a.astype(f32) + b.astype(f32) + c_.astype(f32))
        gain_sum[0:1, :] += gain
        return (mid + back,)

    row_wise(
        first_back,
        [r.tokens, r.middle, r.attn_gain, out_terms, r.mid.early, r.mid.late],
        [r.tokens_grad],
    )
    qkv_forward(0)
    out_forward(1)
    up_end(r.up_total)
    r.gain_near_sum[...] = over_all(r.gain_near, gain_sum, m, MP, 4)
    r.gains[...] = over_all(r.gain_far, r.gain_near_sum, d, DP, 8)
    qkv_forward(1)
    out_end(r.out_total)
    arrive(*mlp_early, *mlp_late)
    row_wise(
        lambda mid, *t: (mid + total(t),),
        [r.residual_mid, mlp_terms, r.attn.early, r.attn.late],
        [r.layer_output],
    )
    qkv_end()
    wire.finish()


def named(tree):
    return Names(**{k: named(v) for k, v in tree.items()}) if isinstance(tree, dict) else tree


def layer(ins, half, width, columns, units, length):
    full, rows = 2 * half, 8 * half
    share = width // 8
    big, own = shape((rows, width)), shape((full, width))
    arrivals = dict(far=own, early=own, late=own)

    def grad(n):
        line, sums = shape((3, share, n)), shape((2, share, n))
        stack = shape((4, share, n))
        return dict(mine=stack, got=stack, right=line, left=line, right_sums=sums, left_sums=sums)

    outs = dict(
        attn_in=big,
        cot_all=big,
        mlp_in=big,
        middle_all=big,
        out_terms=big,
        mlp_terms=big,
        mid_terms=big,
        hidden=shape((rows, units)),
        pre_grad=shape((rows, units)),
        qkv=shape((rows, 3 * columns)),
        qkv_grad=shape((rows, 3 * columns)),
        context=shape((rows, columns)),
        context_grad=shape((rows, columns)),
        attn=arrivals,
        mid=arrivals,
        sums_a=own,
        sums_b=own,
        down_grad=grad(units),
        up_grad=grad(units),
        qkv_w_grad=grad(3 * columns),
        out_grad=grad(columns),
        residual_mid=shape((full, width), f32),
        middle=shape((full, width), f32),
        layer_output=own,
        tokens_grad=shape((full, width), f32),
        down_total=shape((units, share), f32),
        up_total=shape((share, units), f32),
        out_total=shape((columns, share), f32),
    )
    any_, vmem = pl.BlockSpec(memory_space=pl.ANY), pl.BlockSpec(memory_space=pltpu.VMEM)
    places = dict(jax.tree.map(lambda _: any_, outs), gains=vmem)
    outs = dict(outs, gains=shape((2, width), f32))
    head, head_sum = pltpu.VMEM((length, HEAD_DIM), bf16), pltpu.VMEM((length, HEAD_DIM), f32)
    acc = pltpu.VMEM((full, width), f32)
    scratch = dict(
        qkv_w=pltpu.VMEM((width, 3 * columns), bf16),
        acc_g=acc,
        slopes=pltpu.VMEM((units // 512, full, 512), f32),
        down_acc=pltpu.VMEM((8, share, units), f32),
        gain_sum=pltpu.VMEM((2, width), f32),
        gain_near_sum=pltpu.VMEM((2, width), f32),
        gain_near=pltpu.VMEM((4, 2, width), f32),
        gain_far=pltpu.VMEM((8, 2, width), f32),
        q=head,
        k=head,
        v=head,
        c=head,
        f0=head_sum,
        f1=head_sum,
        f2=head_sum,
        send=pltpu.SemaphoreType.DMA((96,)),
        recv=pltpu.SemaphoreType.DMA((96,)),
        load=pltpu.SemaphoreType.DMA((3,)),
    )
    parts = [jax.tree.flatten(t) for t in (ins, outs, scratch)]
    kinds = [jax.tree.unflatten(t, range(len(v))) for v, t in parts]
    starts = (0, len(parts[0][0]), len(parts[0][0]) + len(parts[1][0]))
    place_of = {}
    for kind, begin in zip(kinds, starts):
        place_of.update(jax.tree.map(lambda i, b=begin: b + i, kind))
    order, tree = jax.tree.flatten(place_of)

    def kernel(*refs):
        layer_kernel((half, width, columns, units, length), tree, *[refs[i] for i in order])

    got = pl.pallas_call(
        kernel,
        in_specs=[any_] * len(parts[0][0]),
        out_specs=jax.tree.leaves(places),
        out_shape=parts[1][0],
        scratch_shapes=parts[2][0],
        compiler_params=pltpu.CompilerParams(
            collective_id=1, has_side_effects=True, vmem_limit_bytes=VMEM_LIMIT
        ),
        name="layer",
    )(*parts[0][0])
    return named(jax.tree.unflatten(parts[1][1], got))


def share_total(got, z, columns):
    mine, right, left = got.mine, got.right, got.left
    _, rows, width = mine.shape
    tile = 128

    def kernel(place, own, a, b, *outs):
        value = own[0].astype(f32)
        value = value + jnp.where(place[0] > 0, a[0].astype(f32), 0.0)
        value = value + jnp.where(place[0] < 3, b[0].astype(f32), 0.0)
        at = 0
        for out in outs:
            out[...] = value[:, at : at + out.shape[1]]
            at += out.shape[1]

    return call(
        kernel,
        [mine, right, left],
        (rows // tile,),
        [pl.BlockSpec((1, tile, width), lambda i, p: (p[0], i, 0))]
        + [pl.BlockSpec((1, tile, width), lambda i, p: (2, i, 0))] * 2,
        [pl.BlockSpec((tile, c), lambda i, p: (i, 0)) for c in columns],
        [shape((rows, c), f32) for c in columns],
        scalars=[z.astype(jnp.int32).reshape(1)],
        name="share_total",
        flops=rows * width,
        moved=rows * width * 10,
    )


def norm_rows(values, gain):
    centre = jnp.mean(values, axis=-1, keepdims=True)
    centred = values - centre
    spread = jnp.mean(centred * centred, axis=-1, keepdims=True)
    return centred * lax.rsqrt(spread + epsilon) * gain


def gelu_tanh(values):
    return jax.nn.gelu(values, approximate=True)


def block_allowed(segment):
    position = jnp.arange(segment.shape[0])
    return (position[None, :] <= position[:, None]) & (segment[:, None] == segment[None, :])


def rows_times(left_rows, right_matrix):
    return jnp.dot(left_rows, right_matrix, preferred_element_type=jnp.float32)


def rows_times_back(left_rows, right_matrix):
    return lax.dot_general(
        left_rows, right_matrix, (((1,), (1,)), ((), ())), preferred_element_type=jnp.float32
    )


def attn_input_back(
    queries_grad, keys_grad, values_grad, query_weight, key_weight, value_weight, score_scale
):
    total_grad = rows_times_back(queries_grad, query_weight) * score_scale
    total_grad = total_grad + rows_times_back(keys_grad, key_weight)
    return total_grad + rows_times_back(values_grad, value_weight)


def attend_forward(packed):
    queries, keys_in, values_in, segment = packed
    scores = jnp.einsum("qhd,khd->hqk", queries, keys_in, preferred_element_type=jnp.float32)
    scores = jnp.where(block_allowed(segment)[None], scores, masked_score)
    row_max = jnp.max(scores, axis=-1, keepdims=True)
    expanded = jnp.exp(scores - row_max)
    row_total = jnp.sum(expanded, axis=-1, keepdims=True)
    probs_low = (expanded / row_total).astype(jnp.bfloat16)
    context = jnp.einsum("hqk,khd->qhd", probs_low, values_in, preferred_element_type=jnp.float32)
    return (context.astype(jnp.bfloat16), (row_max + jnp.log(row_total))[:, :, 0])


def attend_backward(packed):
    queries, keys_in, values_in, segment, context_grad, log_total = packed
    scores = jnp.einsum("qhd,khd->hqk", queries, keys_in, preferred_element_type=jnp.float32)
    scores = jnp.where(block_allowed(segment)[None], scores, masked_score)
    attn_probs = jnp.exp(scores - log_total[:, :, None])
    probs_grad = jnp.einsum(
        "qhd,khd->hqk", context_grad, values_in, preferred_element_type=jnp.float32
    )
    values_grad = jnp.einsum(
        "hqk,qhd->khd",
        attn_probs.astype(jnp.bfloat16),
        context_grad,
        preferred_element_type=jnp.float32,
    )
    inner_sum = jnp.sum(attn_probs * probs_grad, axis=-1, keepdims=True)
    scores_grad = (attn_probs * (probs_grad - inner_sum)).astype(jnp.bfloat16)
    queries_grad = jnp.einsum(
        "hqk,khd->qhd", scores_grad, keys_in, preferred_element_type=jnp.float32
    )
    keys_grad = jnp.einsum("hqk,qhd->khd", scores_grad, queries, preferred_element_type=jnp.float32)
    return (
        queries_grad.astype(jnp.bfloat16),
        keys_grad.astype(jnp.bfloat16),
        values_grad.astype(jnp.bfloat16),
    )


def local_plain(
    tokens,
    segment_ids,
    query_weight,
    key_weight,
    value_weight,
    out_weight,
    up_weight,
    down_weight,
    attn_gain,
    mlp_gain,
    out_cotangent,
):
    seq_count, seq_length = segment_ids.shape
    group_rows = seq_count * seq_length
    head_count = query_weight.shape[1] // HEAD_DIM
    score_scale = 1.0 / math.sqrt(HEAD_DIM)
    shaped = (seq_count, seq_length, head_count, HEAD_DIM)
    flat_shape = (group_rows, head_count * HEAD_DIM)
    residual_in = tokens.astype(jnp.float32)
    normed_attn, attn_norm_back = jax.vjp(norm_rows, residual_in, attn_gain)
    gathered_attn = lax.all_gather(normed_attn.astype(jnp.bfloat16), MP, axis=0, tiled=True)
    queries = (
        jnp.dot(gathered_attn, query_weight, preferred_element_type=jnp.float32) * score_scale
    ).astype(jnp.bfloat16)
    keys_all = jnp.dot(gathered_attn, key_weight, preferred_element_type=jnp.float32).astype(
        jnp.bfloat16
    )
    values_all = jnp.dot(gathered_attn, value_weight, preferred_element_type=jnp.float32).astype(
        jnp.bfloat16
    )
    queries_seq = queries.reshape(shaped)
    keys_seq = keys_all.reshape(shaped)
    values_seq = values_all.reshape(shaped)
    context, log_total = lax.map(attend_forward, (queries_seq, keys_seq, values_seq, segment_ids))
    context_flat = context.reshape(flat_shape)
    attn_rows = lax.psum_scatter(
        rows_times(context_flat, out_weight).astype(jnp.bfloat16),
        MP,
        scatter_dimension=0,
        tiled=True,
    ).astype(jnp.float32)
    residual_mid = residual_in + attn_rows
    normed_mlp, mlp_norm_back = jax.vjp(norm_rows, residual_mid, mlp_gain)
    gathered_mlp = lax.all_gather(normed_mlp.astype(jnp.bfloat16), MP, axis=0, tiled=True)
    pre_act = jnp.dot(gathered_mlp, up_weight, preferred_element_type=jnp.float32)
    activated, gelu_back = jax.vjp(gelu_tanh, pre_act)
    hidden = activated.astype(jnp.bfloat16)
    mlp_rows = lax.psum_scatter(
        rows_times(hidden, down_weight).astype(jnp.bfloat16), MP, scatter_dimension=0, tiled=True
    ).astype(jnp.float32)
    layer_output = (residual_mid + mlp_rows).astype(jnp.bfloat16)
    cotangent_all = lax.all_gather(out_cotangent, MP, axis=0, tiled=True)
    down_weight_grad = jnp.einsum(
        "rf,rd->fd", hidden, cotangent_all, preferred_element_type=jnp.float32
    )
    hidden_grad = lax.dot_general(
        cotangent_all, down_weight, (((1,), (1,)), ((), ())), preferred_element_type=jnp.float32
    )
    pre_grad = gelu_back(hidden_grad)[0].astype(jnp.bfloat16)
    up_weight_grad = jnp.einsum(
        "rd,rf->df", gathered_mlp, pre_grad, preferred_element_type=jnp.float32
    )
    normed_mlp_grad = lax.psum_scatter(
        rows_times_back(pre_grad, up_weight).astype(jnp.bfloat16),
        MP,
        scatter_dimension=0,
        tiled=True,
    ).astype(jnp.float32)
    middle_back, mlp_gain_grad = mlp_norm_back(normed_mlp_grad)
    middle_grad = out_cotangent.astype(jnp.float32) + middle_back
    middle_all_grad = lax.all_gather(middle_grad.astype(jnp.bfloat16), MP, axis=0, tiled=True)
    out_weight_grad = jnp.einsum(
        "rc,rd->cd", context_flat, middle_all_grad, preferred_element_type=jnp.float32
    )
    context_grad = lax.dot_general(
        middle_all_grad, out_weight, (((1,), (1,)), ((), ())), preferred_element_type=jnp.float32
    ).astype(jnp.bfloat16)
    queries_grad, keys_grad, values_grad = lax.map(
        attend_backward,
        (queries_seq, keys_seq, values_seq, segment_ids, context_grad.reshape(shaped), log_total),
    )
    queries_grad = queries_grad.reshape(flat_shape)
    keys_grad = keys_grad.reshape(flat_shape)
    values_grad = values_grad.reshape(flat_shape)
    query_weight_grad = (
        jnp.einsum("rd,rc->dc", gathered_attn, queries_grad, preferred_element_type=jnp.float32)
        * score_scale
    )
    key_weight_grad = jnp.einsum(
        "rd,rc->dc", gathered_attn, keys_grad, preferred_element_type=jnp.float32
    )
    value_weight_grad = jnp.einsum(
        "rd,rc->dc", gathered_attn, values_grad, preferred_element_type=jnp.float32
    )
    normed_attn_grad = lax.psum_scatter(
        attn_input_back(
            queries_grad,
            keys_grad,
            values_grad,
            query_weight,
            key_weight,
            value_weight,
            score_scale,
        ).astype(jnp.bfloat16),
        MP,
        scatter_dimension=0,
        tiled=True,
    ).astype(jnp.float32)
    token_back, attn_gain_grad = attn_norm_back(normed_attn_grad)
    tokens_grad = middle_grad + token_back
    attn_gain_grad, mlp_gain_grad = lax.psum((attn_gain_grad, mlp_gain_grad), (DP, MP))
    (
        query_weight_grad,
        key_weight_grad,
        value_weight_grad,
        out_weight_grad,
        up_weight_grad,
        down_weight_grad,
    ) = (
        lax.psum_scatter(
            query_weight_grad.astype(jnp.bfloat16), DP, scatter_dimension=0, tiled=True
        ).astype(jnp.float32),
        lax.psum_scatter(
            key_weight_grad.astype(jnp.bfloat16), DP, scatter_dimension=0, tiled=True
        ).astype(jnp.float32),
        lax.psum_scatter(
            value_weight_grad.astype(jnp.bfloat16), DP, scatter_dimension=0, tiled=True
        ).astype(jnp.float32),
        lax.psum_scatter(
            out_weight_grad.astype(jnp.bfloat16), DP, scatter_dimension=1, tiled=True
        ).astype(jnp.float32),
        lax.psum_scatter(
            up_weight_grad.astype(jnp.bfloat16), DP, scatter_dimension=0, tiled=True
        ).astype(jnp.float32),
        lax.psum_scatter(
            down_weight_grad.astype(jnp.bfloat16), DP, scatter_dimension=1, tiled=True
        ).astype(jnp.float32),
    )
    return (
        layer_output,
        tokens_grad,
        query_weight_grad,
        key_weight_grad,
        value_weight_grad,
        out_weight_grad,
        up_weight_grad,
        down_weight_grad,
        attn_gain_grad,
        mlp_gain_grad,
    )


def local(
    mp,
    dp,
    tokens,
    segment_ids,
    query_weight,
    key_weight,
    value_weight,
    out_weight,
    up_weight,
    down_weight,
    attn_gain,
    mlp_gain,
    out_cotangent,
):
    width, columns = query_weight.shape
    length = segment_ids.shape[1]
    half = tokens.shape[0] // 2
    z = lax.axis_index(DP) // 2
    attn_gain, mlp_gain = attn_gain.reshape(1, width), mlp_gain.reshape(1, width)
    got = layer(
        dict(
            tokens=tokens,
            seg_col=segment_ids.reshape(2, length, 1),
            seg_row=segment_ids.reshape(2, 1, length),
            query_weight=query_weight,
            key_weight=key_weight,
            value_weight=value_weight,
            out_weight=out_weight,
            up_weight=up_weight,
            down_weight=down_weight,
            attn_gain=attn_gain,
            mlp_gain=mlp_gain,
            out_cotangent=out_cotangent,
        ),
        half,
        width,
        columns,
        up_weight.shape[1],
        length,
    )

    qkv_grads = share_total(got.qkv_w_grad, z, [columns] * 3)
    return (
        got.layer_output,
        got.tokens_grad,
        *qkv_grads,
        got.out_total,
        got.up_total,
        got.down_total,
        got.gains[0],
        got.gains[1],
    )


def solution(mesh):
    mp, dp = mesh.shape[MP], mesh.shape[DP]
    return jax.shard_map(
        functools.partial(local, mp, dp) if (mp, dp) == (4, 8) else local_plain,
        mesh=mesh,
        in_specs=(
            P(BOTH, None),
            P(DP, None),
            P(None, MP),
            P(None, MP),
            P(None, MP),
            P(MP, None),
            P(None, MP),
            P(MP, None),
            P(),
            P(),
            P(BOTH, None),
        ),
        out_specs=(
            P(BOTH, None),
            P(BOTH, None),
            P(DP, MP),
            P(DP, MP),
            P(DP, MP),
            P(MP, DP),
            P(DP, MP),
            P(MP, DP),
            P(),
            P(),
        ),
        check_vma=False,
    )
```

```python
import functools
import math
from types import SimpleNamespace as Names

import jax
import jax.numpy as jnp
from jax import lax
from jax.experimental import pallas as pl
from jax.experimental.pallas import tpu as pltpu
from jax.sharding import PartitionSpec as P

HEAD_DIM = 128
CLIP_MOST = 256
epsilon = 1e-05
masked_score = -1e30
bf16, f32 = jnp.bfloat16, jnp.float32
VMEM_LIMIT = 60 * 1024 * 1024
MESH = pl.DeviceIdType.MESH
WHOLE, VEC = range(2)
DP, MP = BOTH = ("dp", "mp")


def dot(a, b, ca, cb):
    return lax.dot_general(a, b, (((ca,), (cb,)), ((), ())), preferred_element_type=f32)


def shape(dims, kind=bf16):
    return jax.ShapeDtypeStruct(dims, kind)


def call(kernel, args, grid, in_specs, out_specs, outs, *, name, scalars=(), scratch=(), after=(), flops=0, moved=0, **extra):
    lead = len(scalars) + len(args)

    def body(*refs):
        kernel(*refs[:lead], *refs[lead + len(after) :])

    return pl.pallas_call(
        body,
        grid_spec=pltpu.PrefetchScalarGridSpec(
            num_scalar_prefetch=len(scalars),
            grid=grid,
            in_specs=[*in_specs, *[pl.BlockSpec(memory_space=pl.ANY)] * len(after)],
            out_specs=out_specs,
            scratch_shapes=list(scratch),
        ),
        out_shape=outs,
        compiler_params=pltpu.CompilerParams(vmem_limit_bytes=VMEM_LIMIT, **extra),
        cost_estimate=pl.CostEstimate(flops=flops, bytes_accessed=moved, transcendentals=0),
        name=name,
    )(*scalars, *args, *after)


def norm_parts(values):
    centred = values - jnp.mean(values, axis=-1, keepdims=True)
    spread = jnp.mean(centred * centred, axis=-1, keepdims=True)
    scale = lax.rsqrt(spread + epsilon)
    return centred * scale, scale


def norm_back(values, gain, grad):
    unit, scale = norm_parts(values)
    q = grad * gain
    back = scale * (
        q - jnp.mean(q, axis=-1, keepdims=True) - unit * jnp.mean(q * unit, axis=-1, keepdims=True)
    )
    return back, jnp.sum(grad * unit, axis=0, keepdims=True)


def total(values):
    out = values[0].astype(f32)
    for v in values[1:]:
        out = out + v.astype(f32)
    return out


def gelu_both(u):
    c = math.sqrt(2.0 / math.pi)
    square = u * u
    t = jnp.tanh(c * (u + 0.044715 * (u * square)))
    half = 0.5 * (1.0 + t)
    value = u * half
    slope = half + (0.5 * c) * u * (1.0 - t * t) * (1.0 + (3 * 0.044715) * square)
    return value, slope


def allowed_of(seg_col, seg_row, q0, k0, k1, rows):
    same = seg_col[q0 : q0 + rows, :] == seg_row[:, k0:k1]
    dims = (rows, k1 - k0)
    i = lax.broadcasted_iota(jnp.int32, dims, 0) + q0
    j = lax.broadcasted_iota(jnp.int32, dims, 1) + k0
    return same & (j <= i)


class Wire:
    def __init__(self, send, recv):
        self.send, self.recv, self.count, self.ends = send, recv, 0, []

    def slot(self):
        self.count += 1
        return self.count - 1

    def copy(self, slot, source, target, to):
        return pltpu.make_async_remote_copy(
            src_ref=source,
            dst_ref=target,
            send_sem=self.send.at[slot],
            recv_sem=self.recv.at[slot],
            device_id=to,
            device_id_type=MESH,
        )

    def go(self, source, target, to):
        copy = self.copy(self.slot(), source, target, to)
        copy.start()
        self.ends.append(copy)
        return copy

    def sent(self, *copies):
        for copy in copies:
            copy.wait_send()
            self.ends = [c for c in self.ends if c is not copy]

    def finish(self):
        self.sent(*list(self.ends))


def stage(body, grid, ins, outs):
    pltpu.emit_pipeline(
        body,
        grid=grid,
        in_specs=[pl.BlockSpec(b, f) for _, b, f in ins],
        out_specs=[pl.BlockSpec(b, f) for _, b, f in outs],
    )(*[r for r, _, _ in ins], *[r for r, _, _ in outs])


def layer_kernel(dims, tree, *refs):
    half, width, columns, units, length = dims
    full = 2 * half
    rows = 4 * full
    r = named(jax.tree.unflatten(tree, refs))
    m, d = lax.axis_index(MP), lax.axis_index(DP)
    core, z = lax.rem(d, 2), d // 2
    parity = lax.rem(m, 2)
    to_x = {MP: m + 1 - 2 * parity}
    to_y = {MP: m + 2 - 4 * (m // 2)}
    to_core = {DP: d + 1 - 2 * core}
    wire = Wire(r.send, r.recv)
    heads = columns // HEAD_DIM
    score_scale = 1.0 / math.sqrt(HEAD_DIM)

    barrier = pltpu.get_barrier_semaphore()
    others = [{MP: lax.rem(m + i, 4)} for i in range(1, 4)] + [{DP: lax.rem(d + i, 8)} for i in range(1, 8)]
    for peer in others:
        pl.semaphore_signal(barrier, inc=1, device_id=peer, device_id_type=MESH)
    pl.semaphore_wait(barrier, len(others))

    def at(ref, block):
        return ref.at[pl.ds(block * half, half)]

    qkv_w = r.qkv_w
    loads = [
        pltpu.make_async_copy(w, qkv_w.at[:, pl.ds(i * columns, columns)], r.load.at[i])
        for i, w in enumerate((r.query_weight, r.key_weight, r.value_weight))
    ]
    for load in loads:
        load.start()

    tile = half // 2

    def row_ins(*values):
        out = []
        for v in values:
            ref, f = v if isinstance(v, tuple) else (v, lambda i: (i, 0))
            out.append((ref, (1 if ref.shape[0] == 1 else tile, width), (lambda i: (0, 0)) if ref.shape[0] == 1 else f))
        return out

    def row_wise(fn, ins, outs):
        n = len(ins)

        def body(*refs):
            for ref, value in zip(refs[n:], fn(*[x[...] for x in refs[:n]])):
                ref[...] = value.astype(ref.dtype)

        stage(body, (4,), row_ins(*ins), row_ins(*outs))

    def spread(ref):
        return {
            2: wire.go(at(ref, 0), at(ref, 2), to_x),
            5: wire.go(at(ref, 1), at(ref, 5), to_y),
            3: wire.go(at(ref, 1), at(ref, 3), to_x),
            4: wire.go(at(ref, 0), at(ref, 4), to_y),
        }

    def relay(ref):
        return {6: wire.go(at(ref, 2), at(ref, 6), to_y), 7: wire.go(at(ref, 5), at(ref, 7), to_x)}

    def send_far(into, terms):
        return [wire.go(at(terms, 6), at(into.far, 0), to_x), wire.go(at(terms, 7), at(into.far, 1), to_y)]

    def send_early(into, terms):
        return [wire.go(at(terms, 2), at(into.early, 0), to_x), wire.go(at(terms, 5), at(into.early, 1), to_y)]

    def send_late(into, terms, far, sums):
        for copy in far:
            copy.wait_recv()
        row_wise(
            lambda a, b: (a.astype(f32) + b.astype(f32),),
            [(terms, lambda i: (jnp.where(i < 2, 8 + i, 4 + i), 0)), into.far],
            [sums],
        )
        return [wire.go(at(sums, 0), at(into.late, 0), to_y), wire.go(at(sums, 1), at(into.late, 1), to_x)]

    def arrive(*copies):
        for copy in copies:
            copy.wait_recv()

    def product(source, target, blocks, weight, size, count, trans=False, scale=None):
        n = len(blocks)
        depth = source.shape[1]
        ref, ref_block, ref_map = weight if isinstance(weight, tuple) else (None, None, None)

        def body(*refs):
            j = pl.program_id(0)
            x = jnp.concatenate([b[...] for b in refs[:n]], axis=0) if n > 1 else refs[0][...]
            w = refs[n][...] if ref is not None else weight(j)
            acc = dot(x, w, 1, 1 if trans else 0)
            if scale is not None:
                acc = acc * scale(j)
            for i, out in enumerate(refs[-n:]):
                out[...] = acc[i * half : (i + 1) * half].astype(bf16)

        stage(
            body,
            (count,),
            [(source, (half, depth), lambda j, b=b: (b, 0)) for b in blocks]
            + ([(ref, ref_block, ref_map)] if ref is not None else []),
            [(target, (half, size), lambda j, b=b: (b, j)) for b in blocks],
        )

    def project(*blocks):
        product(
            r.attn_in,
            r.qkv,
            blocks,
            lambda j: qkv_w[:, pl.ds(pl.multiple_of(j * columns, columns), columns)],
            columns,
            3,
            scale=lambda j: jnp.where(j == 0, score_scale, 1.0),
        )

    def out_project(*blocks):
        product(
            r.context,
            r.out_terms,
            blocks,
            (r.out_weight, (columns, width // 2), lambda j: (0, j)),
            width // 2,
            2,
        )

    def context_back(*blocks):
        product(
            r.middle_all,
            r.context_grad,
            blocks,
            (r.out_weight, (columns // 2, width), lambda j: (j, 0)),
            columns // 2,
            2,
            trans=True,
        )

    def project_back(*blocks):
        size = width // 4
        product(
            r.qkv_grad,
            r.out_terms,
            blocks,
            lambda j: qkv_w[pl.ds(pl.multiple_of(j * size, size), size), :],
            size,
            4,
            trans=True,
        )

    def turn(block, target):
        for b in range(2):
            to = pl.multiple_of(lax.rem(parity + b, 2) * full, full)
            target[pl.ds(to, full), :] = block[b * full : (b + 1) * full, :]

    def turn_back(source, block):
        for b in range(2):
            come = pl.multiple_of(lax.rem(parity + b, 2) * full, full)
            block[b * full : (b + 1) * full, :] = source[pl.ds(come, full), :].astype(bf16)

    q, k, v, c = r.q, r.k, r.v, r.c
    f0, f1, f2 = r.f0, r.f1, r.f2

    def head_ins(s):
        ins = [
            (r.seg_col, (1, length, 1), lambda h: (lax.rem(m // 2 + s, 2), 0, 0)),
            (r.seg_row, (1, 1, length), lambda h: (lax.rem(m // 2 + s, 2), 0, 0)),
        ]
        for which in range(3):
            ins.append((r.qkv, (length, HEAD_DIM), lambda h, w=which: (s, w * heads + h)))
        return ins

    def scores_of(seg_col, seg_row, q0, k0, k1):
        s = dot(q[q0:k1, :], k[k0:k1, :], 1, 1)
        keep = allowed_of(seg_col.at[0], seg_row.at[0], q0, k0, k1, CLIP_MOST)
        s = jnp.where(keep, s, masked_score)
        e = jnp.exp(s - jnp.max(s, axis=-1, keepdims=True))
        return e * (1.0 / jnp.sum(e, axis=-1, keepdims=True))

    def attend(s):
        def body(seg_col, seg_row, q_in, k_in, v_in, out):
            turn(q_in, q)
            turn(k_in, k)
            turn(v_in, v)
            for q0 in range(0, length, CLIP_MOST):
                k0, k1 = max(0, q0 - CLIP_MOST), q0 + CLIP_MOST
                p = scores_of(seg_col, seg_row, q0, k0, k1).astype(bf16)
                f0[q0:k1, :] = dot(p, v[k0:k1, :], 1, 0)
            turn_back(f0, out)

        stage(body, (heads,), head_ins(s), [(r.context, (length, HEAD_DIM), lambda h: (s, h))])

    def attend_back(s):
        def body(seg_col, seg_row, q_in, k_in, v_in, c_in, dq_out, dk_out, dv_out):
            turn(q_in, q)
            turn(k_in, k)
            turn(v_in, v)
            turn(c_in, c)
            for q0 in range(0, length, CLIP_MOST):
                k0, k1 = max(0, q0 - CLIP_MOST), q0 + CLIP_MOST
                p = scores_of(seg_col, seg_row, q0, k0, k1)
                qb, cb, kb, vb = q[q0:k1, :], c[q0:k1, :], k[k0:k1, :], v[k0:k1, :]
                dp = dot(cb, vb, 1, 1)
                inner = jnp.sum(p * dp, axis=-1, keepdims=True)
                ds = (p * (dp - inner)).astype(bf16)
                f0[q0:k1, :] = dot(ds, kb, 1, 0) * score_scale
                dk, dv = dot(ds, qb, 0, 0), dot(p.astype(bf16), cb, 0, 0)
                if q0 > 0:
                    f1[k0:q0, :] += dk[:CLIP_MOST]
                    f2[k0:q0, :] += dv[:CLIP_MOST]
                    dk, dv = dk[CLIP_MOST:], dv[CLIP_MOST:]
                f1[q0:k1, :] = dk
                f2[q0:k1, :] = dv
            turn_back(f0, dq_out)
            turn_back(f1, dk_out)
            turn_back(f2, dv_out)

        stage(
            body,
            (heads,),
            [*head_ins(s), (r.context_grad, (length, HEAD_DIM), lambda h: (s, h))],
            [(r.qkv_grad, (length, HEAD_DIM), lambda h, w=w: (s, w * heads + h)) for w in range(3)],
        )

    acc_g, slopes = r.acc_g, r.slopes
    size = 512
    tiles = units // size
    up_tile = (r.up_weight, (width, size), lambda j: (0, j))
    down_tile = (r.down_weight, (size, width), lambda j: (j, 0))

    def whole(ref, both):
        return [(ref, (half, width), lambda j, i=i: (i, 0)) for i in both]

    def part(ref, both):
        return [(ref, (half, size), lambda j, i=i: (i, j)) for i in both]

    def rows_of(a, b):
        return jnp.concatenate([a[...], b[...]], axis=0)

    def grads_of(grad, up, p0, p1, g0, g1):
        j = pl.program_id(0)
        grad = grad.astype(bf16)
        p0[...], p1[...] = grad[:half], grad[half:]
        g = dot(grad, up[...], 1, 1)

        @pl.when(j == 0)
        def _():
            acc_g[...] = g

        @pl.when((j > 0) & (j < tiles - 1))
        def _():
            acc_g[...] += g

        @pl.when(j == tiles - 1)
        def _():
            last = acc_g[...] + g
            g0[...], g1[...] = last[:half].astype(bf16), last[half:].astype(bf16)

    def feed(*both):
        def body(x0, x1, c0, c1, up, down, h0, h1, *outs):
            value, slope = gelu_both(dot(rows_of(x0, x1), up[...], 1, 0))
            value = value.astype(bf16)
            h0[...], h1[...] = value[:half], value[half:]
            grads_of(dot(rows_of(c0, c1), down[...], 1, 1) * slope, up, *outs)

        stage(
            body,
            (tiles,),
            [*whole(r.mlp_in, both), *whole(r.cot_all, both), up_tile, down_tile],
            [*part(r.hidden, both), *part(r.pre_grad, both), *whole(r.mid_terms, both)],
        )

    def feed_forward(*both):
        def body(x0, x1, up, h0, h1):
            value, slope = gelu_both(dot(rows_of(x0, x1), up[...], 1, 0))
            value = value.astype(bf16)
            h0[...], h1[...] = value[:half], value[half:]
            slopes[pl.program_id(0)] = slope

        stage(body, (tiles,), [*whole(r.mlp_in, both), up_tile], part(r.hidden, both))

    def feed_back(*both):
        def body(c0, c1, up, down, *outs):
            grads_of(dot(rows_of(c0, c1), down[...], 1, 1) * slopes[pl.program_id(0)], up, *outs)

        stage(
            body,
            (tiles,),
            [*whole(r.cot_all, both), up_tile, down_tile],
            [*part(r.pre_grad, both), *whole(r.mid_terms, both)],
        )

    down_acc = r.down_acc
    share = width // 8

    def down_some(first, count, both, target=None, plus=None):
        begin = 0 in both
        n = len(both)

        def body(*refs):
            s = pl.program_id(0)
            left, right = ([b[...] for b in refs[i * n : (i + 1) * n]] for i in range(2))
            acc = dot(jnp.concatenate(left, axis=0), jnp.concatenate(right, axis=0), 0, 0)
            if not begin:
                acc = acc + down_acc[first + s]
            if target is None:
                down_acc[first + s] = acc
                return
            if plus is not None:
                acc = acc + refs[2 * n][0].astype(f32)
            refs[-1][0] = acc.astype(bf16)

        def column(s):
            k = first + s
            return 2 * lax.rem(k, 4) + jnp.where(k < 4, 1 - core, core)

        block = (1, share, units)
        stage(
            body,
            (count,),
            [(r.cot_all, (half, share), lambda s, i=i: (i, column(s))) for i in both]
            + [(r.hidden, (half, units), lambda s, i=i: (i, 0)) for i in both]
            + ([(plus, block, lambda s: (s, 0, 0))] if plus is not None else []),
            [(target, block, lambda s: (s, 0, 0))] if target is not None else [],
        )

    def grad_product(left, right, which, target, plus=None):
        def body(a, b, *rest):
            acc = dot(a[...], b[...], 0, 0)
            if plus is not None:
                acc = acc + rest[0][0].astype(f32)
            rest[-1][0] = acc.astype(bf16)

        n = right.shape[1]
        block = (1, share, n)
        place = lambda s: (s, 0, 0)
        stage(
            body,
            (4,),
            [
                (left, (rows, share), lambda s: (0, 2 * s + which)),
                (right, (rows, n), lambda s: (0, 0)),
                *([(plus, block, place)] if plus is not None else []),
            ],
            [(target, block, place)],
        )

    def grad_first(into, left, right):
        grad_product(left, right, 1 - core, into.mine)
        return wire.go(into.mine, into.got, to_core)

    def line(mine, got, sums, step, place):
        pick = lambda at: jnp.clip(at if step > 0 else 3 - at, 0, 3)
        slots = [wire.slot() for _ in range(3)]
        to = {DP: jnp.clip(d + 2 * step, 0, 7)}

        def copy(t, source):
            return wire.copy(slots[t], source, got.at[t], to)

        @pl.when(place == 0)
        def _():
            for t in range(3):
                copy(t, mine.at[pick(3 - t)]).start()

        def forward(t):
            @pl.when((place >= 1) & (place <= t + 1))
            def _():
                copy(t, mine.at[0]).wait_recv()
                n = mine.shape[2]
                size = mine.shape[1] // 2

                def body(a, b, out):
                    out[...] = (a[0].astype(f32) + b[...].astype(f32)).astype(bf16)

                stage(
                    body,
                    (2,),
                    [
                        (mine, (1, size, n), lambda i: (pick(place + 2 - t), i, 0)),
                        (got.at[t], (size, n), lambda i: (i, 0)),
                    ],
                    [(sums.at[t], (size, n), lambda i: (i, 0))],
                )
                copy(t + 1, sums.at[t]).start()

        def end():
            @pl.when(place >= 1)
            def _():
                copy(2, mine.at[0]).wait_recv()

            for t in range(3):

                @pl.when((place <= t) & (place < 3))
                def _():
                    copy(t, mine.at[0]).wait_send()

        return forward, end

    def grad_second(into, left, right, swap):
        swap.wait_recv()
        wire.sent(swap)
        grad_product(left, right, core, into.mine, into.got)
        return start_line(into)

    def start_line(into):
        up = line(into.mine, into.right, into.right_sums, 1, z)
        down = line(into.mine, into.left, into.left_sums, -1, 3 - z)

        def forward(t):
            up[0](t)
            down[0](t)

        def end(turned=None):
            up[1]()
            down[1]()
            if turned is not None:
                share_total(into, turned)

        return forward, end

    def share_total(into, target):
        turned = target.shape[1] == share
        n = into.mine.shape[2]
        tile = 128

        def body(own, right, left, out):
            value = own[0].astype(f32)
            value = value + jnp.where(z > 0, right[0].astype(f32), 0.0)
            value = value + jnp.where(z < 3, left[0].astype(f32), 0.0)
            out[...] = value.T if turned else value

        block = (1, tile, n)
        stage(
            body,
            (share // tile,),
            [(into.mine, block, lambda i: (z, i, 0)), (into.right, block, lambda i: (2, i, 0)), (into.left, block, lambda i: (2, i, 0))],
            [(target, (n, tile), lambda i: (0, i)) if turned else (target, (tile, n), lambda i: (i, 0))],
        )

    def over_all(slots, value, me, axis, count):
        copies = [wire.go(value, slots.at[me], {axis: lax.rem(me + i, count)}) for i in range(1, count)]
        slots[pl.ds(me, 1)] = value[...][None]
        arrive(*copies)
        return functools.reduce(lambda a, i: a + slots[i], range(1, count), slots[0])

    attn_in, cot_all, mlp_in, middle_all = r.attn_in, r.cot_all, r.mlp_in, r.middle_all
    row_wise(
        lambda x, g: (norm_parts(x.astype(f32))[0] * g,), [r.tokens, r.attn_gain], [attn_in]
    )
    near = spread(attn_in)
    row_wise(lambda x: (x,), [r.out_cotangent], [cot_all])
    for load in loads:
        load.wait()
    project(0, 1)
    arrive(near[2], near[5])
    far = relay(attn_in)
    arrive(near[3], near[4])
    cot_near = {2: wire.go(at(cot_all, 0), at(cot_all, 2), to_x), 5: wire.go(at(cot_all, 1), at(cot_all, 5), to_y)}
    project(2, 3, 4, 5)
    attend(0)
    arrive(far[6], far[7])
    project(6, 7)
    attend(1)
    out_terms = r.out_terms
    out_project(6, 7)
    attn_far = send_far(r.attn, out_terms)
    out_project(2, 3, 4, 5)
    attn_early = send_early(r.attn, out_terms)
    out_project(0, 1)
    attn_late = send_late(r.attn, out_terms, attn_far, r.sums_a)
    cot_near[3] = wire.go(at(cot_all, 1), at(cot_all, 3), to_x)
    cot_near[4] = wire.go(at(cot_all, 0), at(cot_all, 4), to_y)
    arrive(*attn_early, *attn_late)

    def second(x, g, a, b, c_):
        mid = x.astype(f32) + a.astype(f32) + b.astype(f32) + c_.astype(f32)
        return mid, norm_parts(mid)[0] * g

    row_wise(
        second,
        [r.tokens, r.mlp_gain, out_terms, r.attn.early, r.attn.late],
        [r.residual_mid, mlp_in],
    )
    near = spread(mlp_in)
    arrive(cot_near[2], cot_near[5])
    feed(0, 1)
    arrive(near[2], near[5])
    far = relay(mlp_in)
    cot_far = relay(cot_all)
    feed(2, 5)
    mid_terms = r.mid_terms
    mid_early = send_early(r.mid, mid_terms)
    down_some(0, 8, (0, 1, 2, 5))
    arrive(near[3], near[4], cot_near[3], cot_near[4])
    feed(3, 4)
    arrive(far[6], far[7])
    feed_forward(6, 7)
    arrive(cot_far[6], cot_far[7])
    down, last = r.down_grad, (3, 4, 6, 7)
    down_some(0, 4, last, down.mine)
    swap = wire.go(down.mine, down.got, to_core)
    feed_back(6, 7)
    mid_far = send_far(r.mid, mid_terms)
    arrive(swap)
    wire.sent(swap)
    down_some(4, 4, last, down.mine, down.got)
    down_forward, down_end = start_line(down)
    swap = grad_first(r.up_grad, mlp_in, r.pre_grad)
    mid_late = send_late(r.mid, mid_terms, mid_far, r.sums_b)
    mlp_terms = r.mlp_terms

    def down_project(*blocks):
        product(r.hidden, mlp_terms, blocks, (r.down_weight, (units, size), lambda j: (0, j)), size, width // size)

    down_project(6, 7, 2, 3)
    down_forward(0)
    arrive(*mid_early, *mid_late)
    gain_sum = r.gain_sum
    gain_sum[...] = jnp.zeros_like(gain_sum)

    def second_back(mid, g, cot, a, b, c_):
        back, gain = norm_back(mid, g, a.astype(f32) + b.astype(f32) + c_.astype(f32))
        gain_sum[1:2, :] += gain
        value = cot.astype(f32) + back
        return value, value

    row_wise(
        second_back,
        [r.residual_mid, r.mlp_gain, r.out_cotangent, mid_terms, r.mid.early, r.mid.late],
        [r.middle, middle_all],
    )
    near = spread(middle_all)

    up_forward, up_end = grad_second(r.up_grad, mlp_in, r.pre_grad, swap)
    arrive(near[2], near[5])
    far = relay(middle_all)
    mlp_far = send_far(r.attn, mlp_terms)
    down_forward(1)
    context_back(0, 1)
    down_project(4, 5, 0, 1)
    arrive(near[3], near[4])
    context_back(2, 3, 4, 5)
    attend_back(0)
    arrive(far[6], far[7])
    context_back(6, 7)
    up_forward(0)
    attend_back(1)
    wire.sent(*attn_far, *attn_early)
    project_back(6, 7)
    back_far = send_far(r.mid, out_terms)
    swap = grad_first(r.qkv_w_grad, attn_in, r.qkv_grad)
    project_back(2, 3, 4, 5)
    back_early = send_early(r.mid, out_terms)
    qkv_forward, qkv_end = grad_second(r.qkv_w_grad, attn_in, r.qkv_grad, swap)
    wire.sent(*mid_late)
    back_late = send_late(r.mid, out_terms, back_far, r.sums_b)
    up_forward(1)
    mlp_early = send_early(r.attn, mlp_terms)
    swap = grad_first(r.out_grad, middle_all, r.context)
    wire.sent(*attn_late)
    mlp_late = send_late(r.attn, mlp_terms, mlp_far, r.sums_a)
    out_forward, out_end = grad_second(r.out_grad, middle_all, r.context, swap)
    project_back(0, 1)
    qkv_forward(0)
    down_end(r.down_total)
    arrive(*back_early, *back_late)

    def first_back(x, mid, g, a, b, c_):
        back, gain = norm_back(x.astype(f32), g, a.astype(f32) + b.astype(f32) + c_.astype(f32))
        gain_sum[0:1, :] += gain
        return (mid + back,)

    row_wise(
        first_back,
        [r.tokens, r.middle, r.attn_gain, out_terms, r.mid.early, r.mid.late],
        [r.tokens_grad],
    )
    qkv_forward(1)
    r.gain_near_sum[...] = over_all(r.gain_near, gain_sum, m, MP, 4)
    r.gains[...] = over_all(r.gain_far, r.gain_near_sum, d, DP, 8)
    up_end(r.up_total)
    out_forward(0)
    out_forward(1)
    arrive(*mlp_early, *mlp_late)
    row_wise(
        lambda mid, *t: (mid + total(t),),
        [r.residual_mid, mlp_terms, r.attn.early, r.attn.late],
        [r.layer_output],
    )
    qkv_end()
    out_end(r.out_total)
    wire.finish()


def named(tree):
    return Names(**{k: named(v) for k, v in tree.items()}) if isinstance(tree, dict) else tree


def layer(ins, half, width, columns, units, length):
    full, rows = 2 * half, 8 * half
    share = width // 8
    big, own = shape((rows, width)), shape((full, width))
    arrivals = dict(far=own, early=own, late=own)

    def grad(n):
        line, sums = shape((3, share, n)), shape((2, share, n))
        stack = shape((4, share, n))
        return dict(mine=stack, got=stack, right=line, left=line, right_sums=sums, left_sums=sums)

    outs = dict(
        attn_in=big,
        cot_all=big,
        mlp_in=big,
        middle_all=big,
        out_terms=big,
        mlp_terms=big,
        mid_terms=big,
        hidden=shape((rows, units)),
        pre_grad=shape((rows, units)),
        qkv=shape((rows, 3 * columns)),
        qkv_grad=shape((rows, 3 * columns)),
        context=shape((rows, columns)),
        context_grad=shape((rows, columns)),
        attn=arrivals,
        mid=arrivals,
        sums_a=own,
        sums_b=own,
        down_grad=grad(units),
        up_grad=grad(units),
        qkv_w_grad=grad(3 * columns),
        out_grad=grad(columns),
        residual_mid=shape((full, width), f32),
        middle=shape((full, width), f32),
        layer_output=own,
        tokens_grad=shape((full, width), f32),
        down_total=shape((units, share), f32),
        up_total=shape((share, units), f32),
        out_total=shape((columns, share), f32),
    )
    any_, vmem = pl.BlockSpec(memory_space=pl.ANY), pl.BlockSpec(memory_space=pltpu.VMEM)
    places = dict(jax.tree.map(lambda _: any_, outs), gains=vmem)
    outs = dict(outs, gains=shape((2, width), f32))
    head, head_sum = pltpu.VMEM((length, HEAD_DIM), bf16), pltpu.VMEM((length, HEAD_DIM), f32)
    acc = pltpu.VMEM((full, width), f32)
    scratch = dict(
        qkv_w=pltpu.VMEM((width, 3 * columns), bf16),
        acc_g=acc,
        slopes=pltpu.VMEM((units // 512, full, 512), f32),
        down_acc=pltpu.VMEM((8, share, units), f32),
        gain_sum=pltpu.VMEM((2, width), f32),
        gain_near_sum=pltpu.VMEM((2, width), f32),
        gain_near=pltpu.VMEM((4, 2, width), f32),
        gain_far=pltpu.VMEM((8, 2, width), f32),
        q=head,
        k=head,
        v=head,
        c=head,
        f0=head_sum,
        f1=head_sum,
        f2=head_sum,
        send=pltpu.SemaphoreType.DMA((96,)),
        recv=pltpu.SemaphoreType.DMA((96,)),
        load=pltpu.SemaphoreType.DMA((3,)),
    )
    parts = [jax.tree.flatten(t) for t in (ins, outs, scratch)]
    kinds = [jax.tree.unflatten(t, range(len(v))) for v, t in parts]
    starts = (0, len(parts[0][0]), len(parts[0][0]) + len(parts[1][0]))
    place_of = {}
    for kind, begin in zip(kinds, starts):
        place_of.update(jax.tree.map(lambda i, b=begin: b + i, kind))
    order, tree = jax.tree.flatten(place_of)

    def kernel(*refs):
        layer_kernel((half, width, columns, units, length), tree, *[refs[i] for i in order])

    got = pl.pallas_call(
        kernel,
        in_specs=[any_] * len(parts[0][0]),
        out_specs=jax.tree.leaves(places),
        out_shape=parts[1][0],
        scratch_shapes=parts[2][0],
        compiler_params=pltpu.CompilerParams(
            collective_id=1, has_side_effects=True, vmem_limit_bytes=VMEM_LIMIT
        ),
        name="layer",
    )(*parts[0][0])
    return named(jax.tree.unflatten(parts[1][1], got))


def share_total(got, z, columns):
    mine, right, left = got.mine, got.right, got.left
    _, rows, width = mine.shape
    tile = 128

    def kernel(place, own, a, b, *outs):
        value = own[0].astype(f32)
        value = value + jnp.where(place[0] > 0, a[0].astype(f32), 0.0)
        value = value + jnp.where(place[0] < 3, b[0].astype(f32), 0.0)
        at = 0
        for out in outs:
            out[...] = value[:, at : at + out.shape[1]]
            at += out.shape[1]

    return call(
        kernel,
        [mine, right, left],
        (rows // tile,),
        [pl.BlockSpec((1, tile, width), lambda i, p: (p[0], i, 0))]
        + [pl.BlockSpec((1, tile, width), lambda i, p: (2, i, 0))] * 2,
        [pl.BlockSpec((tile, c), lambda i, p: (i, 0)) for c in columns],
        [shape((rows, c), f32) for c in columns],
        scalars=[z.astype(jnp.int32).reshape(1)],
        name="share_total",
        flops=rows * width,
        moved=rows * width * 10,
    )


def norm_rows(values, gain):
    centre = jnp.mean(values, axis=-1, keepdims=True)
    centred = values - centre
    spread = jnp.mean(centred * centred, axis=-1, keepdims=True)
    return centred * lax.rsqrt(spread + epsilon) * gain


def gelu_tanh(values):
    return jax.nn.gelu(values, approximate=True)


def block_allowed(segment):
    position = jnp.arange(segment.shape[0])
    return (position[None, :] <= position[:, None]) & (segment[:, None] == segment[None, :])


def rows_times(left_rows, right_matrix):
    return jnp.dot(left_rows, right_matrix, preferred_element_type=jnp.float32)


def rows_times_back(left_rows, right_matrix):
    return lax.dot_general(
        left_rows, right_matrix, (((1,), (1,)), ((), ())), preferred_element_type=jnp.float32
    )


def attn_input_back(
    queries_grad, keys_grad, values_grad, query_weight, key_weight, value_weight, score_scale
):
    total_grad = rows_times_back(queries_grad, query_weight) * score_scale
    total_grad = total_grad + rows_times_back(keys_grad, key_weight)
    return total_grad + rows_times_back(values_grad, value_weight)


def attend_forward(packed):
    queries, keys_in, values_in, segment = packed
    scores = jnp.einsum("qhd,khd->hqk", queries, keys_in, preferred_element_type=jnp.float32)
    scores = jnp.where(block_allowed(segment)[None], scores, masked_score)
    row_max = jnp.max(scores, axis=-1, keepdims=True)
    expanded = jnp.exp(scores - row_max)
    row_total = jnp.sum(expanded, axis=-1, keepdims=True)
    probs_low = (expanded / row_total).astype(jnp.bfloat16)
    context = jnp.einsum("hqk,khd->qhd", probs_low, values_in, preferred_element_type=jnp.float32)
    return (context.astype(jnp.bfloat16), (row_max + jnp.log(row_total))[:, :, 0])


def attend_backward(packed):
    queries, keys_in, values_in, segment, context_grad, log_total = packed
    scores = jnp.einsum("qhd,khd->hqk", queries, keys_in, preferred_element_type=jnp.float32)
    scores = jnp.where(block_allowed(segment)[None], scores, masked_score)
    attn_probs = jnp.exp(scores - log_total[:, :, None])
    probs_grad = jnp.einsum(
        "qhd,khd->hqk", context_grad, values_in, preferred_element_type=jnp.float32
    )
    values_grad = jnp.einsum(
        "hqk,qhd->khd",
        attn_probs.astype(jnp.bfloat16),
        context_grad,
        preferred_element_type=jnp.float32,
    )
    inner_sum = jnp.sum(attn_probs * probs_grad, axis=-1, keepdims=True)
    scores_grad = (attn_probs * (probs_grad - inner_sum)).astype(jnp.bfloat16)
    queries_grad = jnp.einsum(
        "hqk,khd->qhd", scores_grad, keys_in, preferred_element_type=jnp.float32
    )
    keys_grad = jnp.einsum("hqk,qhd->khd", scores_grad, queries, preferred_element_type=jnp.float32)
    return (
        queries_grad.astype(jnp.bfloat16),
        keys_grad.astype(jnp.bfloat16),
        values_grad.astype(jnp.bfloat16),
    )


def local_plain(
    tokens,
    segment_ids,
    query_weight,
    key_weight,
    value_weight,
    out_weight,
    up_weight,
    down_weight,
    attn_gain,
    mlp_gain,
    out_cotangent,
):
    seq_count, seq_length = segment_ids.shape
    group_rows = seq_count * seq_length
    head_count = query_weight.shape[1] // HEAD_DIM
    score_scale = 1.0 / math.sqrt(HEAD_DIM)
    shaped = (seq_count, seq_length, head_count, HEAD_DIM)
    flat_shape = (group_rows, head_count * HEAD_DIM)
    residual_in = tokens.astype(jnp.float32)
    normed_attn, attn_norm_back = jax.vjp(norm_rows, residual_in, attn_gain)
    gathered_attn = lax.all_gather(normed_attn.astype(jnp.bfloat16), MP, axis=0, tiled=True)
    queries = (
        jnp.dot(gathered_attn, query_weight, preferred_element_type=jnp.float32) * score_scale
    ).astype(jnp.bfloat16)
    keys_all = jnp.dot(gathered_attn, key_weight, preferred_element_type=jnp.float32).astype(
        jnp.bfloat16
    )
    values_all = jnp.dot(gathered_attn, value_weight, preferred_element_type=jnp.float32).astype(
        jnp.bfloat16
    )
    queries_seq = queries.reshape(shaped)
    keys_seq = keys_all.reshape(shaped)
    values_seq = values_all.reshape(shaped)
    context, log_total = lax.map(attend_forward, (queries_seq, keys_seq, values_seq, segment_ids))
    context_flat = context.reshape(flat_shape)
    attn_rows = lax.psum_scatter(
        rows_times(context_flat, out_weight).astype(jnp.bfloat16),
        MP,
        scatter_dimension=0,
        tiled=True,
    ).astype(jnp.float32)
    residual_mid = residual_in + attn_rows
    normed_mlp, mlp_norm_back = jax.vjp(norm_rows, residual_mid, mlp_gain)
    gathered_mlp = lax.all_gather(normed_mlp.astype(jnp.bfloat16), MP, axis=0, tiled=True)
    pre_act = jnp.dot(gathered_mlp, up_weight, preferred_element_type=jnp.float32)
    activated, gelu_back = jax.vjp(gelu_tanh, pre_act)
    hidden = activated.astype(jnp.bfloat16)
    mlp_rows = lax.psum_scatter(
        rows_times(hidden, down_weight).astype(jnp.bfloat16), MP, scatter_dimension=0, tiled=True
    ).astype(jnp.float32)
    layer_output = (residual_mid + mlp_rows).astype(jnp.bfloat16)
    cotangent_all = lax.all_gather(out_cotangent, MP, axis=0, tiled=True)
    down_weight_grad = jnp.einsum(
        "rf,rd->fd", hidden, cotangent_all, preferred_element_type=jnp.float32
    )
    hidden_grad = lax.dot_general(
        cotangent_all, down_weight, (((1,), (1,)), ((), ())), preferred_element_type=jnp.float32
    )
    pre_grad = gelu_back(hidden_grad)[0].astype(jnp.bfloat16)
    up_weight_grad = jnp.einsum(
        "rd,rf->df", gathered_mlp, pre_grad, preferred_element_type=jnp.float32
    )
    normed_mlp_grad = lax.psum_scatter(
        rows_times_back(pre_grad, up_weight).astype(jnp.bfloat16),
        MP,
        scatter_dimension=0,
        tiled=True,
    ).astype(jnp.float32)
    middle_back, mlp_gain_grad = mlp_norm_back(normed_mlp_grad)
    middle_grad = out_cotangent.astype(jnp.float32) + middle_back
    middle_all_grad = lax.all_gather(middle_grad.astype(jnp.bfloat16), MP, axis=0, tiled=True)
    out_weight_grad = jnp.einsum(
        "rc,rd->cd", context_flat, middle_all_grad, preferred_element_type=jnp.float32
    )
    context_grad = lax.dot_general(
        middle_all_grad, out_weight, (((1,), (1,)), ((), ())), preferred_element_type=jnp.float32
    ).astype(jnp.bfloat16)
    queries_grad, keys_grad, values_grad = lax.map(
        attend_backward,
        (queries_seq, keys_seq, values_seq, segment_ids, context_grad.reshape(shaped), log_total),
    )
    queries_grad = queries_grad.reshape(flat_shape)
    keys_grad = keys_grad.reshape(flat_shape)
    values_grad = values_grad.reshape(flat_shape)
    query_weight_grad = (
        jnp.einsum("rd,rc->dc", gathered_attn, queries_grad, preferred_element_type=jnp.float32)
        * score_scale
    )
    key_weight_grad = jnp.einsum(
        "rd,rc->dc", gathered_attn, keys_grad, preferred_element_type=jnp.float32
    )
    value_weight_grad = jnp.einsum(
        "rd,rc->dc", gathered_attn, values_grad, preferred_element_type=jnp.float32
    )
    normed_attn_grad = lax.psum_scatter(
        attn_input_back(
            queries_grad,
            keys_grad,
            values_grad,
            query_weight,
            key_weight,
            value_weight,
            score_scale,
        ).astype(jnp.bfloat16),
        MP,
        scatter_dimension=0,
        tiled=True,
    ).astype(jnp.float32)
    token_back, attn_gain_grad = attn_norm_back(normed_attn_grad)
    tokens_grad = middle_grad + token_back
    attn_gain_grad, mlp_gain_grad = lax.psum((attn_gain_grad, mlp_gain_grad), (DP, MP))
    (
        query_weight_grad,
        key_weight_grad,
        value_weight_grad,
        out_weight_grad,
        up_weight_grad,
        down_weight_grad,
    ) = (
        lax.psum_scatter(
            query_weight_grad.astype(jnp.bfloat16), DP, scatter_dimension=0, tiled=True
        ).astype(jnp.float32),
        lax.psum_scatter(
            key_weight_grad.astype(jnp.bfloat16), DP, scatter_dimension=0, tiled=True
        ).astype(jnp.float32),
        lax.psum_scatter(
            value_weight_grad.astype(jnp.bfloat16), DP, scatter_dimension=0, tiled=True
        ).astype(jnp.float32),
        lax.psum_scatter(
            out_weight_grad.astype(jnp.bfloat16), DP, scatter_dimension=1, tiled=True
        ).astype(jnp.float32),
        lax.psum_scatter(
            up_weight_grad.astype(jnp.bfloat16), DP, scatter_dimension=0, tiled=True
        ).astype(jnp.float32),
        lax.psum_scatter(
            down_weight_grad.astype(jnp.bfloat16), DP, scatter_dimension=1, tiled=True
        ).astype(jnp.float32),
    )
    return (
        layer_output,
        tokens_grad,
        query_weight_grad,
        key_weight_grad,
        value_weight_grad,
        out_weight_grad,
        up_weight_grad,
        down_weight_grad,
        attn_gain_grad,
        mlp_gain_grad,
    )


def local(
    mp,
    dp,
    tokens,
    segment_ids,
    query_weight,
    key_weight,
    value_weight,
    out_weight,
    up_weight,
    down_weight,
    attn_gain,
    mlp_gain,
    out_cotangent,
):
    width, columns = query_weight.shape
    length = segment_ids.shape[1]
    half = tokens.shape[0] // 2
    z = lax.axis_index(DP) // 2
    attn_gain, mlp_gain = attn_gain.reshape(1, width), mlp_gain.reshape(1, width)
    got = layer(
        dict(
            tokens=tokens,
            seg_col=segment_ids.reshape(2, length, 1),
            seg_row=segment_ids.reshape(2, 1, length),
            query_weight=query_weight,
            key_weight=key_weight,
            value_weight=value_weight,
            out_weight=out_weight,
            up_weight=up_weight,
            down_weight=down_weight,
            attn_gain=attn_gain,
            mlp_gain=mlp_gain,
            out_cotangent=out_cotangent,
        ),
        half,
        width,
        columns,
        up_weight.shape[1],
        length,
    )

    qkv_grads = share_total(got.qkv_w_grad, z, [columns] * 3)
    return (
        got.layer_output,
        got.tokens_grad,
        *qkv_grads,
        got.out_total,
        got.up_total,
        got.down_total,
        got.gains[0],
        got.gains[1],
    )


def solution(mesh):
    mp, dp = mesh.shape[MP], mesh.shape[DP]
    return jax.shard_map(
        functools.partial(local, mp, dp) if (mp, dp) == (4, 8) else local_plain,
        mesh=mesh,
        in_specs=(
            P(BOTH, None),
            P(DP, None),
            P(None, MP),
            P(None, MP),
            P(None, MP),
            P(MP, None),
            P(None, MP),
            P(MP, None),
            P(),
            P(),
            P(BOTH, None),
        ),
        out_specs=(
            P(BOTH, None),
            P(BOTH, None),
            P(DP, MP),
            P(DP, MP),
            P(DP, MP),
            P(MP, DP),
            P(DP, MP),
            P(MP, DP),
            P(),
            P(),
        ),
        check_vma=False,
    )
```

```python
import functools
import math
from types import SimpleNamespace as Names

import jax
import jax.numpy as jnp
from jax import lax
from jax.experimental import pallas as pl
from jax.experimental.pallas import tpu as pltpu
from jax.sharding import PartitionSpec as P

HEAD_DIM = 128
CLIP_MOST = 256
epsilon = 1e-05
masked_score = -1e30
bf16, f32 = jnp.bfloat16, jnp.float32
VMEM_LIMIT = 60 * 1024 * 1024
MESH = pl.DeviceIdType.MESH
WHOLE, VEC = range(2)
DP, MP = BOTH = ("dp", "mp")


def dot(a, b, ca, cb):
    return lax.dot_general(a, b, (((ca,), (cb,)), ((), ())), preferred_element_type=f32)


def shape(dims, kind=bf16):
    return jax.ShapeDtypeStruct(dims, kind)


def call(kernel, args, grid, in_specs, out_specs, outs, *, name, scalars=(), scratch=(), after=(), flops=0, moved=0, **extra):
    lead = len(scalars) + len(args)

    def body(*refs):
        kernel(*refs[:lead], *refs[lead + len(after) :])

    return pl.pallas_call(
        body,
        grid_spec=pltpu.PrefetchScalarGridSpec(
            num_scalar_prefetch=len(scalars),
            grid=grid,
            in_specs=[*in_specs, *[pl.BlockSpec(memory_space=pl.ANY)] * len(after)],
            out_specs=out_specs,
            scratch_shapes=list(scratch),
        ),
        out_shape=outs,
        compiler_params=pltpu.CompilerParams(vmem_limit_bytes=VMEM_LIMIT, **extra),
        cost_estimate=pl.CostEstimate(flops=flops, bytes_accessed=moved, transcendentals=0),
        name=name,
    )(*scalars, *args, *after)


def norm_parts(values):
    centred = values - jnp.mean(values, axis=-1, keepdims=True)
    spread = jnp.mean(centred * centred, axis=-1, keepdims=True)
    scale = lax.rsqrt(spread + epsilon)
    return centred * scale, scale


def norm_back(values, gain, grad):
    unit, scale = norm_parts(values)
    q = grad * gain
    back = scale * (
        q - jnp.mean(q, axis=-1, keepdims=True) - unit * jnp.mean(q * unit, axis=-1, keepdims=True)
    )
    return back, jnp.sum(grad * unit, axis=0, keepdims=True)


def total(values):
    out = values[0].astype(f32)
    for v in values[1:]:
        out = out + v.astype(f32)
    return out


def gelu_both(u):
    c = math.sqrt(2.0 / math.pi)
    square = u * u
    t = jnp.tanh(c * (u + 0.044715 * (u * square)))
    half = 0.5 * (1.0 + t)
    value = u * half
    slope = half + (0.5 * c) * u * (1.0 - t * t) * (1.0 + (3 * 0.044715) * square)
    return value, slope


def allowed_of(seg_col, seg_row, q0, k0, k1, rows):
    same = seg_col[q0 : q0 + rows, :] == seg_row[:, k0:k1]
    dims = (rows, k1 - k0)
    i = lax.broadcasted_iota(jnp.int32, dims, 0) + q0
    j = lax.broadcasted_iota(jnp.int32, dims, 1) + k0
    return same & (j <= i)


class Sent:
    def __init__(self, wire, slot, source, target, to):
        self.wire, self.slot, self.ends, self.to = wire, slot, (source, target), to

    def make(self):
        source, target = (e() if callable(e) else e for e in self.ends)
        return self.wire.copy(self.slot, source, target, self.to)

    def wait_recv(self):
        self.make().wait_recv()

    def wait_send(self):
        self.make().wait_send()


class Wire:
    def __init__(self, send, recv):
        self.send, self.recv, self.count, self.ends = send, recv, 0, []

    def slot(self):
        self.count += 1
        return self.count - 1

    def copy(self, slot, source, target, to):
        return pltpu.make_async_remote_copy(
            src_ref=source,
            dst_ref=target,
            send_sem=self.send.at[slot],
            recv_sem=self.recv.at[slot],
            device_id=to,
            device_id_type=MESH,
        )

    def go(self, source, target, to):
        copy = Sent(self, self.slot(), source, target, to)
        copy.make().start()
        self.ends.append(copy)
        return copy

    def sent(self, *copies):
        for copy in copies:
            copy.wait_send()
            self.ends = [c for c in self.ends if c is not copy]

    def finish(self):
        self.sent(*list(self.ends))


def stage(body, grid, ins, outs):
    pltpu.emit_pipeline(
        body,
        grid=grid,
        in_specs=[pl.BlockSpec(b, f) for _, b, f in ins],
        out_specs=[pl.BlockSpec(b, f) for _, b, f in outs],
    )(*[r for r, _, _ in ins], *[r for r, _, _ in outs])


def layer_kernel(dims, tree, *refs):
    half, width, columns, units, length = dims
    full = 2 * half
    rows = 4 * full
    r = named(jax.tree.unflatten(tree, refs))
    m, d = lax.axis_index(MP), lax.axis_index(DP)
    core, z = lax.rem(d, 2), d // 2
    parity = lax.rem(m, 2)
    to_x = {MP: m + 1 - 2 * parity}
    to_y = {MP: m + 2 - 4 * (m // 2)}
    to_core = {DP: d + 1 - 2 * core}
    wire = Wire(r.send, r.recv)
    heads = columns // HEAD_DIM
    score_scale = 1.0 / math.sqrt(HEAD_DIM)

    barrier = pltpu.get_barrier_semaphore()
    others = [{MP: lax.rem(m + i, 4)} for i in range(1, 4)] + [{DP: lax.rem(d + i, 8)} for i in range(1, 8)]
    for peer in others:
        pl.semaphore_signal(barrier, inc=1, device_id=peer, device_id_type=MESH)
    pl.semaphore_wait(barrier, len(others))

    def at(ref, block):
        return lambda: ref.at[pl.ds(block * half, half)]

    qkv_w = r.qkv_w
    loads = [
        pltpu.make_async_copy(w, qkv_w.at[:, pl.ds(i * columns, columns)], r.load.at[i])
        for i, w in enumerate((r.query_weight, r.key_weight, r.value_weight))
    ]
    for load in loads:
        load.start()

    tile = half // 2

    def row_ins(*values):
        out = []
        for v in values:
            ref, f = v if isinstance(v, tuple) else (v, lambda i: (i, 0))
            out.append((ref, (1 if ref.shape[0] == 1 else tile, width), (lambda i: (0, 0)) if ref.shape[0] == 1 else f))
        return out

    def row_wise(fn, ins, outs):
        n = len(ins)

        def body(*refs):
            for ref, value in zip(refs[n:], fn(*[x[...] for x in refs[:n]])):
                ref[...] = value.astype(ref.dtype)

        stage(body, (4,), row_ins(*ins), row_ins(*outs))

    def spread(ref):
        return {
            2: wire.go(at(ref, 0), at(ref, 2), to_x),
            5: wire.go(at(ref, 1), at(ref, 5), to_y),
            3: wire.go(at(ref, 1), at(ref, 3), to_x),
            4: wire.go(at(ref, 0), at(ref, 4), to_y),
        }

    def relay(ref):
        return {6: wire.go(at(ref, 2), at(ref, 6), to_y), 7: wire.go(at(ref, 5), at(ref, 7), to_x)}

    def send_far(into, terms):
        return [wire.go(at(terms, 6), at(into.far, 0), to_x), wire.go(at(terms, 7), at(into.far, 1), to_y)]

    def send_early(into, terms):
        return [wire.go(at(terms, 2), at(into.early, 0), to_x), wire.go(at(terms, 5), at(into.early, 1), to_y)]

    def send_late(into, terms, far, sums):
        for copy in far:
            copy.wait_recv()
        row_wise(
            lambda a, b: (a.astype(f32) + b.astype(f32),),
            [(terms, lambda i: (jnp.where(i < 2, 8 + i, 4 + i), 0)), into.far],
            [sums],
        )
        return [wire.go(at(sums, 0), at(into.late, 0), to_y), wire.go(at(sums, 1), at(into.late, 1), to_x)]

    def arrive(*copies):
        for copy in copies:
            copy.wait_recv()

    def product(source, target, blocks, weight, size, count, trans=False, scale=None):
        n = len(blocks)
        depth = source.shape[1]
        ref, ref_block, ref_map = weight if isinstance(weight, tuple) else (None, None, None)

        def body(*refs):
            j = pl.program_id(0)
            x = jnp.concatenate([b[...] for b in refs[:n]], axis=0) if n > 1 else refs[0][...]
            w = refs[n][...] if ref is not None else weight(j)
            acc = dot(x, w, 1, 1 if trans else 0)
            if scale is not None:
                acc = acc * scale(j)
            for i, out in enumerate(refs[-n:]):
                out[...] = acc[i * half : (i + 1) * half].astype(bf16)

        stage(
            body,
            (count,),
            [(source, (half, depth), lambda j, b=b: (b, 0)) for b in blocks]
            + ([(ref, ref_block, ref_map)] if ref is not None else []),
            [(target, (half, size), lambda j, b=b: (b, j)) for b in blocks],
        )

    def project(*blocks):
        product(
            r.attn_in,
            r.qkv,
            blocks,
            lambda j: qkv_w[:, pl.ds(pl.multiple_of(j * columns, columns), columns)],
            columns,
            3,
            scale=lambda j: jnp.where(j == 0, score_scale, 1.0),
        )

    def out_project(*blocks):
        product(
            r.context,
            r.out_terms,
            blocks,
            (r.out_weight, (columns, width // 2), lambda j: (0, j)),
            width // 2,
            2,
        )

    def context_back(*blocks):
        product(
            r.middle_all,
            r.context_grad,
            blocks,
            (r.out_weight, (columns // 2, width), lambda j: (j, 0)),
            columns // 2,
            2,
            trans=True,
        )

    def project_back(*blocks):
        size = width // 4
        product(
            r.qkv_grad,
            r.out_terms,
            blocks,
            lambda j: qkv_w[pl.ds(pl.multiple_of(j * size, size), size), :],
            size,
            4,
            trans=True,
        )

    def turn(block, target):
        for b in range(2):
            to = pl.multiple_of(lax.rem(parity + b, 2) * full, full)
            target[pl.ds(to, full), :] = block[b * full : (b + 1) * full, :]

    def turn_back(source, block):
        for b in range(2):
            come = pl.multiple_of(lax.rem(parity + b, 2) * full, full)
            block[b * full : (b + 1) * full, :] = source[pl.ds(come, full), :].astype(bf16)

    q, k, v, c = r.q, r.k, r.v, r.c
    f0, f1, f2 = r.f0, r.f1, r.f2

    def head_ins(s):
        ins = [
            (r.seg_col, (1, length, 1), lambda h: (lax.rem(m // 2 + s, 2), 0, 0)),
            (r.seg_row, (1, 1, length), lambda h: (lax.rem(m // 2 + s, 2), 0, 0)),
        ]
        for which in range(3):
            ins.append((r.qkv, (length, HEAD_DIM), lambda h, w=which: (s, w * heads + h)))
        return ins

    def scores_of(seg_col, seg_row, q0, k0, k1):
        s = dot(q[q0:k1, :], k[k0:k1, :], 1, 1)
        keep = allowed_of(seg_col.at[0], seg_row.at[0], q0, k0, k1, CLIP_MOST)
        s = jnp.where(keep, s, masked_score)
        e = jnp.exp(s - jnp.max(s, axis=-1, keepdims=True))
        return e * (1.0 / jnp.sum(e, axis=-1, keepdims=True))

    def attend(s):
        def body(seg_col, seg_row, q_in, k_in, v_in, out):
            turn(q_in, q)
            turn(k_in, k)
            turn(v_in, v)
            for q0 in range(0, length, CLIP_MOST):
                k0, k1 = max(0, q0 - CLIP_MOST), q0 + CLIP_MOST
                p = scores_of(seg_col, seg_row, q0, k0, k1).astype(bf16)
                f0[q0:k1, :] = dot(p, v[k0:k1, :], 1, 0)
            turn_back(f0, out)

        stage(body, (heads,), head_ins(s), [(r.context, (length, HEAD_DIM), lambda h: (s, h))])

    def attend_back(s):
        def body(seg_col, seg_row, q_in, k_in, v_in, c_in, dq_out, dk_out, dv_out):
            turn(q_in, q)
            turn(k_in, k)
            turn(v_in, v)
            turn(c_in, c)
            for q0 in range(0, length, CLIP_MOST):
                k0, k1 = max(0, q0 - CLIP_MOST), q0 + CLIP_MOST
                p = scores_of(seg_col, seg_row, q0, k0, k1)
                qb, cb, kb, vb = q[q0:k1, :], c[q0:k1, :], k[k0:k1, :], v[k0:k1, :]
                dp = dot(cb, vb, 1, 1)
                inner = jnp.sum(p * dp, axis=-1, keepdims=True)
                ds = (p * (dp - inner)).astype(bf16)
                f0[q0:k1, :] = dot(ds, kb, 1, 0) * score_scale
                dk, dv = dot(ds, qb, 0, 0), dot(p.astype(bf16), cb, 0, 0)
                if q0 > 0:
                    f1[k0:q0, :] += dk[:CLIP_MOST]
                    f2[k0:q0, :] += dv[:CLIP_MOST]
                    dk, dv = dk[CLIP_MOST:], dv[CLIP_MOST:]
                f1[q0:k1, :] = dk
                f2[q0:k1, :] = dv
            turn_back(f0, dq_out)
            turn_back(f1, dk_out)
            turn_back(f2, dv_out)

        stage(
            body,
            (heads,),
            [*head_ins(s), (r.context_grad, (length, HEAD_DIM), lambda h: (s, h))],
            [(r.qkv_grad, (length, HEAD_DIM), lambda h, w=w: (s, w * heads + h)) for w in range(3)],
        )

    acc_g, slopes = r.acc_g, r.slopes
    size = 512
    tiles = units // size
    up_tile = (r.up_weight, (width, size), lambda j: (0, j))
    down_tile = (r.down_weight, (size, width), lambda j: (j, 0))

    def whole(ref, both):
        return [(ref, (half, width), lambda j, i=i: (i, 0)) for i in both]

    def part(ref, both):
        return [(ref, (half, size), lambda j, i=i: (i, j)) for i in both]

    def rows_of(a, b):
        return jnp.concatenate([a[...], b[...]], axis=0)

    def grads_of(grad, up, p0, p1, g0, g1):
        j = pl.program_id(0)
        grad = grad.astype(bf16)
        p0[...], p1[...] = grad[:half], grad[half:]
        g = dot(grad, up[...], 1, 1)

        @pl.when(j == 0)
        def _():
            acc_g[...] = g

        @pl.when((j > 0) & (j < tiles - 1))
        def _():
            acc_g[...] += g

        @pl.when(j == tiles - 1)
        def _():
            last = acc_g[...] + g
            g0[...], g1[...] = last[:half].astype(bf16), last[half:].astype(bf16)

    def feed(*both):
        def body(x0, x1, c0, c1, up, down, h0, h1, *outs):
            value, slope = gelu_both(dot(rows_of(x0, x1), up[...], 1, 0))
            value = value.astype(bf16)
            h0[...], h1[...] = value[:half], value[half:]
            grads_of(dot(rows_of(c0, c1), down[...], 1, 1) * slope, up, *outs)

        stage(
            body,
            (tiles,),
            [*whole(r.mlp_in, both), *whole(r.cot_all, both), up_tile, down_tile],
            [*part(r.hidden, both), *part(r.pre_grad, both), *whole(r.mid_terms, both)],
        )

    def feed_forward(*both):
        def body(x0, x1, up, h0, h1):
            value, slope = gelu_both(dot(rows_of(x0, x1), up[...], 1, 0))
            value = value.astype(bf16)
            h0[...], h1[...] = value[:half], value[half:]
            slopes[pl.program_id(0)] = slope

        stage(body, (tiles,), [*whole(r.mlp_in, both), up_tile], part(r.hidden, both))

    def feed_back(*both):
        def body(c0, c1, up, down, *outs):
            grads_of(dot(rows_of(c0, c1), down[...], 1, 1) * slopes[pl.program_id(0)], up, *outs)

        stage(
            body,
            (tiles,),
            [*whole(r.cot_all, both), up_tile, down_tile],
            [*part(r.pre_grad, both), *whole(r.mid_terms, both)],
        )

    down_acc = r.down_acc
    share = width // 8

    def down_some(first, count, both, target=None, plus=None):
        begin = 0 in both
        n = len(both)

        def body(*refs):
            s = pl.program_id(0)
            left, right = ([b[...] for b in refs[i * n : (i + 1) * n]] for i in range(2))
            acc = dot(jnp.concatenate(left, axis=0), jnp.concatenate(right, axis=0), 0, 0)
            if not begin:
                acc = acc + down_acc[first + s]
            if target is None:
                down_acc[first + s] = acc
                return
            if plus is not None:
                acc = acc + refs[2 * n][0].astype(f32)
            refs[-1][0] = acc.astype(bf16)

        def column(s):
            k = first + s
            return 2 * lax.rem(k, 4) + jnp.where(k < 4, 1 - core, core)

        block = (1, share, units)
        stage(
            body,
            (count,),
            [(r.cot_all, (half, share), lambda s, i=i: (i, column(s))) for i in both]
            + [(r.hidden, (half, units), lambda s, i=i: (i, 0)) for i in both]
            + ([(plus, block, lambda s: (s, 0, 0))] if plus is not None else []),
            [(target, block, lambda s: (s, 0, 0))] if target is not None else [],
        )

    def grad_product(left, right, which, target, plus=None):
        def body(a, b, *rest):
            acc = dot(a[...], b[...], 0, 0)
            if plus is not None:
                acc = acc + rest[0][0].astype(f32)
            rest[-1][0] = acc.astype(bf16)

        n = right.shape[1]
        block = (1, share, n)
        place = lambda s: (s, 0, 0)
        stage(
            body,
            (4,),
            [
                (left, (rows, share), lambda s: (0, 2 * s + which)),
                (right, (rows, n), lambda s: (0, 0)),
                *([(plus, block, place)] if plus is not None else []),
            ],
            [(target, block, place)],
        )

    def grad_first(into, left, right):
        grad_product(left, right, 1 - core, into.mine)
        return wire.go(into.mine, into.got, to_core)

    def grad_second(into, left, right, swap):
        swap.wait_recv()
        wire.sent(swap)
        grad_product(left, right, core, into.mine, into.got)
        return start_line(into)

    def start_line(into):
        mine = into.mine
        n = mine.shape[2]
        part = share // 2
        ways = []
        for step, got, sums in ((1, into.right, into.right_sums), (-1, into.left, into.left_sums)):
            slots = [wire.slot() for _ in range(3)]
            to = {DP: jnp.clip(d + 2 * step, 0, 7)}
            place = z if step > 0 else 3 - z
            ways.append((step, place, got, sums, slots, to))

        def of(step, place):
            return jnp.clip(place if step > 0 else 3 - place, 0, 3)

        def copy(way, t, source):
            _, _, got, _, slots, to = way
            return wire.copy(slots[t], source, got.at[t], to)

        for way in ways:

            @pl.when(way[1] == 0)
            def _():
                for t in range(3):
                    copy(way, t, mine.at[of(way[0], 3 - t)]).start()

        def add(t, ways):
            for way in ways:
                copy(way, t, mine.at[0]).wait_recv()

            def body(*refs):
                for w in range(len(ways)):
                    a, b = refs[2 * w : 2 * w + 2]
                    refs[2 * len(ways) + w][...] = (a[0].astype(f32) + b[...].astype(f32)).astype(bf16)

            ins, outs = [], []
            for step, place, got, sums, _, _ in ways:
                ins.append((mine, (1, part, n), lambda i, s=step, p=place: (of(s, p + 2 - t), i, 0)))
                ins.append((got.at[t], (part, n), lambda i: (i, 0)))
                outs.append((sums.at[t], (part, n), lambda i: (i, 0)))
            stage(body, (2,), ins, outs)
            for way in ways:
                copy(way, t + 1, way[3].at[t]).start()

        def forward(t):
            if t == 1:
                pl.when((z == 1) | (z == 2))(lambda: add(1, ways))
                return
            for way in ways:
                pl.when(way[1] == 1)(lambda: add(0, [way]))

        def end(turned=None):
            for way in ways:
                place = way[1]

                @pl.when(place >= 1)
                def _():
                    copy(way, 2, mine.at[0]).wait_recv()

                for t in range(3):

                    @pl.when((place <= t) & (place < 3))
                    def _():
                        copy(way, t, mine.at[0]).wait_send()

            if turned is not None:
                share_total(into, turned)

        return forward, end

    def share_total(into, target):
        turned = target.shape[1] == share
        n = into.mine.shape[2]
        tile = 128

        def body(own, right, left, out):
            value = own[0].astype(f32)
            value = value + jnp.where(z > 0, right[0].astype(f32), 0.0)
            value = value + jnp.where(z < 3, left[0].astype(f32), 0.0)
            out[...] = value.T if turned else value

        block = (1, tile, n)
        stage(
            body,
            (share // tile,),
            [(into.mine, block, lambda i: (z, i, 0)), (into.right, block, lambda i: (2, i, 0)), (into.left, block, lambda i: (2, i, 0))],
            [(target, (n, tile), lambda i: (0, i)) if turned else (target, (tile, n), lambda i: (i, 0))],
        )

    def over_all(slots, value, me, axis, count):
        copies = [wire.go(value, slots.at[me], {axis: lax.rem(me + i, count)}) for i in range(1, count)]
        slots[pl.ds(me, 1)] = value[...][None]
        arrive(*copies)
        return functools.reduce(lambda a, i: a + slots[i], range(1, count), slots[0])

    attn_in, cot_all, mlp_in, middle_all = r.attn_in, r.cot_all, r.mlp_in, r.middle_all
    row_wise(
        lambda x, g: (norm_parts(x.astype(f32))[0] * g,), [r.tokens, r.attn_gain], [attn_in]
    )
    near = spread(attn_in)
    row_wise(lambda x: (x,), [r.out_cotangent], [cot_all])
    for load in loads:
        load.wait()
    project(0, 1)
    arrive(near[2], near[5])
    far = relay(attn_in)
    arrive(near[3], near[4])
    cot_near = {2: wire.go(at(cot_all, 0), at(cot_all, 2), to_x), 5: wire.go(at(cot_all, 1), at(cot_all, 5), to_y)}
    project(2, 3, 4, 5)

    @pl.loop(0, 2)
    def _(s):
        @pl.when(s == 1)
        def _():
            arrive(far[6], far[7])
            project(6, 7)

        attend(s)

    out_terms = r.out_terms
    out_project(6, 7)
    attn_far = send_far(r.attn, out_terms)
    out_project(2, 3, 4, 5)
    attn_early = send_early(r.attn, out_terms)
    out_project(0, 1)
    attn_late = send_late(r.attn, out_terms, attn_far, r.sums_a)
    cot_near[3] = wire.go(at(cot_all, 1), at(cot_all, 3), to_x)
    cot_near[4] = wire.go(at(cot_all, 0), at(cot_all, 4), to_y)
    arrive(*attn_early, *attn_late)

    def second(x, g, a, b, c_):
        mid = x.astype(f32) + a.astype(f32) + b.astype(f32) + c_.astype(f32)
        return mid, norm_parts(mid)[0] * g

    row_wise(
        second,
        [r.tokens, r.mlp_gain, out_terms, r.attn.early, r.attn.late],
        [r.residual_mid, mlp_in],
    )
    near = spread(mlp_in)
    arrive(cot_near[2], cot_near[5])
    mid_terms = r.mid_terms
    far, cot_far, mid_early = {}, {}, []

    @pl.loop(0, 3)
    def _(g):
        @pl.when(g == 1)
        def _():
            arrive(near[2], near[5])
            far.update(relay(mlp_in))
            cot_far.update(relay(cot_all))

        @pl.when(g == 2)
        def _():
            mid_early.extend(send_early(r.mid, mid_terms))
            down_some(0, 8, (0, 1, 2, 5))
            arrive(near[3], near[4], cot_near[3], cot_near[4])

        later = (g + 1) // 2
        feed(g + later, 1 - g + 5 * later)

    arrive(far[6], far[7])
    feed_forward(6, 7)
    arrive(cot_far[6], cot_far[7])
    down, last = r.down_grad, (3, 4, 6, 7)
    down_some(0, 4, last, down.mine)
    swap = wire.go(down.mine, down.got, to_core)
    feed_back(6, 7)
    mid_far = send_far(r.mid, mid_terms)
    arrive(swap)
    wire.sent(swap)
    down_some(4, 4, last, down.mine, down.got)
    down_forward, down_end = start_line(down)
    swap = grad_first(r.up_grad, mlp_in, r.pre_grad)
    mid_late = send_late(r.mid, mid_terms, mid_far, r.sums_b)
    mlp_terms = r.mlp_terms

    def down_project(*blocks):
        product(r.hidden, mlp_terms, blocks, (r.down_weight, (units, size), lambda j: (0, j)), size, width // size)

    down_project(6, 7, 2, 3)
    down_forward(0)
    arrive(*mid_early, *mid_late)
    gain_sum = r.gain_sum
    gain_sum[...] = jnp.zeros_like(gain_sum)

    def second_back(mid, g, cot, a, b, c_):
        back, gain = norm_back(mid, g, a.astype(f32) + b.astype(f32) + c_.astype(f32))
        gain_sum[1:2, :] += gain
        value = cot.astype(f32) + back
        return value, value

    row_wise(
        second_back,
        [r.residual_mid, r.mlp_gain, r.out_cotangent, mid_terms, r.mid.early, r.mid.late],
        [r.middle, middle_all],
    )
    near = spread(middle_all)

    up_forward, up_end = grad_second(r.up_grad, mlp_in, r.pre_grad, swap)
    arrive(near[2], near[5])
    far = relay(middle_all)
    mlp_far = send_far(r.attn, mlp_terms)
    down_forward(1)
    context_back(0, 1)
    down_project(4, 5, 0, 1)
    mlp_early = send_early(r.attn, mlp_terms)
    arrive(near[3], near[4])
    context_back(2, 3, 4, 5)

    @pl.loop(0, 2)
    def _(s):
        @pl.when(s == 1)
        def _():
            arrive(far[6], far[7])
            context_back(6, 7)
            up_forward(0)

        attend_back(s)

    wire.sent(*attn_far, *attn_early)
    swap = grad_first(r.qkv_w_grad, attn_in, r.qkv_grad)
    project_back(6, 7)
    back_far = send_far(r.mid, out_terms)
    qkv_forward, qkv_end = grad_second(r.qkv_w_grad, attn_in, r.qkv_grad, swap)
    project_back(2, 3, 4, 5)
    back_early = send_early(r.mid, out_terms)
    wire.sent(*mid_late)
    back_late = send_late(r.mid, out_terms, back_far, r.sums_b)
    up_forward(1)
    qkv_forward(0)
    swap = grad_first(r.out_grad, middle_all, r.context)
    wire.sent(*attn_late)
    mlp_late = send_late(r.attn, mlp_terms, mlp_far, r.sums_a)
    out_forward, out_end = grad_second(r.out_grad, middle_all, r.context, swap)
    project_back(0, 1)
    down_end(r.down_total)
    arrive(*back_early, *back_late)

    def first_back(x, mid, g, a, b, c_):
        back, gain = norm_back(x.astype(f32), g, a.astype(f32) + b.astype(f32) + c_.astype(f32))
        gain_sum[0:1, :] += gain
        return (mid + back,)

    row_wise(
        first_back,
        [r.tokens, r.middle, r.attn_gain, out_terms, r.mid.early, r.mid.late],
        [r.tokens_grad],
    )
    qkv_forward(1)
    out_forward(0)
    r.gain_near_sum[...] = over_all(r.gain_near, gain_sum, m, MP, 4)
    r.gains[...] = over_all(r.gain_far, r.gain_near_sum, d, DP, 8)
    up_end(r.up_total)
    out_forward(1)
    arrive(*mlp_early, *mlp_late)
    row_wise(
        lambda mid, *t: (mid + total(t),),
        [r.residual_mid, mlp_terms, r.attn.early, r.attn.late],
        [r.layer_output],
    )
    qkv_end()
    out_end(r.out_total)
    wire.finish()


def named(tree):
    return Names(**{k: named(v) for k, v in tree.items()}) if isinstance(tree, dict) else tree


def layer(ins, half, width, columns, units, length):
    full, rows = 2 * half, 8 * half
    share = width // 8
    big, own = shape((rows, width)), shape((full, width))
    arrivals = dict(far=own, early=own, late=own)

    def grad(n):
        line, sums = shape((3, share, n)), shape((2, share, n))
        stack = shape((4, share, n))
        return dict(mine=stack, got=stack, right=line, left=line, right_sums=sums, left_sums=sums)

    outs = dict(
        attn_in=big,
        cot_all=big,
        mlp_in=big,
        middle_all=big,
        out_terms=big,
        mlp_terms=big,
        mid_terms=big,
        hidden=shape((rows, units)),
        pre_grad=shape((rows, units)),
        qkv=shape((rows, 3 * columns)),
        qkv_grad=shape((rows, 3 * columns)),
        context=shape((rows, columns)),
        context_grad=shape((rows, columns)),
        attn=arrivals,
        mid=arrivals,
        sums_a=own,
        sums_b=own,
        down_grad=grad(units),
        up_grad=grad(units),
        qkv_w_grad=grad(3 * columns),
        out_grad=grad(columns),
        residual_mid=shape((full, width), f32),
        middle=shape((full, width), f32),
        layer_output=own,
        tokens_grad=shape((full, width), f32),
        down_total=shape((units, share), f32),
        up_total=shape((share, units), f32),
        out_total=shape((columns, share), f32),
    )
    any_, vmem = pl.BlockSpec(memory_space=pl.ANY), pl.BlockSpec(memory_space=pltpu.VMEM)
    places = dict(jax.tree.map(lambda _: any_, outs), gains=vmem)
    outs = dict(outs, gains=shape((2, width), f32))
    head, head_sum = pltpu.VMEM((length, HEAD_DIM), bf16), pltpu.VMEM((length, HEAD_DIM), f32)
    acc = pltpu.VMEM((full, width), f32)
    scratch = dict(
        qkv_w=pltpu.VMEM((width, 3 * columns), bf16),
        acc_g=acc,
        slopes=pltpu.VMEM((units // 512, full, 512), f32),
        down_acc=pltpu.VMEM((8, share, units), f32),
        gain_sum=pltpu.VMEM((2, width), f32),
        gain_near_sum=pltpu.VMEM((2, width), f32),
        gain_near=pltpu.VMEM((4, 2, width), f32),
        gain_far=pltpu.VMEM((8, 2, width), f32),
        q=head,
        k=head,
        v=head,
        c=head,
        f0=head_sum,
        f1=head_sum,
        f2=head_sum,
        send=pltpu.SemaphoreType.DMA((96,)),
        recv=pltpu.SemaphoreType.DMA((96,)),
        load=pltpu.SemaphoreType.DMA((3,)),
    )
    parts = [jax.tree.flatten(t) for t in (ins, outs, scratch)]
    kinds = [jax.tree.unflatten(t, range(len(v))) for v, t in parts]
    starts = (0, len(parts[0][0]), len(parts[0][0]) + len(parts[1][0]))
    place_of = {}
    for kind, begin in zip(kinds, starts):
        place_of.update(jax.tree.map(lambda i, b=begin: b + i, kind))
    order, tree = jax.tree.flatten(place_of)

    def kernel(*refs):
        layer_kernel((half, width, columns, units, length), tree, *[refs[i] for i in order])

    got = pl.pallas_call(
        kernel,
        in_specs=[any_] * len(parts[0][0]),
        out_specs=jax.tree.leaves(places),
        out_shape=parts[1][0],
        scratch_shapes=parts[2][0],
        compiler_params=pltpu.CompilerParams(
            collective_id=1, has_side_effects=True, vmem_limit_bytes=VMEM_LIMIT
        ),
        name="layer",
    )(*parts[0][0])
    return named(jax.tree.unflatten(parts[1][1], got))


def share_total(got, z, columns):
    mine, right, left = got.mine, got.right, got.left
    _, rows, width = mine.shape
    tile = 128

    def kernel(place, own, a, b, *outs):
        value = own[0].astype(f32)
        value = value + jnp.where(place[0] > 0, a[0].astype(f32), 0.0)
        value = value + jnp.where(place[0] < 3, b[0].astype(f32), 0.0)
        at = 0
        for out in outs:
            out[...] = value[:, at : at + out.shape[1]]
            at += out.shape[1]

    return call(
        kernel,
        [mine, right, left],
        (rows // tile,),
        [pl.BlockSpec((1, tile, width), lambda i, p: (p[0], i, 0))]
        + [pl.BlockSpec((1, tile, width), lambda i, p: (2, i, 0))] * 2,
        [pl.BlockSpec((tile, c), lambda i, p: (i, 0)) for c in columns],
        [shape((rows, c), f32) for c in columns],
        scalars=[z.astype(jnp.int32).reshape(1)],
        name="share_total",
        flops=rows * width,
        moved=rows * width * 10,
    )


def norm_rows(values, gain):
    centre = jnp.mean(values, axis=-1, keepdims=True)
    centred = values - centre
    spread = jnp.mean(centred * centred, axis=-1, keepdims=True)
    return centred * lax.rsqrt(spread + epsilon) * gain


def gelu_tanh(values):
    return jax.nn.gelu(values, approximate=True)


def block_allowed(segment):
    position = jnp.arange(segment.shape[0])
    return (position[None, :] <= position[:, None]) & (segment[:, None] == segment[None, :])


def rows_times(left_rows, right_matrix):
    return jnp.dot(left_rows, right_matrix, preferred_element_type=jnp.float32)


def rows_times_back(left_rows, right_matrix):
    return lax.dot_general(
        left_rows, right_matrix, (((1,), (1,)), ((), ())), preferred_element_type=jnp.float32
    )


def attn_input_back(
    queries_grad, keys_grad, values_grad, query_weight, key_weight, value_weight, score_scale
):
    total_grad = rows_times_back(queries_grad, query_weight) * score_scale
    total_grad = total_grad + rows_times_back(keys_grad, key_weight)
    return total_grad + rows_times_back(values_grad, value_weight)


def attend_forward(packed):
    queries, keys_in, values_in, segment = packed
    scores = jnp.einsum("qhd,khd->hqk", queries, keys_in, preferred_element_type=jnp.float32)
    scores = jnp.where(block_allowed(segment)[None], scores, masked_score)
    row_max = jnp.max(scores, axis=-1, keepdims=True)
    expanded = jnp.exp(scores - row_max)
    row_total = jnp.sum(expanded, axis=-1, keepdims=True)
    probs_low = (expanded / row_total).astype(jnp.bfloat16)
    context = jnp.einsum("hqk,khd->qhd", probs_low, values_in, preferred_element_type=jnp.float32)
    return (context.astype(jnp.bfloat16), (row_max + jnp.log(row_total))[:, :, 0])


def attend_backward(packed):
    queries, keys_in, values_in, segment, context_grad, log_total = packed
    scores = jnp.einsum("qhd,khd->hqk", queries, keys_in, preferred_element_type=jnp.float32)
    scores = jnp.where(block_allowed(segment)[None], scores, masked_score)
    attn_probs = jnp.exp(scores - log_total[:, :, None])
    probs_grad = jnp.einsum(
        "qhd,khd->hqk", context_grad, values_in, preferred_element_type=jnp.float32
    )
    values_grad = jnp.einsum(
        "hqk,qhd->khd",
        attn_probs.astype(jnp.bfloat16),
        context_grad,
        preferred_element_type=jnp.float32,
    )
    inner_sum = jnp.sum(attn_probs * probs_grad, axis=-1, keepdims=True)
    scores_grad = (attn_probs * (probs_grad - inner_sum)).astype(jnp.bfloat16)
    queries_grad = jnp.einsum(
        "hqk,khd->qhd", scores_grad, keys_in, preferred_element_type=jnp.float32
    )
    keys_grad = jnp.einsum("hqk,qhd->khd", scores_grad, queries, preferred_element_type=jnp.float32)
    return (
        queries_grad.astype(jnp.bfloat16),
        keys_grad.astype(jnp.bfloat16),
        values_grad.astype(jnp.bfloat16),
    )


def local_plain(
    tokens,
    segment_ids,
    query_weight,
    key_weight,
    value_weight,
    out_weight,
    up_weight,
    down_weight,
    attn_gain,
    mlp_gain,
    out_cotangent,
):
    seq_count, seq_length = segment_ids.shape
    group_rows = seq_count * seq_length
    head_count = query_weight.shape[1] // HEAD_DIM
    score_scale = 1.0 / math.sqrt(HEAD_DIM)
    shaped = (seq_count, seq_length, head_count, HEAD_DIM)
    flat_shape = (group_rows, head_count * HEAD_DIM)
    residual_in = tokens.astype(jnp.float32)
    normed_attn, attn_norm_back = jax.vjp(norm_rows, residual_in, attn_gain)
    gathered_attn = lax.all_gather(normed_attn.astype(jnp.bfloat16), MP, axis=0, tiled=True)
    queries = (
        jnp.dot(gathered_attn, query_weight, preferred_element_type=jnp.float32) * score_scale
    ).astype(jnp.bfloat16)
    keys_all = jnp.dot(gathered_attn, key_weight, preferred_element_type=jnp.float32).astype(
        jnp.bfloat16
    )
    values_all = jnp.dot(gathered_attn, value_weight, preferred_element_type=jnp.float32).astype(
        jnp.bfloat16
    )
    queries_seq = queries.reshape(shaped)
    keys_seq = keys_all.reshape(shaped)
    values_seq = values_all.reshape(shaped)
    context, log_total = lax.map(attend_forward, (queries_seq, keys_seq, values_seq, segment_ids))
    context_flat = context.reshape(flat_shape)
    attn_rows = lax.psum_scatter(
        rows_times(context_flat, out_weight).astype(jnp.bfloat16),
        MP,
        scatter_dimension=0,
        tiled=True,
    ).astype(jnp.float32)
    residual_mid = residual_in + attn_rows
    normed_mlp, mlp_norm_back = jax.vjp(norm_rows, residual_mid, mlp_gain)
    gathered_mlp = lax.all_gather(normed_mlp.astype(jnp.bfloat16), MP, axis=0, tiled=True)
    pre_act = jnp.dot(gathered_mlp, up_weight, preferred_element_type=jnp.float32)
    activated, gelu_back = jax.vjp(gelu_tanh, pre_act)
    hidden = activated.astype(jnp.bfloat16)
    mlp_rows = lax.psum_scatter(
        rows_times(hidden, down_weight).astype(jnp.bfloat16), MP, scatter_dimension=0, tiled=True
    ).astype(jnp.float32)
    layer_output = (residual_mid + mlp_rows).astype(jnp.bfloat16)
    cotangent_all = lax.all_gather(out_cotangent, MP, axis=0, tiled=True)
    down_weight_grad = jnp.einsum(
        "rf,rd->fd", hidden, cotangent_all, preferred_element_type=jnp.float32
    )
    hidden_grad = lax.dot_general(
        cotangent_all, down_weight, (((1,), (1,)), ((), ())), preferred_element_type=jnp.float32
    )
    pre_grad = gelu_back(hidden_grad)[0].astype(jnp.bfloat16)
    up_weight_grad = jnp.einsum(
        "rd,rf->df", gathered_mlp, pre_grad, preferred_element_type=jnp.float32
    )
    normed_mlp_grad = lax.psum_scatter(
        rows_times_back(pre_grad, up_weight).astype(jnp.bfloat16),
        MP,
        scatter_dimension=0,
        tiled=True,
    ).astype(jnp.float32)
    middle_back, mlp_gain_grad = mlp_norm_back(normed_mlp_grad)
    middle_grad = out_cotangent.astype(jnp.float32) + middle_back
    middle_all_grad = lax.all_gather(middle_grad.astype(jnp.bfloat16), MP, axis=0, tiled=True)
    out_weight_grad = jnp.einsum(
        "rc,rd->cd", context_flat, middle_all_grad, preferred_element_type=jnp.float32
    )
    context_grad = lax.dot_general(
        middle_all_grad, out_weight, (((1,), (1,)), ((), ())), preferred_element_type=jnp.float32
    ).astype(jnp.bfloat16)
    queries_grad, keys_grad, values_grad = lax.map(
        attend_backward,
        (queries_seq, keys_seq, values_seq, segment_ids, context_grad.reshape(shaped), log_total),
    )
    queries_grad = queries_grad.reshape(flat_shape)
    keys_grad = keys_grad.reshape(flat_shape)
    values_grad = values_grad.reshape(flat_shape)
    query_weight_grad = (
        jnp.einsum("rd,rc->dc", gathered_attn, queries_grad, preferred_element_type=jnp.float32)
        * score_scale
    )
    key_weight_grad = jnp.einsum(
        "rd,rc->dc", gathered_attn, keys_grad, preferred_element_type=jnp.float32
    )
    value_weight_grad = jnp.einsum(
        "rd,rc->dc", gathered_attn, values_grad, preferred_element_type=jnp.float32
    )
    normed_attn_grad = lax.psum_scatter(
        attn_input_back(
            queries_grad,
            keys_grad,
            values_grad,
            query_weight,
            key_weight,
            value_weight,
            score_scale,
        ).astype(jnp.bfloat16),
        MP,
        scatter_dimension=0,
        tiled=True,
    ).astype(jnp.float32)
    token_back, attn_gain_grad = attn_norm_back(normed_attn_grad)
    tokens_grad = middle_grad + token_back
    attn_gain_grad, mlp_gain_grad = lax.psum((attn_gain_grad, mlp_gain_grad), (DP, MP))
    (
        query_weight_grad,
        key_weight_grad,
        value_weight_grad,
        out_weight_grad,
        up_weight_grad,
        down_weight_grad,
    ) = (
        lax.psum_scatter(
            query_weight_grad.astype(jnp.bfloat16), DP, scatter_dimension=0, tiled=True
        ).astype(jnp.float32),
        lax.psum_scatter(
            key_weight_grad.astype(jnp.bfloat16), DP, scatter_dimension=0, tiled=True
        ).astype(jnp.float32),
        lax.psum_scatter(
            value_weight_grad.astype(jnp.bfloat16), DP, scatter_dimension=0, tiled=True
        ).astype(jnp.float32),
        lax.psum_scatter(
            out_weight_grad.astype(jnp.bfloat16), DP, scatter_dimension=1, tiled=True
        ).astype(jnp.float32),
        lax.psum_scatter(
            up_weight_grad.astype(jnp.bfloat16), DP, scatter_dimension=0, tiled=True
        ).astype(jnp.float32),
        lax.psum_scatter(
            down_weight_grad.astype(jnp.bfloat16), DP, scatter_dimension=1, tiled=True
        ).astype(jnp.float32),
    )
    return (
        layer_output,
        tokens_grad,
        query_weight_grad,
        key_weight_grad,
        value_weight_grad,
        out_weight_grad,
        up_weight_grad,
        down_weight_grad,
        attn_gain_grad,
        mlp_gain_grad,
    )


def local(
    mp,
    dp,
    tokens,
    segment_ids,
    query_weight,
    key_weight,
    value_weight,
    out_weight,
    up_weight,
    down_weight,
    attn_gain,
    mlp_gain,
    out_cotangent,
):
    width, columns = query_weight.shape
    length = segment_ids.shape[1]
    half = tokens.shape[0] // 2
    z = lax.axis_index(DP) // 2
    attn_gain, mlp_gain = attn_gain.reshape(1, width), mlp_gain.reshape(1, width)
    got = layer(
        dict(
            tokens=tokens,
            seg_col=segment_ids.reshape(2, length, 1),
            seg_row=segment_ids.reshape(2, 1, length),
            query_weight=query_weight,
            key_weight=key_weight,
            value_weight=value_weight,
            out_weight=out_weight,
            up_weight=up_weight,
            down_weight=down_weight,
            attn_gain=attn_gain,
            mlp_gain=mlp_gain,
            out_cotangent=out_cotangent,
        ),
        half,
        width,
        columns,
        up_weight.shape[1],
        length,
    )

    qkv_grads = share_total(got.qkv_w_grad, z, [columns] * 3)
    return (
        got.layer_output,
        got.tokens_grad,
        *qkv_grads,
        got.out_total,
        got.up_total,
        got.down_total,
        got.gains[0],
        got.gains[1],
    )


def solution(mesh):
    mp, dp = mesh.shape[MP], mesh.shape[DP]
    return jax.shard_map(
        functools.partial(local, mp, dp) if (mp, dp) == (4, 8) else local_plain,
        mesh=mesh,
        in_specs=(
            P(BOTH, None),
            P(DP, None),
            P(None, MP),
            P(None, MP),
            P(None, MP),
            P(MP, None),
            P(None, MP),
            P(MP, None),
            P(),
            P(),
            P(BOTH, None),
        ),
        out_specs=(
            P(BOTH, None),
            P(BOTH, None),
            P(DP, MP),
            P(DP, MP),
            P(DP, MP),
            P(MP, DP),
            P(DP, MP),
            P(MP, DP),
            P(),
            P(),
        ),
        check_vma=False,
    )
```

```python
import functools
import math
from types import SimpleNamespace as Names

import jax
import jax.numpy as jnp
from jax import lax
from jax.experimental import pallas as pl
from jax.experimental.pallas import tpu as pltpu
from jax.sharding import PartitionSpec as P

HEAD_DIM = 128
CLIP_MOST = 256
epsilon = 1e-05
masked_score = -1e30
bf16, f32 = jnp.bfloat16, jnp.float32
VMEM_LIMIT = 60 * 1024 * 1024
MESH = pl.DeviceIdType.MESH
WHOLE, VEC = range(2)
DP, MP = BOTH = ("dp", "mp")


def dot(a, b, ca, cb):
    return lax.dot_general(a, b, (((ca,), (cb,)), ((), ())), preferred_element_type=f32)


def shape(dims, kind=bf16):
    return jax.ShapeDtypeStruct(dims, kind)


def call(kernel, args, grid, in_specs, out_specs, outs, *, name, scalars=(), scratch=(), after=(), flops=0, moved=0, **extra):
    lead = len(scalars) + len(args)

    def body(*refs):
        kernel(*refs[:lead], *refs[lead + len(after) :])

    return pl.pallas_call(
        body,
        grid_spec=pltpu.PrefetchScalarGridSpec(
            num_scalar_prefetch=len(scalars),
            grid=grid,
            in_specs=[*in_specs, *[pl.BlockSpec(memory_space=pl.ANY)] * len(after)],
            out_specs=out_specs,
            scratch_shapes=list(scratch),
        ),
        out_shape=outs,
        compiler_params=pltpu.CompilerParams(vmem_limit_bytes=VMEM_LIMIT, **extra),
        cost_estimate=pl.CostEstimate(flops=flops, bytes_accessed=moved, transcendentals=0),
        name=name,
    )(*scalars, *args, *after)


def norm_parts(values):
    centred = values - jnp.mean(values, axis=-1, keepdims=True)
    spread = jnp.mean(centred * centred, axis=-1, keepdims=True)
    scale = lax.rsqrt(spread + epsilon)
    return centred * scale, scale


def norm_back(values, gain, grad):
    unit, scale = norm_parts(values)
    q = grad * gain
    back = scale * (
        q - jnp.mean(q, axis=-1, keepdims=True) - unit * jnp.mean(q * unit, axis=-1, keepdims=True)
    )
    return back, jnp.sum(grad * unit, axis=0, keepdims=True)


def total(values):
    out = values[0].astype(f32)
    for v in values[1:]:
        out = out + v.astype(f32)
    return out


def gelu_both(u):
    c = math.sqrt(2.0 / math.pi)
    square = u * u
    t = jnp.tanh(c * (u + 0.044715 * (u * square)))
    half = 0.5 * (1.0 + t)
    value = u * half
    slope = half + (0.5 * c) * u * (1.0 - t * t) * (1.0 + (3 * 0.044715) * square)
    return value, slope


def allowed_of(seg_col, seg_row, q0, k0, k1, rows):
    same = seg_col[q0 : q0 + rows, :] == seg_row[:, k0:k1]
    dims = (rows, k1 - k0)
    i = lax.broadcasted_iota(jnp.int32, dims, 0) + q0
    j = lax.broadcasted_iota(jnp.int32, dims, 1) + k0
    return same & (j <= i)


class Sent:
    def __init__(self, wire, slot, source, target, to):
        self.wire, self.slot, self.ends, self.to = wire, slot, (source, target), to

    def make(self):
        source, target = (e() if callable(e) else e for e in self.ends)
        return self.wire.copy(self.slot, source, target, self.to)

    def wait_recv(self):
        self.make().wait_recv()

    def wait_send(self):
        self.make().wait_send()


class Wire:
    def __init__(self, send, recv):
        self.send, self.recv, self.count, self.ends = send, recv, 0, []

    def slot(self):
        self.count += 1
        return self.count - 1

    def copy(self, slot, source, target, to):
        return pltpu.make_async_remote_copy(
            src_ref=source,
            dst_ref=target,
            send_sem=self.send.at[slot],
            recv_sem=self.recv.at[slot],
            device_id=to,
            device_id_type=MESH,
        )

    def go(self, source, target, to):
        copy = Sent(self, self.slot(), source, target, to)
        copy.make().start()
        self.ends.append(copy)
        return copy

    def sent(self, *copies):
        for copy in copies:
            copy.wait_send()
            self.ends = [c for c in self.ends if c is not copy]

    def finish(self):
        self.sent(*list(self.ends))


def stage(body, grid, ins, outs):
    pltpu.emit_pipeline(
        body,
        grid=grid,
        in_specs=[pl.BlockSpec(b, f) for _, b, f in ins],
        out_specs=[pl.BlockSpec(b, f) for _, b, f in outs],
    )(*[r for r, _, _ in ins], *[r for r, _, _ in outs])


def layer_kernel(dims, tree, *refs):
    half, width, columns, units, length = dims
    full = 2 * half
    rows = 4 * full
    r = named(jax.tree.unflatten(tree, refs))
    m, d = lax.axis_index(MP), lax.axis_index(DP)
    core, z = lax.rem(d, 2), d // 2
    parity = lax.rem(m, 2)
    to_x = {MP: m + 1 - 2 * parity}
    to_y = {MP: m + 2 - 4 * (m // 2)}
    to_core = {DP: d + 1 - 2 * core}
    wire = Wire(r.send, r.recv)
    heads = columns // HEAD_DIM
    score_scale = 1.0 / math.sqrt(HEAD_DIM)

    barrier = pltpu.get_barrier_semaphore()
    others = [{MP: lax.rem(m + i, 4)} for i in range(1, 4)] + [{DP: lax.rem(d + i, 8)} for i in range(1, 8)]
    for peer in others:
        pl.semaphore_signal(barrier, inc=1, device_id=peer, device_id_type=MESH)
    pl.semaphore_wait(barrier, len(others))

    def at(ref, block):
        return lambda: ref.at[pl.ds(block * half, half)]

    qkv_w = r.qkv_w
    loads = [
        pltpu.make_async_copy(w, qkv_w.at[:, pl.ds(i * columns, columns)], r.load.at[i])
        for i, w in enumerate((r.query_weight, r.key_weight, r.value_weight))
    ]
    for load in loads:
        load.start()

    tile = half // 2

    def row_ins(*values):
        out = []
        for v in values:
            ref, f = v if isinstance(v, tuple) else (v, lambda i: (i, 0))
            out.append((ref, (1 if ref.shape[0] == 1 else tile, width), (lambda i: (0, 0)) if ref.shape[0] == 1 else f))
        return out

    def row_wise(fn, ins, outs):
        n = len(ins)

        def body(*refs):
            for ref, value in zip(refs[n:], fn(*[x[...] for x in refs[:n]])):
                ref[...] = value.astype(ref.dtype)

        stage(body, (4,), row_ins(*ins), row_ins(*outs))

    def spread(ref):
        return {
            2: wire.go(at(ref, 0), at(ref, 2), to_x),
            5: wire.go(at(ref, 1), at(ref, 5), to_y),
            3: wire.go(at(ref, 1), at(ref, 3), to_x),
            4: wire.go(at(ref, 0), at(ref, 4), to_y),
        }

    def relay(ref):
        return {6: wire.go(at(ref, 2), at(ref, 6), to_y), 7: wire.go(at(ref, 5), at(ref, 7), to_x)}

    def send_far(into, terms):
        return [wire.go(at(terms, 6), at(into.far, 0), to_x), wire.go(at(terms, 7), at(into.far, 1), to_y)]

    def send_early(into, terms):
        return [wire.go(at(terms, 2), at(into.early, 0), to_x), wire.go(at(terms, 5), at(into.early, 1), to_y)]

    def send_late(into, terms, far, sums):
        for copy in far:
            copy.wait_recv()
        row_wise(
            lambda a, b: (a.astype(f32) + b.astype(f32),),
            [(terms, lambda i: (jnp.where(i < 2, 8 + i, 4 + i), 0)), into.far],
            [sums],
        )
        return [wire.go(at(sums, 0), at(into.late, 0), to_y), wire.go(at(sums, 1), at(into.late, 1), to_x)]

    def arrive(*copies):
        for copy in copies:
            copy.wait_recv()

    def product(source, target, blocks, weight, size, count, trans=False, scale=None):
        n = len(blocks)
        depth = source.shape[1]
        ref, ref_block, ref_map = weight if isinstance(weight, tuple) else (None, None, None)

        def body(*refs):
            j = pl.program_id(0)
            x = jnp.concatenate([b[...] for b in refs[:n]], axis=0) if n > 1 else refs[0][...]
            w = refs[n][...] if ref is not None else weight(j)
            acc = dot(x, w, 1, 1 if trans else 0)
            if scale is not None:
                acc = acc * scale(j)
            for i, out in enumerate(refs[-n:]):
                out[...] = acc[i * half : (i + 1) * half].astype(bf16)

        stage(
            body,
            (count,),
            [(source, (half, depth), lambda j, b=b: (b, 0)) for b in blocks]
            + ([(ref, ref_block, ref_map)] if ref is not None else []),
            [(target, (half, size), lambda j, b=b: (b, j)) for b in blocks],
        )

    def project(*blocks):
        product(
            r.attn_in,
            r.qkv,
            blocks,
            lambda j: qkv_w[:, pl.ds(pl.multiple_of(j * columns, columns), columns)],
            columns,
            3,
            scale=lambda j: jnp.where(j == 0, score_scale, 1.0),
        )

    def out_project(*blocks):
        product(
            r.context,
            r.out_terms,
            blocks,
            (r.out_weight, (columns, width // 2), lambda j: (0, j)),
            width // 2,
            2,
        )

    def context_back(*blocks):
        product(
            r.middle_all,
            r.context_grad,
            blocks,
            (r.out_weight, (columns // 2, width), lambda j: (j, 0)),
            columns // 2,
            2,
            trans=True,
        )

    def project_back(*blocks):
        size = width // 4
        product(
            r.qkv_grad,
            r.out_terms,
            blocks,
            lambda j: qkv_w[pl.ds(pl.multiple_of(j * size, size), size), :],
            size,
            4,
            trans=True,
        )

    def turn(block, target):
        for b in range(2):
            to = pl.multiple_of(lax.rem(parity + b, 2) * full, full)
            target[pl.ds(to, full), :] = block[b * full : (b + 1) * full, :]

    def turn_back(source, block):
        for b in range(2):
            come = pl.multiple_of(lax.rem(parity + b, 2) * full, full)
            block[b * full : (b + 1) * full, :] = source[pl.ds(come, full), :].astype(bf16)

    q, k, v, c = r.q, r.k, r.v, r.c
    f0, f1, f2 = r.f0, r.f1, r.f2

    def head_ins(s):
        ins = []
        for which in range(3):
            ins.append((r.qkv, (length, HEAD_DIM), lambda h, w=which: (s, w * heads + h)))
        return ins

    def scores_of(s, q0, k0, k1):
        which = lax.rem(m // 2 + s, 2)
        scores = dot(q[q0:k1, :], k[k0:k1, :], 1, 1)
        keep = allowed_of(r.seg_cols.at[which], r.seg_rows.at[which], q0, k0, k1, CLIP_MOST)
        scores = jnp.where(keep, scores, masked_score)
        e = jnp.exp(scores - jnp.max(scores, axis=-1, keepdims=True))
        return e * (1.0 / jnp.sum(e, axis=-1, keepdims=True))

    def attend(s):
        def body(q_in, k_in, v_in, out):
            turn(q_in, q)
            turn(k_in, k)
            turn(v_in, v)
            for q0 in range(0, length, CLIP_MOST):
                k0, k1 = max(0, q0 - CLIP_MOST), q0 + CLIP_MOST
                p = scores_of(s, q0, k0, k1).astype(bf16)
                f0[q0:k1, :] = dot(p, v[k0:k1, :], 1, 0)
            turn_back(f0, out)

        stage(body, (heads,), head_ins(s), [(r.context, (length, HEAD_DIM), lambda h: (s, h))])

    def attend_back(s):
        def body(q_in, k_in, v_in, c_in, dq_out, dk_out, dv_out):
            turn(q_in, q)
            turn(k_in, k)
            turn(v_in, v)
            turn(c_in, c)
            for q0 in range(0, length, CLIP_MOST):
                k0, k1 = max(0, q0 - CLIP_MOST), q0 + CLIP_MOST
                p = scores_of(s, q0, k0, k1)
                qb, cb, kb, vb = q[q0:k1, :], c[q0:k1, :], k[k0:k1, :], v[k0:k1, :]
                dp = dot(cb, vb, 1, 1)
                inner = jnp.sum(p * dp, axis=-1, keepdims=True)
                ds = (p * (dp - inner)).astype(bf16)
                f0[q0:k1, :] = dot(ds, kb, 1, 0) * score_scale
                dk, dv = dot(ds, qb, 0, 0), dot(p.astype(bf16), cb, 0, 0)
                if q0 > 0:
                    f1[k0:q0, :] += dk[:CLIP_MOST]
                    f2[k0:q0, :] += dv[:CLIP_MOST]
                    dk, dv = dk[CLIP_MOST:], dv[CLIP_MOST:]
                f1[q0:k1, :] = dk
                f2[q0:k1, :] = dv
            turn_back(f0, dq_out)
            turn_back(f1, dk_out)
            turn_back(f2, dv_out)

        stage(
            body,
            (heads,),
            [*head_ins(s), (r.context_grad, (length, HEAD_DIM), lambda h: (s, h))],
            [(r.qkv_grad, (length, HEAD_DIM), lambda h, w=w: (s, w * heads + h)) for w in range(3)],
        )

    acc_g, slopes = r.acc_g, r.slopes
    size = 512
    tiles = units // size
    up_tile = (r.up_weight, (width, size), lambda j: (0, j))
    down_tile = (r.down_weight, (size, width), lambda j: (j, 0))

    def whole(ref, both):
        return [(ref, (half, width), lambda j, i=i: (i, 0)) for i in both]

    def part(ref, both):
        return [(ref, (half, size), lambda j, i=i: (i, j)) for i in both]

    def rows_of(a, b):
        return jnp.concatenate([a[...], b[...]], axis=0)

    def grads_of(grad, up, p0, p1, g0, g1):
        j = pl.program_id(0)
        grad = grad.astype(bf16)
        p0[...], p1[...] = grad[:half], grad[half:]
        g = dot(grad, up[...], 1, 1)

        @pl.when(j == 0)
        def _():
            acc_g[...] = g

        @pl.when((j > 0) & (j < tiles - 1))
        def _():
            acc_g[...] += g

        @pl.when(j == tiles - 1)
        def _():
            last = acc_g[...] + g
            g0[...], g1[...] = last[:half].astype(bf16), last[half:].astype(bf16)

    def feed(*both):
        def body(x0, x1, c0, c1, up, down, h0, h1, *outs):
            value, slope = gelu_both(dot(rows_of(x0, x1), up[...], 1, 0))
            value = value.astype(bf16)
            h0[...], h1[...] = value[:half], value[half:]
            grads_of(dot(rows_of(c0, c1), down[...], 1, 1) * slope, up, *outs)

        stage(
            body,
            (tiles,),
            [*whole(r.mlp_in, both), *whole(r.cot_all, both), up_tile, down_tile],
            [*part(r.hidden, both), *part(r.pre_grad, both), *whole(r.mid_terms, both)],
        )

    def feed_forward(*both):
        def body(x0, x1, up, h0, h1):
            value, slope = gelu_both(dot(rows_of(x0, x1), up[...], 1, 0))
            value = value.astype(bf16)
            h0[...], h1[...] = value[:half], value[half:]
            slopes[pl.program_id(0)] = slope

        stage(body, (tiles,), [*whole(r.mlp_in, both), up_tile], part(r.hidden, both))

    def feed_back(*both):
        def body(c0, c1, up, down, *outs):
            grads_of(dot(rows_of(c0, c1), down[...], 1, 1) * slopes[pl.program_id(0)], up, *outs)

        stage(
            body,
            (tiles,),
            [*whole(r.cot_all, both), up_tile, down_tile],
            [*part(r.pre_grad, both), *whole(r.mid_terms, both)],
        )

    down_acc = r.down_acc
    share = width // 8

    def down_some(first, count, both, target=None, plus=None):
        begin = 0 in both
        n = len(both)

        def body(*refs):
            s = pl.program_id(0)
            left, right = ([b[...] for b in refs[i * n : (i + 1) * n]] for i in range(2))
            acc = dot(jnp.concatenate(left, axis=0), jnp.concatenate(right, axis=0), 0, 0)
            if not begin:
                acc = acc + down_acc[first + s]
            if target is None:
                down_acc[first + s] = acc
                return
            if plus is not None:
                acc = acc + refs[2 * n][0].astype(f32)
            refs[-1][0] = acc.astype(bf16)

        def column(s):
            k = first + s
            return 2 * lax.rem(k, 4) + jnp.where(k < 4, 1 - core, core)

        block = (1, share, units)
        stage(
            body,
            (count,),
            [(r.cot_all, (half, share), lambda s, i=i: (i, column(s))) for i in both]
            + [(r.hidden, (half, units), lambda s, i=i: (i, 0)) for i in both]
            + ([(plus, block, lambda s: (s, 0, 0))] if plus is not None else []),
            [(target, block, lambda s: (s, 0, 0))] if target is not None else [],
        )

    def grad_product(left, right, which, target, plus=None):
        def body(a, b, *rest):
            acc = dot(a[...], b[...], 0, 0)
            if plus is not None:
                acc = acc + rest[0][0].astype(f32)
            rest[-1][0] = acc.astype(bf16)

        n = right.shape[1]
        block = (1, share, n)
        place = lambda s: (s, 0, 0)
        stage(
            body,
            (4,),
            [
                (left, (rows, share), lambda s: (0, 2 * s + which)),
                (right, (rows, n), lambda s: (0, 0)),
                *([(plus, block, place)] if plus is not None else []),
            ],
            [(target, block, place)],
        )

    def grad_first(into, left, right):
        grad_product(left, right, 1 - core, into.mine)
        return wire.go(into.mine, into.got, to_core)

    def grad_second(into, left, right, swap):
        swap.wait_recv()
        wire.sent(swap)
        grad_product(left, right, core, into.mine, into.got)
        return start_line(into)

    def start_line(into):
        mine = into.mine
        n = mine.shape[2]
        part = share // 2
        ways = []
        for step, got, sums in ((1, into.right, into.right_sums), (-1, into.left, into.left_sums)):
            slots = [wire.slot() for _ in range(3)]
            to = {DP: jnp.clip(d + 2 * step, 0, 7)}
            place = z if step > 0 else 3 - z
            ways.append((step, place, got, sums, slots, to))

        def of(step, place):
            return jnp.clip(place if step > 0 else 3 - place, 0, 3)

        def copy(way, t, source):
            _, _, got, _, slots, to = way
            return wire.copy(slots[t], source, got.at[t], to)

        for way in ways:

            @pl.when(way[1] == 0)
            def _():
                for t in range(3):
                    copy(way, t, mine.at[of(way[0], 3 - t)]).start()

        def add(t, ways):
            for way in ways:
                copy(way, t, mine.at[0]).wait_recv()

            def body(*refs):
                for w in range(len(ways)):
                    a, b = refs[2 * w : 2 * w + 2]
                    refs[2 * len(ways) + w][...] = (a[0].astype(f32) + b[...].astype(f32)).astype(bf16)

            ins, outs = [], []
            for step, place, got, sums, _, _ in ways:
                ins.append((mine, (1, part, n), lambda i, s=step, p=place: (of(s, p + 2 - t), i, 0)))
                ins.append((got.at[t], (part, n), lambda i: (i, 0)))
                outs.append((sums.at[t], (part, n), lambda i: (i, 0)))
            stage(body, (2,), ins, outs)
            for way in ways:
                copy(way, t + 1, way[3].at[t]).start()

        def forward(t):
            if t == 1:
                pl.when((z == 1) | (z == 2))(lambda: add(1, ways))
                return
            for way in ways:
                pl.when(way[1] == 1)(lambda: add(0, [way]))

        def end(turned=None):
            for way in ways:
                place = way[1]

                @pl.when(place >= 1)
                def _():
                    copy(way, 2, mine.at[0]).wait_recv()

                for t in range(3):

                    @pl.when((place <= t) & (place < 3))
                    def _():
                        copy(way, t, mine.at[0]).wait_send()

            if turned is not None:
                share_total(into, turned)

        return forward, end

    def share_total(into, target):
        turned = target.shape[1] == share
        n = into.mine.shape[2]
        tile = 128

        def body(own, right, left, out):
            value = own[0].astype(f32)
            value = value + jnp.where(z > 0, right[0].astype(f32), 0.0)
            value = value + jnp.where(z < 3, left[0].astype(f32), 0.0)
            out[...] = value.T if turned else value

        block = (1, tile, n)
        stage(
            body,
            (share // tile,),
            [(into.mine, block, lambda i: (z, i, 0)), (into.right, block, lambda i: (2, i, 0)), (into.left, block, lambda i: (2, i, 0))],
            [(target, (n, tile), lambda i: (0, i)) if turned else (target, (tile, n), lambda i: (i, 0))],
        )

    def over_all(slots, value, me, axis, count):
        copies = [wire.go(value, slots.at[me], {axis: lax.rem(me + i, count)}) for i in range(1, count)]
        slots[pl.ds(me, 1)] = value[...][None]
        arrive(*copies)
        return functools.reduce(lambda a, i: a + slots[i], range(1, count), slots[0])

    attn_in, cot_all, mlp_in, middle_all = r.attn_in, r.cot_all, r.mlp_in, r.middle_all
    row_wise(
        lambda x, g: (norm_parts(x.astype(f32))[0] * g,), [r.tokens, r.attn_gain], [attn_in]
    )
    near = spread(attn_in)
    row_wise(lambda x: (x,), [r.out_cotangent], [cot_all])

    def segments(ids):
        same = lax.broadcasted_iota(jnp.int32, (128, 128), 0) == lax.broadcasted_iota(jnp.int32, (128, 128), 1)
        for i in range(2):
            for at_ in range(0, length, 128):
                row = ids[i : i + 1, at_ : at_ + 128].astype(f32)
                r.seg_rows[i, :, at_ : at_ + 128] = row
                r.seg_cols[i, at_ : at_ + 128, :] = jnp.sum(jnp.where(same, row, 0.0), axis=1, keepdims=True)

    stage(segments, (1,), [(r.segment_ids, (2, length), lambda i: (0, 0))], [])
    for load in loads:
        load.wait()
    project(0, 1)
    arrive(near[2], near[5])
    far = relay(attn_in)
    arrive(near[3], near[4])
    cot_near = {2: wire.go(at(cot_all, 0), at(cot_all, 2), to_x), 5: wire.go(at(cot_all, 1), at(cot_all, 5), to_y)}
    project(2, 3, 4, 5)

    @pl.loop(0, 2)
    def _(s):
        @pl.when(s == 1)
        def _():
            arrive(far[6], far[7])
            project(6, 7)

        attend(s)

    out_terms = r.out_terms
    out_project(6, 7)
    attn_far = send_far(r.attn, out_terms)
    out_project(2, 3, 4, 5)
    attn_early = send_early(r.attn, out_terms)
    out_project(0, 1)
    attn_late = send_late(r.attn, out_terms, attn_far, r.sums_a)
    cot_near[3] = wire.go(at(cot_all, 1), at(cot_all, 3), to_x)
    cot_near[4] = wire.go(at(cot_all, 0), at(cot_all, 4), to_y)
    arrive(*attn_early, *attn_late)

    def second(x, g, a, b, c_):
        mid = x.astype(f32) + a.astype(f32) + b.astype(f32) + c_.astype(f32)
        return mid, norm_parts(mid)[0] * g

    row_wise(
        second,
        [r.tokens, r.mlp_gain, out_terms, r.attn.early, r.attn.late],
        [r.residual_mid, mlp_in],
    )
    near = spread(mlp_in)
    arrive(cot_near[2], cot_near[5])
    mid_terms = r.mid_terms
    far, cot_far, mid_early = {}, {}, []

    @pl.loop(0, 3)
    def _(g):
        @pl.when(g == 1)
        def _():
            arrive(near[2], near[5])
            far.update(relay(mlp_in))
            cot_far.update(relay(cot_all))

        @pl.when(g == 2)
        def _():
            mid_early.extend(send_early(r.mid, mid_terms))
            down_some(0, 8, (0, 1, 2, 5))
            arrive(near[3], near[4], cot_near[3], cot_near[4])

        later = (g + 1) // 2
        feed(g + later, 1 - g + 5 * later)

    arrive(far[6], far[7])
    feed_forward(6, 7)
    arrive(cot_far[6], cot_far[7])
    down, last = r.down_grad, (3, 4, 6, 7)
    down_some(0, 4, last, down.mine)
    swap = wire.go(down.mine, down.got, to_core)
    feed_back(6, 7)
    mid_far = send_far(r.mid, mid_terms)
    arrive(swap)
    wire.sent(swap)
    down_some(4, 4, last, down.mine, down.got)
    down_forward, down_end = start_line(down)
    swap = grad_first(r.up_grad, mlp_in, r.pre_grad)
    mid_late = send_late(r.mid, mid_terms, mid_far, r.sums_b)
    mlp_terms = r.mlp_terms

    def down_project(*blocks):
        product(r.hidden, mlp_terms, blocks, (r.down_weight, (units, size), lambda j: (0, j)), size, width // size)

    down_project(6, 7, 2, 3)
    down_forward(0)
    arrive(*mid_early, *mid_late)
    gain_sum = r.gain_sum
    gain_sum[...] = jnp.zeros_like(gain_sum)

    def second_back(mid, g, cot, a, b, c_):
        back, gain = norm_back(mid, g, a.astype(f32) + b.astype(f32) + c_.astype(f32))
        gain_sum[1:2, :] += gain
        value = cot.astype(f32) + back
        return value, value

    row_wise(
        second_back,
        [r.residual_mid, r.mlp_gain, r.out_cotangent, mid_terms, r.mid.early, r.mid.late],
        [r.middle, middle_all],
    )
    near = spread(middle_all)

    up_forward, up_end = grad_second(r.up_grad, mlp_in, r.pre_grad, swap)
    arrive(near[2], near[5])
    far = relay(middle_all)
    mlp_far = send_far(r.attn, mlp_terms)
    down_forward(1)
    down_project(4, 5, 0, 1)
    mlp_early = send_early(r.attn, mlp_terms)
    arrive(near[3], near[4])
    context_back(0, 1, 2, 3, 4, 5)

    @pl.loop(0, 2)
    def _(s):
        @pl.when(s == 1)
        def _():
            arrive(far[6], far[7])
            context_back(6, 7)
            up_forward(0)

        attend_back(s)

    wire.sent(*attn_far, *attn_early)
    swap = grad_first(r.qkv_w_grad, attn_in, r.qkv_grad)
    project_back(6, 7)
    back_far = send_far(r.mid, out_terms)
    qkv_forward, qkv_end = grad_second(r.qkv_w_grad, attn_in, r.qkv_grad, swap)
    project_back(2, 3, 4, 5)
    back_early = send_early(r.mid, out_terms)
    wire.sent(*mid_late)
    back_late = send_late(r.mid, out_terms, back_far, r.sums_b)
    up_forward(1)
    qkv_forward(0)
    swap = grad_first(r.out_grad, middle_all, r.context)
    wire.sent(*attn_late)
    mlp_late = send_late(r.attn, mlp_terms, mlp_far, r.sums_a)
    out_forward, out_end = grad_second(r.out_grad, middle_all, r.context, swap)
    project_back(0, 1)
    down_end(r.down_total)
    arrive(*back_early, *back_late)

    def first_back(x, mid, g, a, b, c_):
        back, gain = norm_back(x.astype(f32), g, a.astype(f32) + b.astype(f32) + c_.astype(f32))
        gain_sum[0:1, :] += gain
        return (mid + back,)

    row_wise(
        first_back,
        [r.tokens, r.middle, r.attn_gain, out_terms, r.mid.early, r.mid.late],
        [r.tokens_grad],
    )
    qkv_forward(1)
    out_forward(0)
    r.gain_near_sum[...] = over_all(r.gain_near, gain_sum, m, MP, 4)
    r.gains[...] = over_all(r.gain_far, r.gain_near_sum, d, DP, 8)
    up_end(r.up_total)
    out_forward(1)
    arrive(*mlp_early, *mlp_late)
    row_wise(
        lambda mid, *t: (mid + total(t),),
        [r.residual_mid, mlp_terms, r.attn.early, r.attn.late],
        [r.layer_output],
    )
    qkv_end()
    out_end(r.out_total)
    wire.finish()


def named(tree):
    return Names(**{k: named(v) for k, v in tree.items()}) if isinstance(tree, dict) else tree


def layer(ins, half, width, columns, units, length):
    full, rows = 2 * half, 8 * half
    share = width // 8
    big, own = shape((rows, width)), shape((full, width))
    arrivals = dict(far=own, early=own, late=own)

    def grad(n):
        line, sums = shape((3, share, n)), shape((2, share, n))
        stack = shape((4, share, n))
        return dict(mine=stack, got=stack, right=line, left=line, right_sums=sums, left_sums=sums)

    outs = dict(
        attn_in=big,
        cot_all=big,
        mlp_in=big,
        middle_all=big,
        out_terms=big,
        mlp_terms=big,
        mid_terms=big,
        hidden=shape((rows, units)),
        pre_grad=shape((rows, units)),
        qkv=shape((rows, 3 * columns)),
        qkv_grad=shape((rows, 3 * columns)),
        context=shape((rows, columns)),
        context_grad=shape((rows, columns)),
        attn=arrivals,
        mid=arrivals,
        sums_a=own,
        sums_b=own,
        down_grad=grad(units),
        up_grad=grad(units),
        qkv_w_grad=grad(3 * columns),
        out_grad=grad(columns),
        residual_mid=shape((full, width), f32),
        middle=shape((full, width), f32),
        layer_output=own,
        tokens_grad=shape((full, width), f32),
        down_total=shape((units, share), f32),
        up_total=shape((share, units), f32),
        out_total=shape((columns, share), f32),
    )
    any_, vmem = pl.BlockSpec(memory_space=pl.ANY), pl.BlockSpec(memory_space=pltpu.VMEM)
    places = dict(jax.tree.map(lambda _: any_, outs), gains=vmem)
    outs = dict(outs, gains=shape((2, width), f32))
    head, head_sum = pltpu.VMEM((length, HEAD_DIM), bf16), pltpu.VMEM((length, HEAD_DIM), f32)
    acc = pltpu.VMEM((full, width), f32)
    scratch = dict(
        qkv_w=pltpu.VMEM((width, 3 * columns), bf16),
        acc_g=acc,
        slopes=pltpu.VMEM((units // 512, full, 512), f32),
        down_acc=pltpu.VMEM((8, share, units), f32),
        gain_sum=pltpu.VMEM((2, width), f32),
        gain_near_sum=pltpu.VMEM((2, width), f32),
        gain_near=pltpu.VMEM((4, 2, width), f32),
        gain_far=pltpu.VMEM((8, 2, width), f32),
        q=head,
        k=head,
        v=head,
        c=head,
        f0=head_sum,
        f1=head_sum,
        f2=head_sum,
        seg_rows=pltpu.VMEM((2, 1, length), f32),
        seg_cols=pltpu.VMEM((2, length, 1), f32),
        send=pltpu.SemaphoreType.DMA((96,)),
        recv=pltpu.SemaphoreType.DMA((96,)),
        load=pltpu.SemaphoreType.DMA((3,)),
    )
    parts = [jax.tree.flatten(t) for t in (ins, outs, scratch)]
    kinds = [jax.tree.unflatten(t, range(len(v))) for v, t in parts]
    starts = (0, len(parts[0][0]), len(parts[0][0]) + len(parts[1][0]))
    place_of = {}
    for kind, begin in zip(kinds, starts):
        place_of.update(jax.tree.map(lambda i, b=begin: b + i, kind))
    order, tree = jax.tree.flatten(place_of)

    def kernel(*refs):
        layer_kernel((half, width, columns, units, length), tree, *[refs[i] for i in order])

    got = pl.pallas_call(
        kernel,
        in_specs=[any_] * len(parts[0][0]),
        out_specs=jax.tree.leaves(places),
        out_shape=parts[1][0],
        scratch_shapes=parts[2][0],
        compiler_params=pltpu.CompilerParams(
            collective_id=1, has_side_effects=True, vmem_limit_bytes=VMEM_LIMIT
        ),
        name="layer",
    )(*parts[0][0])
    return named(jax.tree.unflatten(parts[1][1], got))


def share_total(got, z, columns):
    mine, right, left = got.mine, got.right, got.left
    _, rows, width = mine.shape
    tile = 128

    def kernel(place, own, a, b, *outs):
        value = own[0].astype(f32)
        value = value + jnp.where(place[0] > 0, a[0].astype(f32), 0.0)
        value = value + jnp.where(place[0] < 3, b[0].astype(f32), 0.0)
        at = 0
        for out in outs:
            out[...] = value[:, at : at + out.shape[1]]
            at += out.shape[1]

    return call(
        kernel,
        [mine, right, left],
        (rows // tile,),
        [pl.BlockSpec((1, tile, width), lambda i, p: (p[0], i, 0))]
        + [pl.BlockSpec((1, tile, width), lambda i, p: (2, i, 0))] * 2,
        [pl.BlockSpec((tile, c), lambda i, p: (i, 0)) for c in columns],
        [shape((rows, c), f32) for c in columns],
        scalars=[z.astype(jnp.int32).reshape(1)],
        name="share_total",
        flops=rows * width,
        moved=rows * width * 10,
    )


def norm_rows(values, gain):
    centre = jnp.mean(values, axis=-1, keepdims=True)
    centred = values - centre
    spread = jnp.mean(centred * centred, axis=-1, keepdims=True)
    return centred * lax.rsqrt(spread + epsilon) * gain


def gelu_tanh(values):
    return jax.nn.gelu(values, approximate=True)


def block_allowed(segment):
    position = jnp.arange(segment.shape[0])
    return (position[None, :] <= position[:, None]) & (segment[:, None] == segment[None, :])


def rows_times(left_rows, right_matrix):
    return jnp.dot(left_rows, right_matrix, preferred_element_type=jnp.float32)


def rows_times_back(left_rows, right_matrix):
    return lax.dot_general(
        left_rows, right_matrix, (((1,), (1,)), ((), ())), preferred_element_type=jnp.float32
    )


def attn_input_back(
    queries_grad, keys_grad, values_grad, query_weight, key_weight, value_weight, score_scale
):
    total_grad = rows_times_back(queries_grad, query_weight) * score_scale
    total_grad = total_grad + rows_times_back(keys_grad, key_weight)
    return total_grad + rows_times_back(values_grad, value_weight)


def attend_forward(packed):
    queries, keys_in, values_in, segment = packed
    scores = jnp.einsum("qhd,khd->hqk", queries, keys_in, preferred_element_type=jnp.float32)
    scores = jnp.where(block_allowed(segment)[None], scores, masked_score)
    row_max = jnp.max(scores, axis=-1, keepdims=True)
    expanded = jnp.exp(scores - row_max)
    row_total = jnp.sum(expanded, axis=-1, keepdims=True)
    probs_low = (expanded / row_total).astype(jnp.bfloat16)
    context = jnp.einsum("hqk,khd->qhd", probs_low, values_in, preferred_element_type=jnp.float32)
    return (context.astype(jnp.bfloat16), (row_max + jnp.log(row_total))[:, :, 0])


def attend_backward(packed):
    queries, keys_in, values_in, segment, context_grad, log_total = packed
    scores = jnp.einsum("qhd,khd->hqk", queries, keys_in, preferred_element_type=jnp.float32)
    scores = jnp.where(block_allowed(segment)[None], scores, masked_score)
    attn_probs = jnp.exp(scores - log_total[:, :, None])
    probs_grad = jnp.einsum(
        "qhd,khd->hqk", context_grad, values_in, preferred_element_type=jnp.float32
    )
    values_grad = jnp.einsum(
        "hqk,qhd->khd",
        attn_probs.astype(jnp.bfloat16),
        context_grad,
        preferred_element_type=jnp.float32,
    )
    inner_sum = jnp.sum(attn_probs * probs_grad, axis=-1, keepdims=True)
    scores_grad = (attn_probs * (probs_grad - inner_sum)).astype(jnp.bfloat16)
    queries_grad = jnp.einsum(
        "hqk,khd->qhd", scores_grad, keys_in, preferred_element_type=jnp.float32
    )
    keys_grad = jnp.einsum("hqk,qhd->khd", scores_grad, queries, preferred_element_type=jnp.float32)
    return (
        queries_grad.astype(jnp.bfloat16),
        keys_grad.astype(jnp.bfloat16),
        values_grad.astype(jnp.bfloat16),
    )


def local_plain(
    tokens,
    segment_ids,
    query_weight,
    key_weight,
    value_weight,
    out_weight,
    up_weight,
    down_weight,
    attn_gain,
    mlp_gain,
    out_cotangent,
):
    seq_count, seq_length = segment_ids.shape
    group_rows = seq_count * seq_length
    head_count = query_weight.shape[1] // HEAD_DIM
    score_scale = 1.0 / math.sqrt(HEAD_DIM)
    shaped = (seq_count, seq_length, head_count, HEAD_DIM)
    flat_shape = (group_rows, head_count * HEAD_DIM)
    residual_in = tokens.astype(jnp.float32)
    normed_attn, attn_norm_back = jax.vjp(norm_rows, residual_in, attn_gain)
    gathered_attn = lax.all_gather(normed_attn.astype(jnp.bfloat16), MP, axis=0, tiled=True)
    queries = (
        jnp.dot(gathered_attn, query_weight, preferred_element_type=jnp.float32) * score_scale
    ).astype(jnp.bfloat16)
    keys_all = jnp.dot(gathered_attn, key_weight, preferred_element_type=jnp.float32).astype(
        jnp.bfloat16
    )
    values_all = jnp.dot(gathered_attn, value_weight, preferred_element_type=jnp.float32).astype(
        jnp.bfloat16
    )
    queries_seq = queries.reshape(shaped)
    keys_seq = keys_all.reshape(shaped)
    values_seq = values_all.reshape(shaped)
    context, log_total = lax.map(attend_forward, (queries_seq, keys_seq, values_seq, segment_ids))
    context_flat = context.reshape(flat_shape)
    attn_rows = lax.psum_scatter(
        rows_times(context_flat, out_weight).astype(jnp.bfloat16),
        MP,
        scatter_dimension=0,
        tiled=True,
    ).astype(jnp.float32)
    residual_mid = residual_in + attn_rows
    normed_mlp, mlp_norm_back = jax.vjp(norm_rows, residual_mid, mlp_gain)
    gathered_mlp = lax.all_gather(normed_mlp.astype(jnp.bfloat16), MP, axis=0, tiled=True)
    pre_act = jnp.dot(gathered_mlp, up_weight, preferred_element_type=jnp.float32)
    activated, gelu_back = jax.vjp(gelu_tanh, pre_act)
    hidden = activated.astype(jnp.bfloat16)
    mlp_rows = lax.psum_scatter(
        rows_times(hidden, down_weight).astype(jnp.bfloat16), MP, scatter_dimension=0, tiled=True
    ).astype(jnp.float32)
    layer_output = (residual_mid + mlp_rows).astype(jnp.bfloat16)
    cotangent_all = lax.all_gather(out_cotangent, MP, axis=0, tiled=True)
    down_weight_grad = jnp.einsum(
        "rf,rd->fd", hidden, cotangent_all, preferred_element_type=jnp.float32
    )
    hidden_grad = lax.dot_general(
        cotangent_all, down_weight, (((1,), (1,)), ((), ())), preferred_element_type=jnp.float32
    )
    pre_grad = gelu_back(hidden_grad)[0].astype(jnp.bfloat16)
    up_weight_grad = jnp.einsum(
        "rd,rf->df", gathered_mlp, pre_grad, preferred_element_type=jnp.float32
    )
    normed_mlp_grad = lax.psum_scatter(
        rows_times_back(pre_grad, up_weight).astype(jnp.bfloat16),
        MP,
        scatter_dimension=0,
        tiled=True,
    ).astype(jnp.float32)
    middle_back, mlp_gain_grad = mlp_norm_back(normed_mlp_grad)
    middle_grad = out_cotangent.astype(jnp.float32) + middle_back
    middle_all_grad = lax.all_gather(middle_grad.astype(jnp.bfloat16), MP, axis=0, tiled=True)
    out_weight_grad = jnp.einsum(
        "rc,rd->cd", context_flat, middle_all_grad, preferred_element_type=jnp.float32
    )
    context_grad = lax.dot_general(
        middle_all_grad, out_weight, (((1,), (1,)), ((), ())), preferred_element_type=jnp.float32
    ).astype(jnp.bfloat16)
    queries_grad, keys_grad, values_grad = lax.map(
        attend_backward,
        (queries_seq, keys_seq, values_seq, segment_ids, context_grad.reshape(shaped), log_total),
    )
    queries_grad = queries_grad.reshape(flat_shape)
    keys_grad = keys_grad.reshape(flat_shape)
    values_grad = values_grad.reshape(flat_shape)
    query_weight_grad = (
        jnp.einsum("rd,rc->dc", gathered_attn, queries_grad, preferred_element_type=jnp.float32)
        * score_scale
    )
    key_weight_grad = jnp.einsum(
        "rd,rc->dc", gathered_attn, keys_grad, preferred_element_type=jnp.float32
    )
    value_weight_grad = jnp.einsum(
        "rd,rc->dc", gathered_attn, values_grad, preferred_element_type=jnp.float32
    )
    normed_attn_grad = lax.psum_scatter(
        attn_input_back(
            queries_grad,
            keys_grad,
            values_grad,
            query_weight,
            key_weight,
            value_weight,
            score_scale,
        ).astype(jnp.bfloat16),
        MP,
        scatter_dimension=0,
        tiled=True,
    ).astype(jnp.float32)
    token_back, attn_gain_grad = attn_norm_back(normed_attn_grad)
    tokens_grad = middle_grad + token_back
    attn_gain_grad, mlp_gain_grad = lax.psum((attn_gain_grad, mlp_gain_grad), (DP, MP))
    (
        query_weight_grad,
        key_weight_grad,
        value_weight_grad,
        out_weight_grad,
        up_weight_grad,
        down_weight_grad,
    ) = (
        lax.psum_scatter(
            query_weight_grad.astype(jnp.bfloat16), DP, scatter_dimension=0, tiled=True
        ).astype(jnp.float32),
        lax.psum_scatter(
            key_weight_grad.astype(jnp.bfloat16), DP, scatter_dimension=0, tiled=True
        ).astype(jnp.float32),
        lax.psum_scatter(
            value_weight_grad.astype(jnp.bfloat16), DP, scatter_dimension=0, tiled=True
        ).astype(jnp.float32),
        lax.psum_scatter(
            out_weight_grad.astype(jnp.bfloat16), DP, scatter_dimension=1, tiled=True
        ).astype(jnp.float32),
        lax.psum_scatter(
            up_weight_grad.astype(jnp.bfloat16), DP, scatter_dimension=0, tiled=True
        ).astype(jnp.float32),
        lax.psum_scatter(
            down_weight_grad.astype(jnp.bfloat16), DP, scatter_dimension=1, tiled=True
        ).astype(jnp.float32),
    )
    return (
        layer_output,
        tokens_grad,
        query_weight_grad,
        key_weight_grad,
        value_weight_grad,
        out_weight_grad,
        up_weight_grad,
        down_weight_grad,
        attn_gain_grad,
        mlp_gain_grad,
    )


def local(
    mp,
    dp,
    tokens,
    segment_ids,
    query_weight,
    key_weight,
    value_weight,
    out_weight,
    up_weight,
    down_weight,
    attn_gain,
    mlp_gain,
    out_cotangent,
):
    width, columns = query_weight.shape
    length = segment_ids.shape[1]
    half = tokens.shape[0] // 2
    z = lax.axis_index(DP) // 2
    attn_gain, mlp_gain = attn_gain.reshape(1, width), mlp_gain.reshape(1, width)
    got = layer(
        dict(
            tokens=tokens,
            segment_ids=segment_ids,
            query_weight=query_weight,
            key_weight=key_weight,
            value_weight=value_weight,
            out_weight=out_weight,
            up_weight=up_weight,
            down_weight=down_weight,
            attn_gain=attn_gain,
            mlp_gain=mlp_gain,
            out_cotangent=out_cotangent,
        ),
        half,
        width,
        columns,
        up_weight.shape[1],
        length,
    )

    qkv_grads = share_total(got.qkv_w_grad, z, [columns] * 3)
    return (
        got.layer_output,
        got.tokens_grad,
        *qkv_grads,
        got.out_total,
        got.up_total,
        got.down_total,
        got.gains[0],
        got.gains[1],
    )


def solution(mesh):
    mp, dp = mesh.shape[MP], mesh.shape[DP]
    return jax.shard_map(
        functools.partial(local, mp, dp) if (mp, dp) == (4, 8) else local_plain,
        mesh=mesh,
        in_specs=(
            P(BOTH, None),
            P(DP, None),
            P(None, MP),
            P(None, MP),
            P(None, MP),
            P(MP, None),
            P(None, MP),
            P(MP, None),
            P(),
            P(),
            P(BOTH, None),
        ),
        out_specs=(
            P(BOTH, None),
            P(BOTH, None),
            P(DP, MP),
            P(DP, MP),
            P(DP, MP),
            P(MP, DP),
            P(DP, MP),
            P(MP, DP),
            P(),
            P(),
        ),
        check_vma=False,
    )
```

```python
import functools
import math
from types import SimpleNamespace as Names

import jax
import jax.numpy as jnp
from jax import lax
from jax.experimental import pallas as pl
from jax.experimental.pallas import tpu as pltpu
from jax.sharding import PartitionSpec as P

HEAD_DIM = 128
CLIP_MOST = 256
epsilon = 1e-05
masked_score = -1e30
bf16, f32 = jnp.bfloat16, jnp.float32
VMEM_LIMIT = 60 * 1024 * 1024
MESH = pl.DeviceIdType.MESH
WHOLE, VEC = range(2)
DP, MP = BOTH = ("dp", "mp")


def dot(a, b, ca, cb):
    return lax.dot_general(a, b, (((ca,), (cb,)), ((), ())), preferred_element_type=f32)


def shape(dims, kind=bf16):
    return jax.ShapeDtypeStruct(dims, kind)


def call(kernel, args, grid, in_specs, out_specs, outs, *, name, scalars=(), scratch=(), after=(), flops=0, moved=0, **extra):
    lead = len(scalars) + len(args)

    def body(*refs):
        kernel(*refs[:lead], *refs[lead + len(after) :])

    return pl.pallas_call(
        body,
        grid_spec=pltpu.PrefetchScalarGridSpec(
            num_scalar_prefetch=len(scalars),
            grid=grid,
            in_specs=[*in_specs, *[pl.BlockSpec(memory_space=pl.ANY)] * len(after)],
            out_specs=out_specs,
            scratch_shapes=list(scratch),
        ),
        out_shape=outs,
        compiler_params=pltpu.CompilerParams(vmem_limit_bytes=VMEM_LIMIT, **extra),
        cost_estimate=pl.CostEstimate(flops=flops, bytes_accessed=moved, transcendentals=0),
        name=name,
    )(*scalars, *args, *after)


def norm_parts(values):
    centred = values - jnp.mean(values, axis=-1, keepdims=True)
    spread = jnp.mean(centred * centred, axis=-1, keepdims=True)
    scale = lax.rsqrt(spread + epsilon)
    return centred * scale, scale


def norm_back(values, gain, grad):
    unit, scale = norm_parts(values)
    q = grad * gain
    back = scale * (
        q - jnp.mean(q, axis=-1, keepdims=True) - unit * jnp.mean(q * unit, axis=-1, keepdims=True)
    )
    return back, jnp.sum(grad * unit, axis=0, keepdims=True)


def total(values):
    out = values[0].astype(f32)
    for v in values[1:]:
        out = out + v.astype(f32)
    return out


def gelu_both(u):
    c = math.sqrt(2.0 / math.pi)
    square = u * u
    t = jnp.tanh(c * (u + 0.044715 * (u * square)))
    half = 0.5 * (1.0 + t)
    value = u * half
    slope = half + (0.5 * c) * u * (1.0 - t * t) * (1.0 + (3 * 0.044715) * square)
    return value, slope


def allowed_of(seg_col, seg_row, q0, k0, k1, rows):
    same = seg_col[q0 : q0 + rows, :] == seg_row[:, k0:k1]
    dims = (rows, k1 - k0)
    i = lax.broadcasted_iota(jnp.int32, dims, 0) + q0
    j = lax.broadcasted_iota(jnp.int32, dims, 1) + k0
    return same & (j <= i)


class Sent:
    def __init__(self, wire, slot, source, target, to):
        self.wire, self.slot, self.ends, self.to = wire, slot, (source, target), to

    def make(self):
        source, target = (e() if callable(e) else e for e in self.ends)
        return self.wire.copy(self.slot, source, target, self.to)

    def wait_recv(self):
        self.make().wait_recv()

    def wait_send(self):
        self.make().wait_send()


class Wire:
    def __init__(self, send, recv):
        self.send, self.recv, self.count, self.ends = send, recv, 0, []

    def slot(self):
        self.count += 1
        return self.count - 1

    def copy(self, slot, source, target, to):
        return pltpu.make_async_remote_copy(
            src_ref=source,
            dst_ref=target,
            send_sem=self.send.at[slot],
            recv_sem=self.recv.at[slot],
            device_id=to,
            device_id_type=MESH,
        )

    def go(self, source, target, to):
        copy = Sent(self, self.slot(), source, target, to)
        copy.make().start()
        self.ends.append(copy)
        return copy

    def sent(self, *copies):
        for copy in copies:
            copy.wait_send()
            self.ends = [c for c in self.ends if c is not copy]

    def finish(self):
        self.sent(*list(self.ends))


def stage(body, grid, ins, outs):
    pltpu.emit_pipeline(
        body,
        grid=grid,
        in_specs=[pl.BlockSpec(b, f) for _, b, f in ins],
        out_specs=[pl.BlockSpec(b, f) for _, b, f in outs],
    )(*[r for r, _, _ in ins], *[r for r, _, _ in outs])


def layer_kernel(dims, tree, *refs):
    half, width, columns, units, length = dims
    full = 2 * half
    rows = 4 * full
    r = named(jax.tree.unflatten(tree, refs))
    m, d = lax.axis_index(MP), lax.axis_index(DP)
    core, z = lax.rem(d, 2), d // 2
    parity = lax.rem(m, 2)
    to_x = {MP: m + 1 - 2 * parity}
    to_y = {MP: m + 2 - 4 * (m // 2)}
    to_core = {DP: d + 1 - 2 * core}
    wire = Wire(r.send, r.recv)
    heads = columns // HEAD_DIM
    score_scale = 1.0 / math.sqrt(HEAD_DIM)

    barrier = pltpu.get_barrier_semaphore()
    others = [{MP: lax.rem(m + i, 4)} for i in range(1, 4)] + [{DP: lax.rem(d + i, 8)} for i in range(1, 8)]
    for peer in others:
        pl.semaphore_signal(barrier, inc=1, device_id=peer, device_id_type=MESH)
    pl.semaphore_wait(barrier, len(others))

    def at(ref, block):
        return lambda: ref.at[pl.ds(block * half, half)]

    qkv_w = r.qkv_w
    loads = [
        pltpu.make_async_copy(w, qkv_w.at[:, pl.ds(i * columns, columns)], r.load.at[i])
        for i, w in enumerate((r.query_weight, r.key_weight, r.value_weight))
    ]
    for load in loads:
        load.start()

    tile = half // 2

    def row_ins(*values):
        out = []
        for v in values:
            ref, f = v if isinstance(v, tuple) else (v, lambda i: (i, 0))
            out.append((ref, (1 if ref.shape[0] == 1 else tile, width), (lambda i: (0, 0)) if ref.shape[0] == 1 else f))
        return out

    def row_wise(fn, ins, outs):
        n = len(ins)

        def body(*refs):
            for ref, value in zip(refs[n:], fn(*[x[...] for x in refs[:n]])):
                ref[...] = value.astype(ref.dtype)

        stage(body, (4,), row_ins(*ins), row_ins(*outs))

    def spread(ref):
        return {
            2: wire.go(at(ref, 0), at(ref, 2), to_x),
            5: wire.go(at(ref, 1), at(ref, 5), to_y),
            3: wire.go(at(ref, 1), at(ref, 3), to_x),
            4: wire.go(at(ref, 0), at(ref, 4), to_y),
        }

    def relay(ref):
        return {6: wire.go(at(ref, 2), at(ref, 6), to_y), 7: wire.go(at(ref, 5), at(ref, 7), to_x)}

    def send_far(into, terms):
        return [wire.go(at(terms, 6), at(into.far, 0), to_x), wire.go(at(terms, 7), at(into.far, 1), to_y)]

    def send_early(into, terms):
        return [wire.go(at(terms, 2), at(into.early, 0), to_x), wire.go(at(terms, 5), at(into.early, 1), to_y)]

    def send_late(into, terms, far, sums):
        for copy in far:
            copy.wait_recv()
        row_wise(
            lambda a, b: (a.astype(f32) + b.astype(f32),),
            [(terms, lambda i: (jnp.where(i < 2, 8 + i, 4 + i), 0)), into.far],
            [sums],
        )
        return [wire.go(at(sums, 0), at(into.late, 0), to_y), wire.go(at(sums, 1), at(into.late, 1), to_x)]

    def arrive(*copies):
        for copy in copies:
            copy.wait_recv()

    def product(source, target, blocks, weight, size, count, trans=False, scale=None):
        n = len(blocks)
        depth = source.shape[1]
        ref, ref_block, ref_map = weight if isinstance(weight, tuple) else (None, None, None)

        def body(*refs):
            j = pl.program_id(0)
            x = jnp.concatenate([b[...] for b in refs[:n]], axis=0) if n > 1 else refs[0][...]
            w = refs[n][...] if ref is not None else weight(j)
            acc = dot(x, w, 1, 1 if trans else 0)
            if scale is not None:
                acc = acc * scale(j)
            for i, out in enumerate(refs[-n:]):
                out[...] = acc[i * half : (i + 1) * half].astype(bf16)

        stage(
            body,
            (count,),
            [(source, (half, depth), lambda j, b=b: (b, 0)) for b in blocks]
            + ([(ref, ref_block, ref_map)] if ref is not None else []),
            [(target, (half, size), lambda j, b=b: (b, j)) for b in blocks],
        )

    def project(*blocks):
        product(
            r.attn_in,
            r.qkv,
            blocks,
            lambda j: qkv_w[:, pl.ds(pl.multiple_of(j * columns, columns), columns)],
            columns,
            3,
            scale=lambda j: jnp.where(j == 0, score_scale, 1.0),
        )

    def out_project(*blocks):
        product(
            r.context,
            r.out_terms,
            blocks,
            (r.out_weight, (columns, width // 2), lambda j: (0, j)),
            width // 2,
            2,
        )

    def context_back(*blocks):
        product(
            r.middle_all,
            r.context_grad,
            blocks,
            (r.out_weight, (columns // 2, width), lambda j: (j, 0)),
            columns // 2,
            2,
            trans=True,
        )

    def project_back(*blocks):
        size = width // 4
        product(
            r.qkv_grad,
            r.out_terms,
            blocks,
            lambda j: qkv_w[pl.ds(pl.multiple_of(j * size, size), size), :],
            size,
            4,
            trans=True,
        )

    def turn(block, target):
        for b in range(2):
            to = pl.multiple_of(lax.rem(parity + b, 2) * full, full)
            target[pl.ds(to, full), :] = block[b * full : (b + 1) * full, :]

    def turn_back(source, block):
        for b in range(2):
            come = pl.multiple_of(lax.rem(parity + b, 2) * full, full)
            block[b * full : (b + 1) * full, :] = source[pl.ds(come, full), :].astype(bf16)

    q, k, v, c = r.q, r.k, r.v, r.c
    f0, f1, f2 = r.f0, r.f1, r.f2

    def head_ins(s):
        ins = []
        for which in range(3):
            ins.append((r.qkv, (length, HEAD_DIM), lambda h, w=which: (s, w * heads + h)))
        return ins

    def scores_of(s, q0, k0, k1):
        which = lax.rem(m // 2 + s, 2)
        scores = dot(q[q0:k1, :], k[k0:k1, :], 1, 1)
        keep = allowed_of(r.seg_cols.at[which], r.seg_rows.at[which], q0, k0, k1, CLIP_MOST)
        scores = jnp.where(keep, scores, masked_score)
        e = jnp.exp(scores - jnp.max(scores, axis=-1, keepdims=True))
        return e * (1.0 / jnp.sum(e, axis=-1, keepdims=True))

    def attend(s):
        def body(q_in, k_in, v_in, out):
            turn(q_in, q)
            turn(k_in, k)
            turn(v_in, v)
            for q0 in range(0, length, CLIP_MOST):
                k0, k1 = max(0, q0 - CLIP_MOST), q0 + CLIP_MOST
                p = scores_of(s, q0, k0, k1).astype(bf16)
                f0[q0:k1, :] = dot(p, v[k0:k1, :], 1, 0)
            turn_back(f0, out)

        stage(body, (heads,), head_ins(s), [(r.context, (length, HEAD_DIM), lambda h: (s, h))])

    def attend_back(s):
        def body(q_in, k_in, v_in, c_in, dq_out, dk_out, dv_out):
            turn(q_in, q)
            turn(k_in, k)
            turn(v_in, v)
            turn(c_in, c)
            for q0 in range(0, length, CLIP_MOST):
                k0, k1 = max(0, q0 - CLIP_MOST), q0 + CLIP_MOST
                p = scores_of(s, q0, k0, k1)
                qb, cb, kb, vb = q[q0:k1, :], c[q0:k1, :], k[k0:k1, :], v[k0:k1, :]
                dp = dot(cb, vb, 1, 1)
                inner = jnp.sum(p * dp, axis=-1, keepdims=True)
                ds = (p * (dp - inner)).astype(bf16)
                f0[q0:k1, :] = dot(ds, kb, 1, 0) * score_scale
                dk, dv = dot(ds, qb, 0, 0), dot(p.astype(bf16), cb, 0, 0)
                if q0 > 0:
                    f1[k0:q0, :] += dk[:CLIP_MOST]
                    f2[k0:q0, :] += dv[:CLIP_MOST]
                    dk, dv = dk[CLIP_MOST:], dv[CLIP_MOST:]
                f1[q0:k1, :] = dk
                f2[q0:k1, :] = dv
            turn_back(f0, dq_out)
            turn_back(f1, dk_out)
            turn_back(f2, dv_out)

        stage(
            body,
            (heads,),
            [*head_ins(s), (r.context_grad, (length, HEAD_DIM), lambda h: (s, h))],
            [(r.qkv_grad, (length, HEAD_DIM), lambda h, w=w: (s, w * heads + h)) for w in range(3)],
        )

    acc_g, slopes = r.acc_g, r.slopes
    size = 512
    tiles = units // size
    up_tile = (r.up_weight, (width, size), lambda j: (0, j))
    down_tile = (r.down_weight, (size, width), lambda j: (j, 0))

    def whole(ref, both):
        return [(ref, (half, width), lambda j, i=i: (i, 0)) for i in both]

    def part(ref, both):
        return [(ref, (half, size), lambda j, i=i: (i, j)) for i in both]

    def rows_of(a, b):
        return jnp.concatenate([a[...], b[...]], axis=0)

    def grads_of(grad, up, p0, p1, g0, g1):
        j = pl.program_id(0)
        grad = grad.astype(bf16)
        p0[...], p1[...] = grad[:half], grad[half:]
        g = dot(grad, up[...], 1, 1)

        @pl.when(j == 0)
        def _():
            acc_g[...] = g

        @pl.when((j > 0) & (j < tiles - 1))
        def _():
            acc_g[...] += g

        @pl.when(j == tiles - 1)
        def _():
            last = acc_g[...] + g
            g0[...], g1[...] = last[:half].astype(bf16), last[half:].astype(bf16)

    def feed(*both):
        def body(x0, x1, c0, c1, up, down, h0, h1, *outs):
            value, slope = gelu_both(dot(rows_of(x0, x1), up[...], 1, 0))
            value = value.astype(bf16)
            h0[...], h1[...] = value[:half], value[half:]
            grads_of(dot(rows_of(c0, c1), down[...], 1, 1) * slope, up, *outs)

        stage(
            body,
            (tiles,),
            [*whole(r.mlp_in, both), *whole(r.cot_all, both), up_tile, down_tile],
            [*part(r.hidden, both), *part(r.pre_grad, both), *whole(r.mid_terms, both)],
        )

    def feed_forward(*both):
        def body(x0, x1, up, h0, h1):
            value, slope = gelu_both(dot(rows_of(x0, x1), up[...], 1, 0))
            value = value.astype(bf16)
            h0[...], h1[...] = value[:half], value[half:]
            slopes[pl.program_id(0)] = slope

        stage(body, (tiles,), [*whole(r.mlp_in, both), up_tile], part(r.hidden, both))

    def feed_back(*both):
        def body(c0, c1, up, down, *outs):
            grads_of(dot(rows_of(c0, c1), down[...], 1, 1) * slopes[pl.program_id(0)], up, *outs)

        stage(
            body,
            (tiles,),
            [*whole(r.cot_all, both), up_tile, down_tile],
            [*part(r.pre_grad, both), *whole(r.mid_terms, both)],
        )

    down_acc = r.down_acc
    share = width // 8

    def down_some(first, count, both, target=None, plus=None):
        begin = 0 in both
        n = len(both)

        def body(*refs):
            s = pl.program_id(0)
            left, right = ([b[...] for b in refs[i * n : (i + 1) * n]] for i in range(2))
            acc = dot(jnp.concatenate(left, axis=0), jnp.concatenate(right, axis=0), 0, 0)
            if not begin:
                acc = acc + down_acc[first + s]
            if target is None:
                down_acc[first + s] = acc
                return
            if plus is not None:
                acc = acc + refs[2 * n][0].astype(f32)
            refs[-1][0] = acc.astype(bf16)

        def column(s):
            k = first + s
            return 2 * lax.rem(k, 4) + jnp.where(k < 4, 1 - core, core)

        block = (1, share, units)
        stage(
            body,
            (count,),
            [(r.cot_all, (half, share), lambda s, i=i: (i, column(s))) for i in both]
            + [(r.hidden, (half, units), lambda s, i=i: (i, 0)) for i in both]
            + ([(plus, block, lambda s: (s, 0, 0))] if plus is not None else []),
            [(target, block, lambda s: (s, 0, 0))] if target is not None else [],
        )

    def grad_product(left, right, which, target, plus=None):
        def body(a, b, *rest):
            acc = dot(a[...], b[...], 0, 0)
            if plus is not None:
                acc = acc + rest[0][0].astype(f32)
            rest[-1][0] = acc.astype(bf16)

        n = right.shape[1]
        block = (1, share, n)
        place = lambda s: (s, 0, 0)
        stage(
            body,
            (4,),
            [
                (left, (rows, share), lambda s: (0, 2 * s + which)),
                (right, (rows, n), lambda s: (0, 0)),
                *([(plus, block, place)] if plus is not None else []),
            ],
            [(target, block, place)],
        )

    def grad_first(into, left, right):
        grad_product(left, right, 1 - core, into.mine)
        return wire.go(into.mine, into.got, to_core)

    def grad_second(into, left, right, swap):
        swap.wait_recv()
        wire.sent(swap)
        grad_product(left, right, core, into.mine, into.got)
        return start_line(into)

    def start_line(into):
        mine = into.mine
        n = mine.shape[2]
        part = share // 2
        ways = []
        for step, got, sums in ((1, into.right, into.right_sums), (-1, into.left, into.left_sums)):
            slots = [wire.slot() for _ in range(3)]
            to = {DP: jnp.clip(d + 2 * step, 0, 7)}
            place = z if step > 0 else 3 - z
            ways.append((step, place, got, sums, slots, to))

        def of(step, place):
            return jnp.clip(place if step > 0 else 3 - place, 0, 3)

        def copy(way, t, source):
            _, _, got, _, slots, to = way
            return wire.copy(slots[t], source, got.at[t], to)

        for way in ways:

            @pl.when(way[1] == 0)
            def _():
                for t in range(3):
                    copy(way, t, mine.at[of(way[0], 3 - t)]).start()

        def add(t, ways):
            for way in ways:
                copy(way, t, mine.at[0]).wait_recv()

            def body(*refs):
                for w in range(len(ways)):
                    a, b = refs[2 * w : 2 * w + 2]
                    refs[2 * len(ways) + w][...] = (a[0].astype(f32) + b[...].astype(f32)).astype(bf16)

            ins, outs = [], []
            for step, place, got, sums, _, _ in ways:
                ins.append((mine, (1, part, n), lambda i, s=step, p=place: (of(s, p + 2 - t), i, 0)))
                ins.append((got.at[t], (part, n), lambda i: (i, 0)))
                outs.append((sums.at[t], (part, n), lambda i: (i, 0)))
            stage(body, (2,), ins, outs)
            for way in ways:
                copy(way, t + 1, way[3].at[t]).start()

        def forward(t):
            if t == 1:
                pl.when((z == 1) | (z == 2))(lambda: add(1, ways))
                return
            for way in ways:
                pl.when(way[1] == 1)(lambda: add(0, [way]))

        def end(turned=None):
            for way in ways:
                place = way[1]

                @pl.when(place >= 1)
                def _():
                    copy(way, 2, mine.at[0]).wait_recv()

                for t in range(3):

                    @pl.when((place <= t) & (place < 3))
                    def _():
                        copy(way, t, mine.at[0]).wait_send()

            if turned is not None:
                share_total(into, turned)

        return forward, end

    def share_total(into, target):
        turned = target.shape[1] == share
        n = into.mine.shape[2]
        tile = 128

        def body(own, right, left, out):
            value = own[0].astype(f32)
            value = value + jnp.where(z > 0, right[0].astype(f32), 0.0)
            value = value + jnp.where(z < 3, left[0].astype(f32), 0.0)
            out[...] = value.T if turned else value

        block = (1, tile, n)
        stage(
            body,
            (share // tile,),
            [(into.mine, block, lambda i: (z, i, 0)), (into.right, block, lambda i: (2, i, 0)), (into.left, block, lambda i: (2, i, 0))],
            [(target, (n, tile), lambda i: (0, i)) if turned else (target, (tile, n), lambda i: (i, 0))],
        )

    def over_all(slots, value, me, axis, count):
        copies = [wire.go(value, slots.at[me], {axis: lax.rem(me + i, count)}) for i in range(1, count)]
        slots[pl.ds(me, 1)] = value[...][None]
        arrive(*copies)
        return functools.reduce(lambda a, i: a + slots[i], range(1, count), slots[0])

    attn_in, cot_all, mlp_in, middle_all = r.attn_in, r.cot_all, r.mlp_in, r.middle_all
    row_wise(
        lambda x, g: (norm_parts(x.astype(f32))[0] * g,), [r.tokens, r.attn_gain], [attn_in]
    )
    near = spread(attn_in)
    row_wise(lambda x: (x,), [r.out_cotangent], [cot_all])

    def segments(ids):
        same = lax.broadcasted_iota(jnp.int32, (128, 128), 0) == lax.broadcasted_iota(jnp.int32, (128, 128), 1)
        for i in range(2):
            for at_ in range(0, length, 128):
                row = ids[i : i + 1, at_ : at_ + 128].astype(f32)
                r.seg_rows[i, :, at_ : at_ + 128] = row
                r.seg_cols[i, at_ : at_ + 128, :] = jnp.sum(jnp.where(same, row, 0.0), axis=1, keepdims=True)

    stage(segments, (1,), [(r.segment_ids, (2, length), lambda i: (0, 0))], [])
    for load in loads:
        load.wait()
    project(0, 1)
    arrive(near[2], near[5])
    far = relay(attn_in)
    arrive(near[3], near[4])
    cot_near = {2: wire.go(at(cot_all, 0), at(cot_all, 2), to_x), 5: wire.go(at(cot_all, 1), at(cot_all, 5), to_y)}
    project(2, 3, 4, 5)

    @pl.loop(0, 2)
    def _(s):
        @pl.when(s == 1)
        def _():
            arrive(far[6], far[7])
            project(6, 7)

        attend(s)

    out_terms = r.out_terms
    out_project(6, 7)
    attn_far = send_far(r.attn, out_terms)
    out_project(2, 3, 4, 5)
    attn_early = send_early(r.attn, out_terms)
    out_project(0, 1)
    attn_late = send_late(r.attn, out_terms, attn_far, r.sums_a)
    cot_near[3] = wire.go(at(cot_all, 1), at(cot_all, 3), to_x)
    cot_near[4] = wire.go(at(cot_all, 0), at(cot_all, 4), to_y)
    arrive(*attn_early, *attn_late)

    def second(x, g, a, b, c_):
        mid = x.astype(f32) + a.astype(f32) + b.astype(f32) + c_.astype(f32)
        return mid, norm_parts(mid)[0] * g

    row_wise(
        second,
        [r.tokens, r.mlp_gain, out_terms, r.attn.early, r.attn.late],
        [r.residual_mid, mlp_in],
    )
    near = spread(mlp_in)
    arrive(cot_near[2], cot_near[5])
    mid_terms = r.mid_terms
    far, cot_far, mid_early = {}, {}, []

    @pl.loop(0, 3)
    def _(g):
        @pl.when(g == 1)
        def _():
            arrive(near[2], near[5])
            far.update(relay(mlp_in))
            cot_far.update(relay(cot_all))

        @pl.when(g == 2)
        def _():
            mid_early.extend(send_early(r.mid, mid_terms))
            down_some(0, 8, (0, 1, 2, 5))
            arrive(near[3], near[4], cot_near[3], cot_near[4])

        later = (g + 1) // 2
        feed(g + later, 1 - g + 5 * later)

    arrive(far[6], far[7])
    feed_forward(6, 7)
    arrive(cot_far[6], cot_far[7])
    down, last = r.down_grad, (3, 4, 6, 7)
    down_some(0, 4, last, down.mine)
    swap = wire.go(down.mine, down.got, to_core)
    feed_back(6, 7)
    mid_far = send_far(r.mid, mid_terms)
    arrive(swap)
    wire.sent(swap)
    down_some(4, 4, last, down.mine, down.got)
    down_forward, down_end = start_line(down)
    swap = grad_first(r.up_grad, mlp_in, r.pre_grad)
    mid_late = send_late(r.mid, mid_terms, mid_far, r.sums_b)
    mlp_terms = r.mlp_terms

    def down_project(*blocks):
        product(r.hidden, mlp_terms, blocks, (r.down_weight, (units, size), lambda j: (0, j)), size, width // size)

    down_project(6, 7, 2, 3)
    down_forward(0)
    arrive(*mid_early, *mid_late)
    gain_sum = r.gain_sum
    gain_sum[...] = jnp.zeros_like(gain_sum)

    def second_back(mid, g, cot, a, b, c_):
        back, gain = norm_back(mid, g, a.astype(f32) + b.astype(f32) + c_.astype(f32))
        gain_sum[1:2, :] += gain
        value = cot.astype(f32) + back
        return value, value

    row_wise(
        second_back,
        [r.residual_mid, r.mlp_gain, r.out_cotangent, mid_terms, r.mid.early, r.mid.late],
        [r.middle, middle_all],
    )
    near = spread(middle_all)

    up_forward, up_end = grad_second(r.up_grad, mlp_in, r.pre_grad, swap)
    arrive(near[2], near[5])
    far = relay(middle_all)
    mlp_far = send_far(r.attn, mlp_terms)
    down_forward(1)
    down_project(4, 5, 0, 1)
    mlp_early = send_early(r.attn, mlp_terms)
    arrive(near[3], near[4])
    context_back(0, 1, 2, 3, 4, 5)

    @pl.loop(0, 2)
    def _(s):
        @pl.when(s == 1)
        def _():
            arrive(far[6], far[7])
            context_back(6, 7)
            up_forward(0)

        attend_back(s)

    wire.sent(*attn_far, *attn_early)
    swap = grad_first(r.qkv_w_grad, attn_in, r.qkv_grad)
    project_back(6, 7)
    back_far = send_far(r.mid, out_terms)
    qkv_forward, qkv_end = grad_second(r.qkv_w_grad, attn_in, r.qkv_grad, swap)
    project_back(2, 3, 4, 5)
    back_early = send_early(r.mid, out_terms)
    wire.sent(*mid_late)
    back_late = send_late(r.mid, out_terms, back_far, r.sums_b)
    up_forward(1)
    qkv_forward(0)
    swap = grad_first(r.out_grad, middle_all, r.context)
    wire.sent(*attn_late)
    mlp_late = send_late(r.attn, mlp_terms, mlp_far, r.sums_a)
    out_forward, out_end = grad_second(r.out_grad, middle_all, r.context, swap)
    project_back(0, 1)
    qkv_forward(1)
    arrive(*back_early, *back_late)

    def first_back(x, mid, g, a, b, c_):
        back, gain = norm_back(x.astype(f32), g, a.astype(f32) + b.astype(f32) + c_.astype(f32))
        gain_sum[0:1, :] += gain
        return (mid + back,)

    row_wise(
        first_back,
        [r.tokens, r.middle, r.attn_gain, out_terms, r.mid.early, r.mid.late],
        [r.tokens_grad],
    )
    out_forward(0)
    r.gain_near_sum[...] = over_all(r.gain_near, gain_sum, m, MP, 4)
    r.gains[...] = over_all(r.gain_far, r.gain_near_sum, d, DP, 8)
    up_end(r.up_total)
    out_forward(1)
    down_end(r.down_total)
    arrive(*mlp_early, *mlp_late)
    row_wise(
        lambda mid, *t: (mid + total(t),),
        [r.residual_mid, mlp_terms, r.attn.early, r.attn.late],
        [r.layer_output],
    )
    qkv_end()
    out_end(r.out_total)
    wire.finish()


def named(tree):
    return Names(**{k: named(v) for k, v in tree.items()}) if isinstance(tree, dict) else tree


def layer(ins, half, width, columns, units, length):
    full, rows = 2 * half, 8 * half
    share = width // 8
    big, own = shape((rows, width)), shape((full, width))
    arrivals = dict(far=own, early=own, late=own)

    def grad(n):
        line, sums = shape((3, share, n)), shape((2, share, n))
        stack = shape((4, share, n))
        return dict(mine=stack, got=stack, right=line, left=line, right_sums=sums, left_sums=sums)

    outs = dict(
        attn_in=big,
        cot_all=big,
        mlp_in=big,
        middle_all=big,
        out_terms=big,
        mlp_terms=big,
        mid_terms=big,
        hidden=shape((rows, units)),
        pre_grad=shape((rows, units)),
        qkv=shape((rows, 3 * columns)),
        qkv_grad=shape((rows, 3 * columns)),
        context=shape((rows, columns)),
        context_grad=shape((rows, columns)),
        attn=arrivals,
        mid=arrivals,
        sums_a=own,
        sums_b=own,
        down_grad=grad(units),
        up_grad=grad(units),
        qkv_w_grad=grad(3 * columns),
        out_grad=grad(columns),
        residual_mid=shape((full, width), f32),
        middle=shape((full, width), f32),
        layer_output=own,
        tokens_grad=shape((full, width), f32),
        down_total=shape((units, share), f32),
        up_total=shape((share, units), f32),
        out_total=shape((columns, share), f32),
    )
    any_, vmem = pl.BlockSpec(memory_space=pl.ANY), pl.BlockSpec(memory_space=pltpu.VMEM)
    places = dict(jax.tree.map(lambda _: any_, outs), gains=vmem)
    outs = dict(outs, gains=shape((2, width), f32))
    head, head_sum = pltpu.VMEM((length, HEAD_DIM), bf16), pltpu.VMEM((length, HEAD_DIM), f32)
    acc = pltpu.VMEM((full, width), f32)
    scratch = dict(
        qkv_w=pltpu.VMEM((width, 3 * columns), bf16),
        acc_g=acc,
        slopes=pltpu.VMEM((units // 512, full, 512), f32),
        down_acc=pltpu.VMEM((8, share, units), f32),
        gain_sum=pltpu.VMEM((2, width), f32),
        gain_near_sum=pltpu.VMEM((2, width), f32),
        gain_near=pltpu.VMEM((4, 2, width), f32),
        gain_far=pltpu.VMEM((8, 2, width), f32),
        q=head,
        k=head,
        v=head,
        c=head,
        f0=head_sum,
        f1=head_sum,
        f2=head_sum,
        seg_rows=pltpu.VMEM((2, 1, length), f32),
        seg_cols=pltpu.VMEM((2, length, 1), f32),
        send=pltpu.SemaphoreType.DMA((96,)),
        recv=pltpu.SemaphoreType.DMA((96,)),
        load=pltpu.SemaphoreType.DMA((3,)),
    )
    parts = [jax.tree.flatten(t) for t in (ins, outs, scratch)]
    kinds = [jax.tree.unflatten(t, range(len(v))) for v, t in parts]
    starts = (0, len(parts[0][0]), len(parts[0][0]) + len(parts[1][0]))
    place_of = {}
    for kind, begin in zip(kinds, starts):
        place_of.update(jax.tree.map(lambda i, b=begin: b + i, kind))
    order, tree = jax.tree.flatten(place_of)

    def kernel(*refs):
        layer_kernel((half, width, columns, units, length), tree, *[refs[i] for i in order])

    got = pl.pallas_call(
        kernel,
        in_specs=[any_] * len(parts[0][0]),
        out_specs=jax.tree.leaves(places),
        out_shape=parts[1][0],
        scratch_shapes=parts[2][0],
        compiler_params=pltpu.CompilerParams(
            collective_id=1, has_side_effects=True, vmem_limit_bytes=VMEM_LIMIT
        ),
        name="layer",
    )(*parts[0][0])
    return named(jax.tree.unflatten(parts[1][1], got))


def share_total(got, z, columns):
    mine, right, left = got.mine, got.right, got.left
    _, rows, width = mine.shape
    tile = 128

    def kernel(place, own, a, b, *outs):
        value = own[0].astype(f32)
        value = value + jnp.where(place[0] > 0, a[0].astype(f32), 0.0)
        value = value + jnp.where(place[0] < 3, b[0].astype(f32), 0.0)
        at = 0
        for out in outs:
            out[...] = value[:, at : at + out.shape[1]]
            at += out.shape[1]

    return call(
        kernel,
        [mine, right, left],
        (rows // tile,),
        [pl.BlockSpec((1, tile, width), lambda i, p: (p[0], i, 0))]
        + [pl.BlockSpec((1, tile, width), lambda i, p: (2, i, 0))] * 2,
        [pl.BlockSpec((tile, c), lambda i, p: (i, 0)) for c in columns],
        [shape((rows, c), f32) for c in columns],
        scalars=[z.astype(jnp.int32).reshape(1)],
        name="share_total",
        flops=rows * width,
        moved=rows * width * 10,
    )


def norm_rows(values, gain):
    centre = jnp.mean(values, axis=-1, keepdims=True)
    centred = values - centre
    spread = jnp.mean(centred * centred, axis=-1, keepdims=True)
    return centred * lax.rsqrt(spread + epsilon) * gain


def gelu_tanh(values):
    return jax.nn.gelu(values, approximate=True)


def block_allowed(segment):
    position = jnp.arange(segment.shape[0])
    return (position[None, :] <= position[:, None]) & (segment[:, None] == segment[None, :])


def rows_times(left_rows, right_matrix):
    return jnp.dot(left_rows, right_matrix, preferred_element_type=jnp.float32)


def rows_times_back(left_rows, right_matrix):
    return lax.dot_general(
        left_rows, right_matrix, (((1,), (1,)), ((), ())), preferred_element_type=jnp.float32
    )


def attn_input_back(
    queries_grad, keys_grad, values_grad, query_weight, key_weight, value_weight, score_scale
):
    total_grad = rows_times_back(queries_grad, query_weight) * score_scale
    total_grad = total_grad + rows_times_back(keys_grad, key_weight)
    return total_grad + rows_times_back(values_grad, value_weight)


def attend_forward(packed):
    queries, keys_in, values_in, segment = packed
    scores = jnp.einsum("qhd,khd->hqk", queries, keys_in, preferred_element_type=jnp.float32)
    scores = jnp.where(block_allowed(segment)[None], scores, masked_score)
    row_max = jnp.max(scores, axis=-1, keepdims=True)
    expanded = jnp.exp(scores - row_max)
    row_total = jnp.sum(expanded, axis=-1, keepdims=True)
    probs_low = (expanded / row_total).astype(jnp.bfloat16)
    context = jnp.einsum("hqk,khd->qhd", probs_low, values_in, preferred_element_type=jnp.float32)
    return (context.astype(jnp.bfloat16), (row_max + jnp.log(row_total))[:, :, 0])


def attend_backward(packed):
    queries, keys_in, values_in, segment, context_grad, log_total = packed
    scores = jnp.einsum("qhd,khd->hqk", queries, keys_in, preferred_element_type=jnp.float32)
    scores = jnp.where(block_allowed(segment)[None], scores, masked_score)
    attn_probs = jnp.exp(scores - log_total[:, :, None])
    probs_grad = jnp.einsum(
        "qhd,khd->hqk", context_grad, values_in, preferred_element_type=jnp.float32
    )
    values_grad = jnp.einsum(
        "hqk,qhd->khd",
        attn_probs.astype(jnp.bfloat16),
        context_grad,
        preferred_element_type=jnp.float32,
    )
    inner_sum = jnp.sum(attn_probs * probs_grad, axis=-1, keepdims=True)
    scores_grad = (attn_probs * (probs_grad - inner_sum)).astype(jnp.bfloat16)
    queries_grad = jnp.einsum(
        "hqk,khd->qhd", scores_grad, keys_in, preferred_element_type=jnp.float32
    )
    keys_grad = jnp.einsum("hqk,qhd->khd", scores_grad, queries, preferred_element_type=jnp.float32)
    return (
        queries_grad.astype(jnp.bfloat16),
        keys_grad.astype(jnp.bfloat16),
        values_grad.astype(jnp.bfloat16),
    )


def local_plain(
    tokens,
    segment_ids,
    query_weight,
    key_weight,
    value_weight,
    out_weight,
    up_weight,
    down_weight,
    attn_gain,
    mlp_gain,
    out_cotangent,
):
    seq_count, seq_length = segment_ids.shape
    group_rows = seq_count * seq_length
    head_count = query_weight.shape[1] // HEAD_DIM
    score_scale = 1.0 / math.sqrt(HEAD_DIM)
    shaped = (seq_count, seq_length, head_count, HEAD_DIM)
    flat_shape = (group_rows, head_count * HEAD_DIM)
    residual_in = tokens.astype(jnp.float32)
    normed_attn, attn_norm_back = jax.vjp(norm_rows, residual_in, attn_gain)
    gathered_attn = lax.all_gather(normed_attn.astype(jnp.bfloat16), MP, axis=0, tiled=True)
    queries = (
        jnp.dot(gathered_attn, query_weight, preferred_element_type=jnp.float32) * score_scale
    ).astype(jnp.bfloat16)
    keys_all = jnp.dot(gathered_attn, key_weight, preferred_element_type=jnp.float32).astype(
        jnp.bfloat16
    )
    values_all = jnp.dot(gathered_attn, value_weight, preferred_element_type=jnp.float32).astype(
        jnp.bfloat16
    )
    queries_seq = queries.reshape(shaped)
    keys_seq = keys_all.reshape(shaped)
    values_seq = values_all.reshape(shaped)
    context, log_total = lax.map(attend_forward, (queries_seq, keys_seq, values_seq, segment_ids))
    context_flat = context.reshape(flat_shape)
    attn_rows = lax.psum_scatter(
        rows_times(context_flat, out_weight).astype(jnp.bfloat16),
        MP,
        scatter_dimension=0,
        tiled=True,
    ).astype(jnp.float32)
    residual_mid = residual_in + attn_rows
    normed_mlp, mlp_norm_back = jax.vjp(norm_rows, residual_mid, mlp_gain)
    gathered_mlp = lax.all_gather(normed_mlp.astype(jnp.bfloat16), MP, axis=0, tiled=True)
    pre_act = jnp.dot(gathered_mlp, up_weight, preferred_element_type=jnp.float32)
    activated, gelu_back = jax.vjp(gelu_tanh, pre_act)
    hidden = activated.astype(jnp.bfloat16)
    mlp_rows = lax.psum_scatter(
        rows_times(hidden, down_weight).astype(jnp.bfloat16), MP, scatter_dimension=0, tiled=True
    ).astype(jnp.float32)
    layer_output = (residual_mid + mlp_rows).astype(jnp.bfloat16)
    cotangent_all = lax.all_gather(out_cotangent, MP, axis=0, tiled=True)
    down_weight_grad = jnp.einsum(
        "rf,rd->fd", hidden, cotangent_all, preferred_element_type=jnp.float32
    )
    hidden_grad = lax.dot_general(
        cotangent_all, down_weight, (((1,), (1,)), ((), ())), preferred_element_type=jnp.float32
    )
    pre_grad = gelu_back(hidden_grad)[0].astype(jnp.bfloat16)
    up_weight_grad = jnp.einsum(
        "rd,rf->df", gathered_mlp, pre_grad, preferred_element_type=jnp.float32
    )
    normed_mlp_grad = lax.psum_scatter(
        rows_times_back(pre_grad, up_weight).astype(jnp.bfloat16),
        MP,
        scatter_dimension=0,
        tiled=True,
    ).astype(jnp.float32)
    middle_back, mlp_gain_grad = mlp_norm_back(normed_mlp_grad)
    middle_grad = out_cotangent.astype(jnp.float32) + middle_back
    middle_all_grad = lax.all_gather(middle_grad.astype(jnp.bfloat16), MP, axis=0, tiled=True)
    out_weight_grad = jnp.einsum(
        "rc,rd->cd", context_flat, middle_all_grad, preferred_element_type=jnp.float32
    )
    context_grad = lax.dot_general(
        middle_all_grad, out_weight, (((1,), (1,)), ((), ())), preferred_element_type=jnp.float32
    ).astype(jnp.bfloat16)
    queries_grad, keys_grad, values_grad = lax.map(
        attend_backward,
        (queries_seq, keys_seq, values_seq, segment_ids, context_grad.reshape(shaped), log_total),
    )
    queries_grad = queries_grad.reshape(flat_shape)
    keys_grad = keys_grad.reshape(flat_shape)
    values_grad = values_grad.reshape(flat_shape)
    query_weight_grad = (
        jnp.einsum("rd,rc->dc", gathered_attn, queries_grad, preferred_element_type=jnp.float32)
        * score_scale
    )
    key_weight_grad = jnp.einsum(
        "rd,rc->dc", gathered_attn, keys_grad, preferred_element_type=jnp.float32
    )
    value_weight_grad = jnp.einsum(
        "rd,rc->dc", gathered_attn, values_grad, preferred_element_type=jnp.float32
    )
    normed_attn_grad = lax.psum_scatter(
        attn_input_back(
            queries_grad,
            keys_grad,
            values_grad,
            query_weight,
            key_weight,
            value_weight,
            score_scale,
        ).astype(jnp.bfloat16),
        MP,
        scatter_dimension=0,
        tiled=True,
    ).astype(jnp.float32)
    token_back, attn_gain_grad = attn_norm_back(normed_attn_grad)
    tokens_grad = middle_grad + token_back
    attn_gain_grad, mlp_gain_grad = lax.psum((attn_gain_grad, mlp_gain_grad), (DP, MP))
    (
        query_weight_grad,
        key_weight_grad,
        value_weight_grad,
        out_weight_grad,
        up_weight_grad,
        down_weight_grad,
    ) = (
        lax.psum_scatter(
            query_weight_grad.astype(jnp.bfloat16), DP, scatter_dimension=0, tiled=True
        ).astype(jnp.float32),
        lax.psum_scatter(
            key_weight_grad.astype(jnp.bfloat16), DP, scatter_dimension=0, tiled=True
        ).astype(jnp.float32),
        lax.psum_scatter(
            value_weight_grad.astype(jnp.bfloat16), DP, scatter_dimension=0, tiled=True
        ).astype(jnp.float32),
        lax.psum_scatter(
            out_weight_grad.astype(jnp.bfloat16), DP, scatter_dimension=1, tiled=True
        ).astype(jnp.float32),
        lax.psum_scatter(
            up_weight_grad.astype(jnp.bfloat16), DP, scatter_dimension=0, tiled=True
        ).astype(jnp.float32),
        lax.psum_scatter(
            down_weight_grad.astype(jnp.bfloat16), DP, scatter_dimension=1, tiled=True
        ).astype(jnp.float32),
    )
    return (
        layer_output,
        tokens_grad,
        query_weight_grad,
        key_weight_grad,
        value_weight_grad,
        out_weight_grad,
        up_weight_grad,
        down_weight_grad,
        attn_gain_grad,
        mlp_gain_grad,
    )


def local(
    mp,
    dp,
    tokens,
    segment_ids,
    query_weight,
    key_weight,
    value_weight,
    out_weight,
    up_weight,
    down_weight,
    attn_gain,
    mlp_gain,
    out_cotangent,
):
    width, columns = query_weight.shape
    length = segment_ids.shape[1]
    half = tokens.shape[0] // 2
    z = lax.axis_index(DP) // 2
    attn_gain, mlp_gain = attn_gain.reshape(1, width), mlp_gain.reshape(1, width)
    got = layer(
        dict(
            tokens=tokens,
            segment_ids=segment_ids,
            query_weight=query_weight,
            key_weight=key_weight,
            value_weight=value_weight,
            out_weight=out_weight,
            up_weight=up_weight,
            down_weight=down_weight,
            attn_gain=attn_gain,
            mlp_gain=mlp_gain,
            out_cotangent=out_cotangent,
        ),
        half,
        width,
        columns,
        up_weight.shape[1],
        length,
    )

    qkv_grads = share_total(got.qkv_w_grad, z, [columns] * 3)
    return (
        got.layer_output,
        got.tokens_grad,
        *qkv_grads,
        got.out_total,
        got.up_total,
        got.down_total,
        got.gains[0],
        got.gains[1],
    )


def solution(mesh):
    mp, dp = mesh.shape[MP], mesh.shape[DP]
    return jax.shard_map(
        functools.partial(local, mp, dp) if (mp, dp) == (4, 8) else local_plain,
        mesh=mesh,
        in_specs=(
            P(BOTH, None),
            P(DP, None),
            P(None, MP),
            P(None, MP),
            P(None, MP),
            P(MP, None),
            P(None, MP),
            P(MP, None),
            P(),
            P(),
            P(BOTH, None),
        ),
        out_specs=(
            P(BOTH, None),
            P(BOTH, None),
            P(DP, MP),
            P(DP, MP),
            P(DP, MP),
            P(MP, DP),
            P(DP, MP),
            P(MP, DP),
            P(),
            P(),
        ),
        check_vma=False,
    )
```
